32 devices in a mesh: mode: 8 (over z, y), rep: 4 (over x, core).
Axes of the slice: x: 2, y: 2, z: 4, core: 2. Of those that a mesh axis runs over, the one named last changes fastest.
Arguments:
- first_cores: float32 [2, 8, 128, 64], P(None, 'rep', 'mode'), may hold values from -6 to 6
- mid_cores: float32 [2, 8, 3, 128, 4096], P(None, 'rep', None, 'mode'), may hold values from -2 to 2
- last_cores: float32 [2, 8, 128, 64], P(None, 'rep', 'mode'), may hold values from -0.75 to 0.75
- sketch_mid: float32 [3, 128, 4096], P(None, 'mode'), may hold values from -0.0625 to 0.0625
- sketch_last: float32 [128, 64], P('mode'), may hold values from -0.5 to 0.5
- ranks: int32 [4], replicated, may hold values from 32 to 64, as said below
Outputs:
- rounded_first: float32 [2, 128, 64], P(None, 'mode')
- rounded_mid: float32 [2, 3, 128, 4096], P(None, None, 'mode')
- rounded_last: float32 [2, 128, 64], P(None, 'mode')
The draws below stay inside these ranges and needn't reach their ends.
Inputs may be any that keep to these rules, and one draw needn't show every extreme that they name: `ranks`: some bond has rank 64.
All inputs are finite; a program needn't handle non-finite values.
Results may differ from the reference program's by a relative error of at most 0.00019.
Values sent between devices are 32-bit elements; how exact they have to be, the bound alone decides.
No kernel may reach another device: no remote copies, remote signals or barrier semaphores. Data moves between devices by JAX's collectives and lax.ppermute only.
A program may use at most 64 MiB of HBM per device.

```python
import jax
import jax.numpy as jnp
from jax import lax

N = 128
R = 64
SUMS = 8
ORDER = 5
BATCH = 2
MID = 3


def draw_ranks(key, part):
    value_key, pick_key = jax.random.split(jax.random.fold_in(key, 17))
    values = jax.random.randint(value_key, (ORDER - 1,), R // 2, R + 1)
    chosen = jax.random.randint(pick_key, (), 0, ORDER - 1)
    return jnp.where(jnp.arange(ORDER - 1) == chosen, R, values).astype(jnp.int32)


def shard_levels(rng, dims, shards, least, high):
    level = 1.0
    for dim, parts in shards:
        draws = jax.random.uniform(jax.random.fold_in(jax.random.fold_in(rng, 6), dim), (parts,), jnp.float32, least / len(shards), high / len(shards))
        level = level * jnp.repeat(jnp.exp(draws), dims[dim] // parts).reshape((-1,) + (1,) * (len(dims) - 1 - dim))
    return level


def noise(own_key, extent, deviation, reach, shards=(), kind=jnp.bfloat16):
    values = deviation * jax.random.normal(own_key, extent, jnp.float32)
    if shards:
        values = values * shard_levels(own_key, extent, shards, -0.22, 0.18)
    return jnp.clip(values, -reach, reach).astype(kind)


def setup_inputs(seed: int = 0) -> dict:
    streams_of = jax.random.split(jax.random.key(seed), 7)
    first_cores = noise(streams_of[0], (BATCH, SUMS, N, R), 1.0, 6.0, ((1, 4), (2, 8)), jnp.float32)
    mid_cores = noise(streams_of[1], (BATCH, SUMS, MID, N, R * R), (R // 8) ** -0.5, 2.0, ((1, 4), (3, 8)), jnp.float32)
    last_cores = noise(streams_of[2], (BATCH, SUMS, N, R), R ** -0.5, 0.75, ((1, 4), (2, 8)), jnp.float32)
    sketch_mid = noise(streams_of[3], (MID, N, R * R), (N * R) ** -0.5, 0.0625, ((1, 8),), jnp.float32)
    sketch_last = noise(streams_of[4], (N, R), N ** -0.5, 0.5, ((0, 8),), jnp.float32)
    ranks = draw_ranks(jax.random.fold_in(streams_of[6], 71), 0)
    return {"first_cores": first_cores, "mid_cores": mid_cores, "last_cores": last_cores, "sketch_mid": sketch_mid, "sketch_last": sketch_last, "ranks": ranks}


PRECISE = lax.Precision.HIGHEST

def lower_inverse(gram_matrix):
    factor = jnp.linalg.cholesky(gram_matrix)
    identity = jnp.eye(gram_matrix.shape[-1], dtype=gram_matrix.dtype)
    return jax.vmap(lambda single: jax.scipy.linalg.solve_triangular(single, identity, lower=True))(factor)

def orthogonal(pieces, sketch, bond_mask, row_count):
    mixture = jnp.einsum('bsiad,bsde->biae', pieces, sketch, precision=PRECISE)
    gram_matrix = jnp.einsum('biae,biaf->bef', mixture, mixture, precision=PRECISE) / row_count
    gram_matrix = gram_matrix + jnp.diag(1.0 - bond_mask)
    inverse = lower_inverse(gram_matrix)
    ortho_basis = jnp.einsum('biae,bfe->biaf', mixture, inverse, precision=PRECISE)
    carried = jnp.einsum('biaf,bsiad->bsfd', ortho_basis, pieces, precision=PRECISE) / row_count
    return (ortho_basis, carried)

def reference(first_cores, mid_cores, last_cores, sketch_mid, sketch_last, ranks):
    members, summands, slices, rank_size = first_cores.shape
    middle = mid_cores.shape[2]
    bond_masks = (jnp.arange(rank_size, dtype=jnp.int32)[None, :] < ranks[:, None]).astype(first_cores.dtype)
    middle_cores = mid_cores.reshape(members, summands, middle, slices, rank_size, rank_size)
    sketch_cores = sketch_mid.reshape(middle, slices, rank_size, rank_size)
    sketches = [None] * (middle + 1)
    sketches[middle] = jnp.einsum('bsic,ie->bsce', last_cores, sketch_last, precision=PRECISE) * bond_masks[middle]
    for position in range(middle - 1, -1, -1):
        partial_value = jnp.einsum('bsicd,bsde->bsice', middle_cores[:, :, position], sketches[position + 1], precision=PRECISE)
        sketches[position] = jnp.einsum('bsice,ife->bscf', partial_value, sketch_cores[position], precision=PRECISE) * bond_masks[position]
    pieces = first_cores[:, :, :, None, :]
    ortho_basis, carried = orthogonal(pieces, sketches[0], bond_masks[0], slices)
    rounded_first = ortho_basis[:, :, 0, :]
    blocks = []
    for position in range(middle):
        pieces = jnp.einsum('bsac,bsicd->bsiad', carried, middle_cores[:, :, position], precision=PRECISE)
        ortho_basis, carried = orthogonal(pieces, sketches[position + 1], bond_masks[position + 1], slices * rank_size)
        blocks.append(ortho_basis.reshape(members, slices, rank_size * rank_size))
    rounded_mid = jnp.stack(blocks, axis=1)
    rounded_last = jnp.einsum('bsac,bsic->bia', carried, last_cores, precision=PRECISE)
    return (rounded_first, rounded_mid, rounded_last)
```

```python
import jax
import jax.numpy as jnp
from jax import lax
from jax.sharding import PartitionSpec as P

PRECISE = lax.Precision.HIGHEST
FAST = lax.Precision.HIGH


def lower_inverse(gram_matrix):
    factor = jnp.linalg.cholesky(gram_matrix)
    identity = jnp.eye(gram_matrix.shape[-1], dtype=gram_matrix.dtype)
    return jax.scipy.linalg.solve_triangular(factor, identity, lower=True)


def flip(value, axis, bits):
    size = lax.axis_size(axis)
    return lax.ppermute(value, axis, [(index, index ^ bits) for index in range(size)])


def radices(size):
    stride, out = 1, []
    if (size.bit_length() - 1) % 2:
        out.append((2, stride))
        stride *= 2
    while stride < size:
        out.append((4, stride))
        stride *= 4
    return out


def total(value, axis, size=None):
    for radix, stride in radices(size or lax.axis_size(axis)):
        parts = [flip(value, axis, step * stride) for step in range(1, radix)]
        value = sum(parts, value)
    return value


def gathered(value, axis, dim):
    for radix, stride in radices(lax.axis_size(axis)):
        parts = [flip(value, axis, step * stride) for step in range(1, radix)]
        value = jnp.concatenate([value] + parts, axis=dim)
    return value


def per_device(first_cores, mid_cores, last_cores, sketch_mid, sketch_last, ranks):
    members, _, slices, rank_size = first_cores.shape
    middle = mid_cores.shape[2]
    total_slices = slices * lax.axis_size("mode")
    low = lax.axis_size("rep") // members
    member = lax.axis_index("rep") // low
    masks = (jnp.arange(rank_size, dtype=jnp.int32)[None, :] < ranks[:, None]).astype(jnp.float32)

    def own_and_other(value):
        kept = lax.dynamic_index_in_dim(value, member, 0, keepdims=False)
        sent = lax.dynamic_index_in_dim(value, 1 - member, 0, keepdims=False)
        return jnp.concatenate([kept, flip(sent, "rep", low)], axis=0)

    def both_members(value):
        other = flip(value, "rep", low)
        return jnp.stack(
            [jnp.where(member == 0, value, other), jnp.where(member == 0, other, value)]
        )

    last = own_and_other(last_cores)
    first = own_and_other(first_cores)
    cores = [None] * middle
    for position in range(middle - 1, -1, -1):
        cores[position] = own_and_other(
            mid_cores[:, :, position].reshape(members, -1, slices, rank_size, rank_size)
        )
    sketch_cores = sketch_mid.reshape(middle, slices, rank_size, rank_size)
    sketches = [None] * (middle + 1)
    mixed = [None] * middle
    sketches[middle] = (
        total(jnp.einsum("sic,ie->sce", last, sketch_last, precision=FAST), "mode") * masks[middle]
    )
    for position in range(middle - 1, -1, -1):
        mixed[position] = jnp.einsum(
            "sicd,sde->sice", cores[position], sketches[position + 1], precision=FAST
        )
        folded = jnp.einsum(
            "sice,ife->scf", mixed[position], sketch_cores[position], precision=FAST
        )
        sketches[position] = total(folded, "mode") * masks[position]

    everything = gathered(first, "mode", 1)
    mixture = total(
        jnp.einsum("sid,sde->ie", everything, sketches[0], precision=PRECISE), "rep", low
    )
    gram = jnp.einsum("ie,if->ef", mixture, mixture, precision=PRECISE)
    raw = jnp.einsum("ie,sid->sed", mixture, everything, precision=PRECISE)
    inverse = lower_inverse(gram / total_slices + jnp.diag(1.0 - masks[0]))
    carried = jnp.einsum("fe,sed->sfd", inverse, raw, precision=PRECISE) / total_slices
    basis = jnp.einsum("ie,fe->if", mixture[:slices], inverse, precision=PRECISE)
    rounded_first = both_members(basis)

    rows = total_slices * rank_size
    blocks = []
    for position in range(middle):
        mixture = total(
            jnp.einsum("sac,sice->iae", carried, mixed[position], precision=FAST), "rep", low
        )
        gram = jnp.einsum("iae,iaf->ef", mixture, mixture, precision=PRECISE)
        spread = jnp.einsum("sac,iae->sice", carried, mixture, precision=FAST)
        raw = jnp.einsum("sice,sicd->sed", spread, cores[position], precision=FAST)
        both = total(jnp.concatenate([raw, gram[None]], axis=0), "mode")
        raw, gram = both[:-1], both[-1]
        inverse = lower_inverse(gram / rows + jnp.diag(1.0 - masks[position + 1]))
        carried = jnp.einsum("fe,sed->sfd", inverse, raw, precision=PRECISE) / rows
        basis = jnp.einsum("iae,fe->iaf", mixture, inverse, precision=FAST)
        blocks.append(both_members(basis.reshape(slices, rank_size * rank_size)))
    rounded_mid = jnp.stack(blocks, axis=1)
    local_last = jnp.einsum("sac,sic->ia", carried, last, precision=PRECISE)
    rounded_last = both_members(total(local_last, "rep", low))
    return (rounded_first, rounded_mid, rounded_last)


def solution(mesh):
    return jax.shard_map(
        per_device,
        mesh=mesh,
        in_specs=(
            P(None, "rep", "mode", None),
            P(None, "rep", None, "mode", None),
            P(None, "rep", "mode", None),
            P(None, "mode", None),
            P("mode", None),
            P(),
        ),
        out_specs=(P(None, "mode", None), P(None, None, "mode", None), P(None, "mode", None)),
        check_vma=False,
    )
```

```python
import functools

import jax
import jax.numpy as jnp
from jax import lax
from jax.experimental import pallas as pl
from jax.experimental.pallas import tpu as pltpu
from jax.sharding import PartitionSpec as P

PRECISE = lax.Precision.HIGHEST
FAST = lax.Precision.HIGH


def lower_inverse(gram_matrix):
    factor = jnp.linalg.cholesky(gram_matrix)
    identity = jnp.eye(gram_matrix.shape[-1], dtype=gram_matrix.dtype)
    return jax.scipy.linalg.solve_triangular(factor, identity, lower=True)


def flip(value, axis, bits):
    size = lax.axis_size(axis)
    return lax.ppermute(value, axis, [(index, index ^ bits) for index in range(size)])


def radices(size):
    stride, out = 1, []
    if (size.bit_length() - 1) % 2:
        out.append((2, stride))
        stride *= 2
    while stride < size:
        out.append((4, stride))
        stride *= 4
    return out


def total(value, axis, size=None):
    for radix, stride in radices(size or lax.axis_size(axis)):
        parts = [flip(value, axis, step * stride) for step in range(1, radix)]
        value = sum(parts, value)
    return value


def gathered(value, axis, dim):
    for radix, stride in radices(lax.axis_size(axis)):
        parts = [flip(value, axis, step * stride) for step in range(1, radix)]
        value = jnp.concatenate([value] + parts, axis=dim)
    return value


def general(first_cores, mid_cores, last_cores, sketch_mid, sketch_last, ranks):
    members, _, slices, rank_size = first_cores.shape
    middle = mid_cores.shape[2]
    total_slices = slices * lax.axis_size("mode")
    low = lax.axis_size("rep") // members
    member = lax.axis_index("rep") // low
    masks = (jnp.arange(rank_size, dtype=jnp.int32)[None, :] < ranks[:, None]).astype(jnp.float32)

    def own_and_other(value):
        kept = lax.dynamic_index_in_dim(value, member, 0, keepdims=False)
        sent = lax.dynamic_index_in_dim(value, 1 - member, 0, keepdims=False)
        return jnp.concatenate([kept, flip(sent, "rep", low)], axis=0)

    def both_members(value):
        other = flip(value, "rep", low)
        return jnp.stack(
            [jnp.where(member == 0, value, other), jnp.where(member == 0, other, value)]
        )

    last = own_and_other(last_cores)
    first = own_and_other(first_cores)
    cores = [None] * middle
    for position in range(middle - 1, -1, -1):
        cores[position] = own_and_other(
            mid_cores[:, :, position].reshape(members, -1, slices, rank_size, rank_size)
        )
    sketch_cores = sketch_mid.reshape(middle, slices, rank_size, rank_size)
    sketches = [None] * (middle + 1)
    mixed = [None] * middle
    sketches[middle] = (
        total(jnp.einsum("sic,ie->sce", last, sketch_last, precision=FAST), "mode") * masks[middle]
    )
    for position in range(middle - 1, -1, -1):
        mixed[position] = jnp.einsum(
            "sicd,sde->sice", cores[position], sketches[position + 1], precision=FAST
        )
        folded = jnp.einsum(
            "sice,ife->scf", mixed[position], sketch_cores[position], precision=FAST
        )
        sketches[position] = total(folded, "mode") * masks[position]

    everything = gathered(first, "mode", 1)
    mixture = total(
        jnp.einsum("sid,sde->ie", everything, sketches[0], precision=PRECISE), "rep", low
    )
    gram = jnp.einsum("ie,if->ef", mixture, mixture, precision=PRECISE)
    raw = jnp.einsum("ie,sid->sed", mixture, everything, precision=PRECISE)
    inverse = lower_inverse(gram / total_slices + jnp.diag(1.0 - masks[0]))
    carried = jnp.einsum("fe,sed->sfd", inverse, raw, precision=PRECISE) / total_slices
    basis = jnp.einsum("ie,fe->if", mixture[:slices], inverse, precision=PRECISE)
    rounded_first = both_members(basis)

    rows = total_slices * rank_size
    blocks = []
    for position in range(middle):
        mixture = total(
            jnp.einsum("sac,sice->iae", carried, mixed[position], precision=FAST), "rep", low
        )
        gram = jnp.einsum("iae,iaf->ef", mixture, mixture, precision=PRECISE)
        spread = jnp.einsum("sac,iae->sice", carried, mixture, precision=FAST)
        raw = jnp.einsum("sice,sicd->sed", spread, cores[position], precision=FAST)
        both = total(jnp.concatenate([raw, gram[None]], axis=0), "mode")
        raw, gram = both[:-1], both[-1]
        inverse = lower_inverse(gram / rows + jnp.diag(1.0 - masks[position + 1]))
        carried = jnp.einsum("fe,sed->sfd", inverse, raw, precision=PRECISE) / rows
        basis = jnp.einsum("iae,fe->iaf", mixture, inverse, precision=FAST)
        blocks.append(both_members(basis.reshape(slices, rank_size * rank_size)))
    rounded_mid = jnp.stack(blocks, axis=1)
    local_last = jnp.einsum("sac,sic->ia", carried, last, precision=PRECISE)
    rounded_last = both_members(total(local_last, "rep", low))
    return (rounded_first, rounded_mid, rounded_last)


LANES = 128
SUBLANES = 8
HALF = 64
NN = (((1,), (0,)), ((), ()))
NT = (((1,), (1,)), ((), ()))
TN = (((0,), (0,)), ((), ()))


def left_half(rows):
    return lax.broadcasted_iota(jnp.int32, (rows, LANES), 1) < HALF


def swap(value):
    return pltpu.roll(value, HALF, 1)


def pick(left, right):
    return jnp.where(left_half(left.shape[0]), left, right)


def split(value):
    high = value.astype(jnp.bfloat16)
    return high, (value - high.astype(jnp.float32)).astype(jnp.bfloat16)


def dot(left, right, dims=NN):
    return lax.dot_general(left, right, dims, preferred_element_type=jnp.float32)


def dot3(left, right, dims=NN):
    (lh, ll), (rh, rl) = left, right
    return dot(lh, rh, dims) + dot(lh, rl, dims) + dot(ll, rh, dims)


def exact(left, right, dims=NN):
    return lax.dot_general(
        left, right, dims, precision=PRECISE, preferred_element_type=jnp.float32
    )


def block_diagonal(value):
    zero = jnp.zeros_like(value)
    return jnp.concatenate([pick(value, zero), pick(zero, swap(value))], axis=0)


def spread_rows(packed, scratch):
    count = packed.shape[0]
    scratch[pl.ds(0, count, stride=2), :] = packed
    scratch[pl.ds(1, count, stride=2), :] = swap(packed)
    return scratch[pl.ds(0, 2 * count), :]


def start_kernel(kept, other, sketch, out, scratch):
    count = kept.shape[0]
    for half, cores in enumerate((kept, other)):
        for index in range(count):
            scratch[pl.ds((half * count + index) * HALF, HALF), pl.ds(0, HALF)] = exact(
                cores[index], sketch[...], TN
            )
    rows = out.shape[0]
    even = scratch[pl.ds(0, rows, stride=2), :]
    odd = scratch[pl.ds(1, rows, stride=2), :]
    out[...] = pick(even, swap(odd))


def added(parts):
    value = parts[0][...]
    for part in parts[1:]:
        value = value + part[...]
    return value


def sketch_kernel(n_parts, *refs):
    parts, refs = refs[:n_parts], refs[n_parts:]
    mask, kept, other, sketch, out, high, low, wide, product, narrow = refs
    count = kept.shape[0]
    rows = kept.shape[1]
    tiles = rows // 256
    natural = spread_rows(added(parts) * mask[...], wide)
    for half, cores in enumerate((kept, other)):
        for index in range(count):
            s = half * count + index
            weight = split(block_diagonal(natural[s * HALF : (s + 1) * HALF]))
            result = dot3(split(cores[index]), weight)
            for tile in range(tiles):
                product[pl.ds((tile * 2 * count + s) * 256, 256), :] = result[
                    tile * 256 : (tile + 1) * 256
                ]
    height = 2 * count * 32
    total_value = jnp.zeros(out.shape, jnp.float32)
    for tile in range(tiles):
        for sub in range(SUBLANES):
            i = tile * SUBLANES + sub
            packed = sketch[pl.ds(tile * 256 + sub, 32, stride=SUBLANES), :]
            weight = split(block_diagonal(spread_rows(packed, narrow.at[i])))
            own = split(product[pl.ds(tile * height * SUBLANES + sub, height, stride=SUBLANES), :])
            high[i] = own[0]
            low[i] = own[1]
            total_value = total_value + dot3(own, weight, NT)
    out[...] = total_value


def first_kernel(n_parts, *refs):
    parts, refs = refs[:n_parts], refs[n_parts:]
    mask, cores, out, wide = refs
    natural = spread_rows(added(parts) * mask[...], wide)
    natural = pick(natural, jnp.zeros_like(natural))
    value = exact(cores[0], natural[:LANES])
    for pair in range(1, cores.shape[0]):
        value = value + exact(cores[pair], natural[pair * LANES : (pair + 1) * LANES])
    out[...] = value


def eliminate(gram, mask, row_count):
    size = gram.shape[0]
    row = lax.broadcasted_iota(jnp.int32, (size, LANES), 0)
    lane = lax.broadcasted_iota(jnp.int32, (size, LANES), 1)
    scaled = gram * (1.0 / row_count)
    diagonal = jnp.where(lane == row, 1.0 - mask, 0.0)
    work = jnp.where(lane < HALF, scaled + diagonal, jnp.where(lane - HALF == row, 1.0, 0.0))
    step = 4
    done = []
    for base in range(0, size, step):
        start = base - base % SUBLANES
        if base % SUBLANES == 0 and base:
            work = work[SUBLANES:]
        live = size - start
        offset = base - start
        columns = [
            jnp.broadcast_to(work[:, base + k : base + k + 1], (live, LANES)) for k in range(step)
        ]
        factors, pivots = [], []
        for k in range(step):
            at = offset + k
            column, pivot = columns[k], work[at : at + 1]
            for m in range(k):
                weight = factors[m][at : at + 1]
                column = column - factors[m] * weight
                pivot = pivot - pivots[m] * weight
            scale = lax.rsqrt(column[at : at + 1])
            factors.append(column * scale)
            pivots.append(pivot * scale)
        update = work
        for k in range(step):
            update = update - factors[k] * pivots[k]
        place = lax.broadcasted_iota(jnp.int32, (live, LANES), 0)
        work = jnp.where(place >= offset + step, update, work)
        for k in range(step):
            work = jnp.where(place == offset + k, pivots[k], work)
        if offset + step == SUBLANES:
            done.append(work[:SUBLANES])
    return jnp.concatenate(done, axis=0)


def project(raw, gram, mask, row_count, square):
    solved = eliminate(gram, mask, row_count)
    square[pl.ds(0, HALF), :] = solved
    planar = jnp.concatenate(
        [square[pl.ds(0, HALF // 2, stride=2), :], square[pl.ds(1, HALF // 2, stride=2), :]], axis=0
    )
    carried = exact(raw, block_diagonal(swap(planar)), NT) * (1.0 / row_count)
    square[...] = carried
    pairs = carried.shape[0] // HALF
    even = square[pl.ds(0, pairs * 32, stride=2), :]
    odd = square[pl.ds(1, pairs * 32, stride=2), :]
    first, second = pick(even, swap(odd)), pick(swap(even), odd)
    blocks = []
    for pair in range(pairs):
        blocks += [first[pair * 32 : (pair + 1) * 32], second[pair * 32 : (pair + 1) * 32]]
    return swap(solved), jnp.concatenate(blocks, axis=0)


def mix(carried, high, low, out):
    weight = split(carried.T)
    for i in range(high.shape[0]):
        tile, sub = i // SUBLANES, i % SUBLANES
        value = dot3(weight, (high[i], low[i]))
        straight = pick(value[0:32], value[96:128])
        crossed = pick(value[32:64], value[64:96])
        out[pl.ds(tile * 256 + sub, 32, stride=SUBLANES), :] = straight + swap(crossed)


def unpack_gram(packed):
    return jnp.concatenate([packed, swap(packed)], axis=0)


def bond_one_kernel(row_count, slices, kept, other, cores, mask, high, low, *refs):
    inverse, carried, basis, out, square = refs
    mixture = kept[...] + other[...]
    gram = exact(mixture, mixture, TN)[:HALF]
    raw = []
    for pair in range(cores.shape[0]):
        value = exact(cores[pair], mixture, TN)
        raw.append(pick(value[:HALF], swap(value[HALF:])))
    solved, moved = project(jnp.concatenate(raw, axis=0), gram, mask[...], row_count, square)
    inverse[...] = solved
    carried[...] = moved
    basis[...] = exact(mixture[:slices], pick(solved, jnp.zeros_like(solved)), NT)
    mix(moved, high, low, out)


def bond_kernel(row_count, n_parts, *refs):
    parts, refs = refs[:n_parts], refs[n_parts:]
    mask, high, low, inverse, carried, out, square = refs
    value = added(parts)
    solved, moved = project(
        value[:LANES], unpack_gram(value[LANES:]), mask[...], row_count, square
    )
    inverse[...] = solved
    carried[...] = moved
    mix(moved, high, low, out)


def last_kernel(row_count, n_parts, *refs):
    parts, refs = refs[:n_parts], refs[n_parts:]
    mask, kept, other, out = refs
    value = added(parts)
    solved = swap(eliminate(unpack_gram(value[LANES:]), mask[...], row_count))
    carried = exact(value[:LANES], block_diagonal(solved), NT) * (1.0 / row_count)
    count, slices = kept.shape[0], kept.shape[1]
    sides = [jnp.zeros((slices, LANES), jnp.float32)] * 2
    for half, cores in enumerate((kept, other)):
        for index in range(count):
            s = half * count + index
            sides[s % 2] = sides[s % 2] + exact(
                cores[index], carried[s // 2 * HALF : (s // 2 + 1) * HALF]
            )
    out[pl.ds(0, slices), :] = sides[0] + swap(sides[1])
    out[pl.ds(slices, HALF), :] = solved


def gram_kernel(mine, theirs, carried, kept, other, mixture, out, spread):
    count, rows = kept.shape[0], kept.shape[1]
    tiles = rows // 256
    mixture[...] = mine[...] + theirs[...]
    everything = mixture[...]
    gram = exact(everything, everything, TN)
    weight = split(carried[...])
    height = 2 * count * 32
    for tile in range(tiles):
        for sub in range(SUBLANES):
            packed = mixture[pl.ds(tile * 256 + sub, 32, stride=SUBLANES), :]
            crossed = swap(packed)
            zero = jnp.zeros_like(packed)
            blocks = jnp.concatenate(
                [pick(packed, zero), pick(crossed, zero), pick(zero, crossed), pick(zero, packed)],
                axis=0,
            )
            spread[pl.ds(tile * height * SUBLANES + sub, height, stride=SUBLANES), :] = dot3(
                weight, split(blocks)
            )
    raw = []
    for half, cores in enumerate((kept, other)):
        for index in range(count):
            s = half * count + index
            own = jnp.concatenate(
                [spread[pl.ds((tile * 2 * count + s) * 256, 256), :] for tile in range(tiles)],
                axis=0,
            )
            raw.append(dot3(split(cores[index]), split(own), TN))
    for pair in range(count):
        even, odd = raw[2 * pair], raw[2 * pair + 1]
        out[pl.ds(pair * HALF, HALF), :] = pick(even[:HALF], odd[HALF:]) + swap(
            pick(odd[:HALF], even[HALF:])
        )
    gram = gram[:HALF] + swap(gram[HALF:])
    out[pl.ds(2 * HALF, 32), :] = pick(gram[:32], swap(gram[32:]))


def basis_kernel(mixture, inverse, out):
    weight = split(block_diagonal(inverse[...]))
    out[...] = dot3(split(mixture[...]), weight, NT)


def kernel_call(body, outs, scratch, *operands, flops=0):
    vmem = pl.BlockSpec(memory_space=pltpu.VMEM)
    moved = sum(x.size * x.dtype.itemsize for x in (*operands, *outs))
    return pl.pallas_call(
        body,
        out_shape=outs,
        in_specs=[vmem] * len(operands),
        out_specs=[vmem] * len(outs),
        scratch_shapes=scratch,
        compiler_params=pltpu.CompilerParams(vmem_limit_bytes=24 << 20),
        cost_estimate=pl.CostEstimate(flops=flops, bytes_accessed=moved, transcendentals=0),
    )(*operands)


def shape(*dims, dtype=jnp.float32):
    return jax.ShapeDtypeStruct(dims, dtype)


def scratch(*dims):
    return pltpu.VMEM(dims, jnp.float32)


def in_rows(value):
    lead, (slices, width) = value.shape[:-2], value.shape[-2:]
    value = value.reshape(*lead, slices // SUBLANES, SUBLANES, width // LANES, LANES)
    value = jnp.swapaxes(value, -2, -3)
    return value.reshape(*lead, slices * width // LANES, LANES)


def out_of_rows(value, slices):
    lead, (rows, _) = value.shape[:-2], value.shape[-2:]
    value = value.reshape(*lead, slices // SUBLANES, rows // slices, SUBLANES, LANES)
    value = jnp.swapaxes(value, -2, -3)
    return value.reshape(*lead, slices, rows // slices * LANES)


def exchanged(value, axis):
    steps = radices(lax.axis_size(axis))
    for at, (radix, stride) in enumerate(steps):
        parts = [value] + [flip(value, axis, step * stride) for step in range(1, radix)]
        if at < len(steps) - 1:
            value = sum(parts[1:], parts[0])
    return parts


def tiled(first_cores, mid_cores, last_cores, sketch_mid, sketch_last, ranks):
    members, count, slices, rank_size = first_cores.shape
    middle = mid_cores.shape[2]
    total_slices = slices * lax.axis_size("mode")
    low = lax.axis_size("rep") // members
    member = lax.axis_index("rep") // low
    masks = (jnp.arange(rank_size, dtype=jnp.int32)[None, :] < ranks[:, None]).astype(jnp.float32)
    masks = jnp.concatenate([masks, masks], axis=1)[:, None, :]
    height = 2 * count * 32
    rows = slices * 32

    def own(value):
        return lax.dynamic_index_in_dim(value, member, 0, keepdims=False)

    def traded(value):
        sent = lax.dynamic_index_in_dim(value, 1 - member, 0, keepdims=False)
        return flip(sent, "rep", low)

    last = (own(last_cores), traded(last_cores))
    mid_rows = in_rows(mid_cores)
    cores = [None] * middle
    for position in range(middle - 1, -1, -1):
        here = mid_rows[:, :, position]
        cores[position] = (own(here), traded(here))
    sketch_rows = in_rows(sketch_mid)

    pairs = first_cores.transpose(0, 2, 1, 3).reshape(members, slices, count * rank_size)
    first = jnp.stack([own(pairs), traded(pairs)])
    first = gathered(first, "mode", 1)

    (part,) = kernel_call(
        start_kernel, [shape(height, LANES)], [scratch(2 * height, LANES)], *last, sketch_last
    )
    mixed = [None] * middle
    for position in range(middle - 1, -1, -1):
        parts = exchanged(part, "mode")
        wide = shape(slices, height, LANES, dtype=jnp.bfloat16)
        part, *mixed[position] = kernel_call(
            functools.partial(sketch_kernel, len(parts)),
            [shape(height, LANES), wide, wide],
            [
                scratch(2 * height, LANES),
                scratch(height * slices, LANES),
                scratch(slices, HALF, LANES),
            ],
            *parts,
            masks[position + 1],
            *cores[position],
            sketch_rows[position],
        )
    parts = exchanged(part, "mode")
    (part,) = kernel_call(
        functools.partial(first_kernel, len(parts)),
        [shape(total_slices, LANES)],
        [scratch(2 * height, LANES)],
        *parts,
        masks[0],
        first,
    )
    square = scratch(count * HALF, LANES)
    inverse, carried, basis, part = kernel_call(
        functools.partial(bond_one_kernel, float(total_slices), slices),
        [shape(HALF, LANES), shape(height, LANES), shape(slices, HALF), shape(rows, LANES)],
        [square],
        part,
        flip(part, "rep", 1),
        first,
        masks[0],
        *mixed[0],
    )

    def both_members(value, other):
        return jnp.stack(
            [jnp.where(member == 0, value, other), jnp.where(member == 0, other, value)]
        )

    rounded_first = both_members(basis, flip(basis, "rep", low))
    row_count = float(total_slices * rank_size)
    blocks = jnp.zeros((members, middle, rows, LANES), jnp.float32)
    for position in range(middle):
        mixture, part = kernel_call(
            gram_kernel,
            [shape(rows, LANES), shape(2 * HALF + 32, LANES)],
            [scratch(height * slices, LANES)],
            part,
            flip(part, "rep", 1),
            carried,
            *cores[position],
        )
        parts = exchanged(part, "mode")
        mask = masks[position + 1]
        if position < middle - 1:
            inverse, carried, part = kernel_call(
                functools.partial(bond_kernel, row_count, len(parts)),
                [shape(HALF, LANES), shape(height, LANES), shape(rows, LANES)],
                [square],
                *parts,
                mask,
                *mixed[position + 1],
            )
            (basis,) = kernel_call(basis_kernel, [shape(rows, LANES)], [], mixture, inverse)
            other = flip(basis, "rep", low)
        else:
            away = flip(mixture, "rep", low)
            (final,) = kernel_call(
                functools.partial(last_kernel, row_count, len(parts)),
                [shape(slices + HALF, LANES)],
                [],
                *parts,
                mask,
                *last,
            )
            near = flip(final, "rep", 1)
            far = flip(final, "rep", low)
            across = flip(final, "rep", low + 1)
            (basis,) = kernel_call(
                basis_kernel, [shape(rows, LANES)], [], mixture, final[slices:]
            )
            (other,) = kernel_call(basis_kernel, [shape(rows, LANES)], [], away, far[slices:])
            value = (final + near)[:slices, :HALF]
            rounded_last = both_members(value, (far + across)[:slices, :HALF])
        blocks = lax.dynamic_update_slice(blocks, basis[None, None], (member, position, 0, 0))
        blocks = lax.dynamic_update_slice(blocks, other[None, None], (1 - member, position, 0, 0))
    return (rounded_first, out_of_rows(blocks, slices), rounded_last)


def per_device(*arguments):
    members, count, slices, rank_size = arguments[0].shape
    fits = (
        members == 2
        and count == 2
        and rank_size == HALF
        and slices % SUBLANES == 0
        and lax.axis_size("rep") == 2 * members
        and slices * lax.axis_size("mode") % LANES == 0
    )
    return tiled(*arguments) if fits else general(*arguments)


def solution(mesh):
    return jax.shard_map(
        per_device,
        mesh=mesh,
        in_specs=(
            P(None, "rep", "mode", None),
            P(None, "rep", None, "mode", None),
            P(None, "rep", "mode", None),
            P(None, "mode", None),
            P("mode", None),
            P(),
        ),
        out_specs=(P(None, "mode", None), P(None, None, "mode", None), P(None, "mode", None)),
        check_vma=False,
    )
```

```python
import functools

import jax
import jax.numpy as jnp
from jax import lax
from jax.experimental import pallas as pl
from jax.experimental.pallas import tpu as pltpu
from jax.sharding import PartitionSpec as P

PRECISE = lax.Precision.HIGHEST
FAST = lax.Precision.HIGH


def lower_inverse(gram_matrix):
    factor = jnp.linalg.cholesky(gram_matrix)
    identity = jnp.eye(gram_matrix.shape[-1], dtype=gram_matrix.dtype)
    return jax.scipy.linalg.solve_triangular(factor, identity, lower=True)


def flip(value, axis, bits):
    size = lax.axis_size(axis)
    return lax.ppermute(value, axis, [(index, index ^ bits) for index in range(size)])


def radices(size):
    stride, out = 1, []
    if (size.bit_length() - 1) % 2:
        out.append((2, stride))
        stride *= 2
    while stride < size:
        out.append((4, stride))
        stride *= 4
    return out


def total(value, axis, size=None):
    for radix, stride in radices(size or lax.axis_size(axis)):
        parts = [flip(value, axis, step * stride) for step in range(1, radix)]
        value = sum(parts, value)
    return value


def gathered(value, axis, dim):
    for radix, stride in radices(lax.axis_size(axis)):
        parts = [flip(value, axis, step * stride) for step in range(1, radix)]
        value = jnp.concatenate([value] + parts, axis=dim)
    return value


def general(first_cores, mid_cores, last_cores, sketch_mid, sketch_last, ranks):
    members, _, slices, rank_size = first_cores.shape
    middle = mid_cores.shape[2]
    total_slices = slices * lax.axis_size("mode")
    low = lax.axis_size("rep") // members
    member = lax.axis_index("rep") // low
    masks = (jnp.arange(rank_size, dtype=jnp.int32)[None, :] < ranks[:, None]).astype(jnp.float32)

    def own_and_other(value):
        kept = lax.dynamic_index_in_dim(value, member, 0, keepdims=False)
        sent = lax.dynamic_index_in_dim(value, 1 - member, 0, keepdims=False)
        return jnp.concatenate([kept, flip(sent, "rep", low)], axis=0)

    def both_members(value):
        other = flip(value, "rep", low)
        return jnp.stack(
            [jnp.where(member == 0, value, other), jnp.where(member == 0, other, value)]
        )

    last = own_and_other(last_cores)
    first = own_and_other(first_cores)
    cores = [None] * middle
    for position in range(middle - 1, -1, -1):
        cores[position] = own_and_other(
            mid_cores[:, :, position].reshape(members, -1, slices, rank_size, rank_size)
        )
    sketch_cores = sketch_mid.reshape(middle, slices, rank_size, rank_size)
    sketches = [None] * (middle + 1)
    mixed = [None] * middle
    sketches[middle] = (
        total(jnp.einsum("sic,ie->sce", last, sketch_last, precision=FAST), "mode") * masks[middle]
    )
    for position in range(middle - 1, -1, -1):
        mixed[position] = jnp.einsum(
            "sicd,sde->sice", cores[position], sketches[position + 1], precision=FAST
        )
        folded = jnp.einsum(
            "sice,ife->scf", mixed[position], sketch_cores[position], precision=FAST
        )
        sketches[position] = total(folded, "mode") * masks[position]

    everything = gathered(first, "mode", 1)
    mixture = total(
        jnp.einsum("sid,sde->ie", everything, sketches[0], precision=PRECISE), "rep", low
    )
    gram = jnp.einsum("ie,if->ef", mixture, mixture, precision=PRECISE)
    raw = jnp.einsum("ie,sid->sed", mixture, everything, precision=PRECISE)
    inverse = lower_inverse(gram / total_slices + jnp.diag(1.0 - masks[0]))
    carried = jnp.einsum("fe,sed->sfd", inverse, raw, precision=PRECISE) / total_slices
    basis = jnp.einsum("ie,fe->if", mixture[:slices], inverse, precision=PRECISE)
    rounded_first = both_members(basis)

    rows = total_slices * rank_size
    blocks = []
    for position in range(middle):
        mixture = total(
            jnp.einsum("sac,sice->iae", carried, mixed[position], precision=FAST), "rep", low
        )
        gram = jnp.einsum("iae,iaf->ef", mixture, mixture, precision=PRECISE)
        spread = jnp.einsum("sac,iae->sice", carried, mixture, precision=FAST)
        raw = jnp.einsum("sice,sicd->sed", spread, cores[position], precision=FAST)
        both = total(jnp.concatenate([raw, gram[None]], axis=0), "mode")
        raw, gram = both[:-1], both[-1]
        inverse = lower_inverse(gram / rows + jnp.diag(1.0 - masks[position + 1]))
        carried = jnp.einsum("fe,sed->sfd", inverse, raw, precision=PRECISE) / rows
        basis = jnp.einsum("iae,fe->iaf", mixture, inverse, precision=FAST)
        blocks.append(both_members(basis.reshape(slices, rank_size * rank_size)))
    rounded_mid = jnp.stack(blocks, axis=1)
    local_last = jnp.einsum("sac,sic->ia", carried, last, precision=PRECISE)
    rounded_last = both_members(total(local_last, "rep", low))
    return (rounded_first, rounded_mid, rounded_last)


LANES = 128
SUBLANES = 8
HALF = 64
NN = (((1,), (0,)), ((), ()))
NT = (((1,), (1,)), ((), ()))
TN = (((0,), (0,)), ((), ()))


def left_half(rows):
    return lax.broadcasted_iota(jnp.int32, (rows, LANES), 1) < HALF


def swap(value):
    return pltpu.roll(value, HALF, 1)


def pick(left, right):
    return jnp.where(left_half(left.shape[0]), left, right)


def split(value):
    high = value.astype(jnp.bfloat16)
    return high, (value - high.astype(jnp.float32)).astype(jnp.bfloat16)


def dot(left, right, dims=NN):
    return lax.dot_general(left, right, dims, preferred_element_type=jnp.float32)


def dot3(left, right, dims=NN):
    (lh, ll), (rh, rl) = left, right
    return dot(lh, rh, dims) + dot(lh, rl, dims) + dot(ll, rh, dims)


def exact(left, right, dims=NN):
    return lax.dot_general(
        left, right, dims, precision=PRECISE, preferred_element_type=jnp.float32
    )


def block_diagonal(value):
    zero = jnp.zeros_like(value)
    return jnp.concatenate([pick(value, zero), pick(zero, swap(value))], axis=0)


def spread_rows(packed, scratch):
    count = packed.shape[0]
    scratch[pl.ds(0, count, stride=2), :] = packed
    scratch[pl.ds(1, count, stride=2), :] = swap(packed)
    return scratch[pl.ds(0, 2 * count), :]


def start_kernel(member, last, first, sketch, keep, send, scratch):
    count = last.shape[1]
    for out, index in ((keep, member[0]), (send, 1 - member[0])):
        cores, heads = last[index], first[index]
        for s in range(count):
            scratch[pl.ds(s * HALF, HALF), pl.ds(0, HALF)] = exact(cores[s], sketch[...], TN)
        rows = count * 32
        even = scratch[pl.ds(0, rows, stride=2), :]
        odd = scratch[pl.ds(1, rows, stride=2), :]
        out[pl.ds(0, rows), :] = pick(even, swap(odd))
        slices = heads.shape[1]
        out[pl.ds(rows, slices), :] = jnp.concatenate([heads[0], heads[1]], axis=1)
        if out.shape[0] > rows + slices:
            out[pl.ds(rows + slices, slices), :] = jnp.concatenate([cores[0], cores[1]], axis=1)


def merge_kernel(n_parts, rows, slices, *refs):
    keeps, sends, out = refs[:n_parts], refs[n_parts : 2 * n_parts], refs[-1]
    for pair, parts in enumerate((keeps, sends)):
        out[pl.ds(pair * rows, rows), :] = added([part.at[pl.ds(0, rows)] for part in parts])
        for at, part in enumerate(parts):
            out[pl.ds(2 * rows + (pair * n_parts + at) * slices, slices), :] = part[
                pl.ds(rows, slices), :
            ]


def heads_of(parts, pair):
    rows = (parts[0].shape[0] - LANES) // 2
    return jnp.concatenate(
        [part[pl.ds(LANES + pair * rows, rows), :] for part in parts], axis=0
    )


def added(parts):
    value = parts[0][...]
    for part in parts[1:]:
        value = value + part[...]
    return value


def sketch_kernel(n_parts, *refs):
    parts, refs = refs[:n_parts], refs[n_parts:]
    mask, kept, other, sketch, out, high, low, wide, product, narrow = refs
    count = kept.shape[0]
    rows = kept.shape[1]
    tiles = rows // 256
    value = added([part.at[pl.ds(0, LANES)] for part in parts])
    natural = spread_rows(value * mask[...], wide)
    for half, cores in enumerate((kept, other)):
        for index in range(count):
            s = half * count + index
            weight = split(block_diagonal(natural[s * HALF : (s + 1) * HALF]))
            result = dot3(split(cores[index]), weight)
            for tile in range(tiles):
                product[pl.ds((tile * 2 * count + s) * 256, 256), :] = result[
                    tile * 256 : (tile + 1) * 256
                ]
    height = 2 * count * 32
    total_value = jnp.zeros(out.shape, jnp.float32)
    for tile in range(tiles):
        for sub in range(SUBLANES):
            i = tile * SUBLANES + sub
            packed = sketch[pl.ds(tile * 256 + sub, 32, stride=SUBLANES), :]
            weight = split(block_diagonal(spread_rows(packed, narrow.at[i])))
            own = split(product[pl.ds(tile * height * SUBLANES + sub, height, stride=SUBLANES), :])
            high[i] = own[0]
            low[i] = own[1]
            total_value = total_value + dot3(own, weight, NT)
    out[...] = total_value


def first_kernel(n_parts, *refs):
    parts, refs = refs[:n_parts], refs[n_parts:]
    heads, (mask, out, wide) = refs[:n_parts], refs[n_parts:]
    natural = spread_rows(added(parts) * mask[...], wide)
    natural = pick(natural, jnp.zeros_like(natural))
    value = exact(heads_of(heads, 0), natural[:LANES])
    out[...] = value + exact(heads_of(heads, 1), natural[LANES:])


def eliminate(gram, mask, row_count):
    size = gram.shape[0]
    row = lax.broadcasted_iota(jnp.int32, (size, LANES), 0)
    lane = lax.broadcasted_iota(jnp.int32, (size, LANES), 1)
    scaled = gram * (1.0 / row_count)
    diagonal = jnp.where(lane == row, 1.0 - mask, 0.0)
    work = jnp.where(lane < HALF, scaled + diagonal, jnp.where(lane - HALF == row, 1.0, 0.0))
    step = 4
    done = []
    for base in range(0, size, step):
        start = base - base % SUBLANES
        if base % SUBLANES == 0 and base:
            work = work[SUBLANES:]
        live = size - start
        offset = base - start
        columns = [
            jnp.broadcast_to(work[:, base + k : base + k + 1], (live, LANES)) for k in range(step)
        ]
        factors, pivots = [], []
        for k in range(step):
            at = offset + k
            column, pivot = columns[k], work[at : at + 1]
            for m in range(k):
                weight = factors[m][at : at + 1]
                column = column - factors[m] * weight
                pivot = pivot - pivots[m] * weight
            scale = lax.rsqrt(column[at : at + 1])
            factors.append(column * scale)
            pivots.append(pivot * scale)
        update = work
        for k in range(step):
            update = update - factors[k] * pivots[k]
        place = lax.broadcasted_iota(jnp.int32, (live, LANES), 0)
        work = jnp.where(place >= offset + step, update, work)
        for k in range(step):
            work = jnp.where(place == offset + k, pivots[k], work)
        if offset + step == SUBLANES:
            done.append(work[:SUBLANES])
    return jnp.concatenate(done, axis=0)


def project(raw, gram, mask, row_count, square):
    solved = eliminate(gram, mask, row_count)
    square[pl.ds(0, HALF), :] = solved
    planar = jnp.concatenate(
        [square[pl.ds(0, HALF // 2, stride=2), :], square[pl.ds(1, HALF // 2, stride=2), :]], axis=0
    )
    carried = exact(raw, block_diagonal(swap(planar)), NT) * (1.0 / row_count)
    square[...] = carried
    pairs = carried.shape[0] // HALF
    even = square[pl.ds(0, pairs * 32, stride=2), :]
    odd = square[pl.ds(1, pairs * 32, stride=2), :]
    first, second = pick(even, swap(odd)), pick(swap(even), odd)
    blocks = []
    for pair in range(pairs):
        blocks += [first[pair * 32 : (pair + 1) * 32], second[pair * 32 : (pair + 1) * 32]]
    return swap(solved), jnp.concatenate(blocks, axis=0)


def mix(carried, high, low, out):
    weight = split(carried.T)
    for i in range(high.shape[0]):
        tile, sub = i // SUBLANES, i % SUBLANES
        value = dot3(weight, (high[i], low[i]))
        straight = pick(value[0:32], value[96:128])
        crossed = pick(value[32:64], value[64:96])
        out[pl.ds(tile * 256 + sub, 32, stride=SUBLANES), :] = straight + swap(crossed)


def unpack_gram(packed):
    return jnp.concatenate([packed, swap(packed)], axis=0)


def bond_one_kernel(row_count, n_parts, kept, other, *refs):
    heads, (mask, high, low, *refs) = refs[:n_parts], refs[n_parts:]
    inverse, carried, basis, out, square = refs
    mixture = kept[...] + other[...]
    gram = exact(mixture, mixture, TN)[:HALF]
    raw = []
    for pair in range(2):
        value = exact(heads_of(heads, pair), mixture, TN)
        raw.append(pick(value[:HALF], swap(value[HALF:])))
    solved, moved = project(jnp.concatenate(raw, axis=0), gram, mask[...], row_count, square)
    inverse[...] = solved
    carried[...] = moved
    slices = basis.shape[0]
    full = jnp.concatenate([pick(solved, jnp.zeros_like(solved)), jnp.zeros_like(solved)], axis=0)
    basis[...] = exact(mixture[:slices], full, NT)
    mix(moved, high, low, out)


def bond_kernel(row_count, n_parts, *refs):
    parts, refs = refs[:n_parts], refs[n_parts:]
    mask, high, low, inverse, carried, out, square = refs
    value = added(parts)
    solved, moved = project(
        value[:LANES], unpack_gram(value[LANES:]), mask[...], row_count, square
    )
    inverse[...] = solved
    carried[...] = moved
    mix(moved, high, low, out)


def last_kernel(row_count, n_parts, *refs):
    parts, refs = refs[:n_parts], refs[n_parts:]
    mask, member, kept, traded, basis, out = refs
    value = added(parts)
    solved = swap(eliminate(unpack_gram(value[LANES:]), mask[...], row_count))
    carried = exact(value[:LANES], block_diagonal(solved), NT) * (1.0 / row_count)
    cores = kept[member[0]]
    slices = cores.shape[1]
    own = jnp.concatenate([cores[0], cores[1]], axis=1)
    term = None
    for pair, both in enumerate((own, traded[...])):
        side = carried[pair * HALF : (pair + 1) * HALF]
        zero = jnp.zeros_like(side)
        both = exact(both, jnp.concatenate([pick(side, zero), pick(swap(side), zero)], axis=0))
        term = both if term is None else term + both
    out[pl.ds(0, slices), :] = pick(term, swap(basis[...]))
    out[pl.ds(slices, HALF), :] = solved


def place_kernel(position, member, mine, theirs, *refs):
    out, sems = refs[-2:]
    here = member[0]
    copies = [
        pltpu.make_async_copy(mine, out.at[here, position], sems.at[0]),
        pltpu.make_async_copy(theirs, out.at[1 - here, position], sems.at[1]),
    ]
    for copy in copies:
        copy.start()
    for copy in copies:
        copy.wait()


def final_kernel(position, member, mine, near, far, across, mixture, away, before, *refs):
    first, last, out, blocks, sems = refs
    here = member[0]
    slices = first.shape[1]
    copies = []
    for at, (place, value, terms) in enumerate(
        ((here, mixture, (mine, near)), (1 - here, away, (far, across)))
    ):
        weight = split(block_diagonal(terms[0][pl.ds(slices, HALF), :]))
        blocks[at] = dot3(split(value[...]), weight, NT)
        copy = pltpu.make_async_copy(blocks.at[at], out.at[place, position], sems.at[at])
        copy.start()
        copies.append(copy)
        head = terms[0][pl.ds(0, slices), :]
        first[place] = swap(head)[:, :HALF]
        last[place] = (head + terms[1][pl.ds(0, slices), :])[:, :HALF]
    for copy in copies:
        copy.wait()


def gram_kernel(mine, theirs, carried, kept, other, mixture, out, spread):
    count, rows = kept.shape[0], kept.shape[1]
    tiles = rows // 256
    mixture[...] = mine[...] + theirs[...]
    everything = mixture[...]
    gram = exact(everything, everything, TN)
    weight = split(carried[...])
    height = 2 * count * 32
    for tile in range(tiles):
        for sub in range(SUBLANES):
            packed = mixture[pl.ds(tile * 256 + sub, 32, stride=SUBLANES), :]
            crossed = swap(packed)
            zero = jnp.zeros_like(packed)
            blocks = jnp.concatenate(
                [pick(packed, zero), pick(crossed, zero), pick(zero, crossed), pick(zero, packed)],
                axis=0,
            )
            spread[pl.ds(tile * height * SUBLANES + sub, height, stride=SUBLANES), :] = dot3(
                weight, split(blocks)
            )
    raw = []
    for half, cores in enumerate((kept, other)):
        for index in range(count):
            s = half * count + index
            own = jnp.concatenate(
                [spread[pl.ds((tile * 2 * count + s) * 256, 256), :] for tile in range(tiles)],
                axis=0,
            )
            raw.append(dot3(split(cores[index]), split(own), TN))
    for pair in range(count):
        even, odd = raw[2 * pair], raw[2 * pair + 1]
        out[pl.ds(pair * HALF, HALF), :] = pick(even[:HALF], odd[HALF:]) + swap(
            pick(odd[:HALF], even[HALF:])
        )
    gram = gram[:HALF] + swap(gram[HALF:])
    out[pl.ds(2 * HALF, 32), :] = pick(gram[:32], swap(gram[32:]))


def basis_kernel(mixture, inverse, out):
    weight = split(block_diagonal(inverse[...]))
    out[...] = dot3(split(mixture[...]), weight, NT)


def kernel_call(body, outs, scratch, *operands, aliases=None, in_hbm=()):
    moved = sum(x.size * x.dtype.itemsize for x in (*operands, *outs))
    specs = []
    for at, x in enumerate((*operands, *outs)):
        space = pltpu.VMEM
        if at in in_hbm:
            space = pltpu.HBM
        elif x.dtype == jnp.int32:
            space = pltpu.SMEM
        specs.append(pl.BlockSpec(memory_space=space))
    return pl.pallas_call(
        body,
        out_shape=outs,
        in_specs=specs[: len(operands)],
        out_specs=specs[len(operands) :],
        scratch_shapes=scratch,
        input_output_aliases=aliases or {},
        compiler_params=pltpu.CompilerParams(vmem_limit_bytes=24 << 20),
        cost_estimate=pl.CostEstimate(flops=0, bytes_accessed=moved, transcendentals=0),
    )(*operands)


def shape(*dims, dtype=jnp.float32):
    return jax.ShapeDtypeStruct(dims, dtype)


def scratch(*dims):
    return pltpu.VMEM(dims, jnp.float32)


def in_rows(value):
    lead, (slices, width) = value.shape[:-2], value.shape[-2:]
    value = value.reshape(*lead, slices // SUBLANES, SUBLANES, width // LANES, LANES)
    value = jnp.swapaxes(value, -2, -3)
    return value.reshape(*lead, slices * width // LANES, LANES)


def out_of_rows(value, slices):
    lead, (rows, _) = value.shape[:-2], value.shape[-2:]
    value = value.reshape(*lead, slices // SUBLANES, rows // slices, SUBLANES, LANES)
    value = jnp.swapaxes(value, -2, -3)
    return value.reshape(*lead, slices, rows // slices * LANES)


def spread(value, axis, step):
    radix, stride = step
    return [value] + [flip(value, axis, other * stride) for other in range(1, radix)]


def exchanged(value, axis):
    steps = radices(lax.axis_size(axis))
    for at, (radix, stride) in enumerate(steps):
        parts = spread(value, axis, (radix, stride))
        if at < len(steps) - 1:
            value = sum(parts[1:], parts[0])
    return parts


def tiled(first_cores, mid_cores, last_cores, sketch_mid, sketch_last, ranks):
    members, count, slices, rank_size = first_cores.shape
    middle = mid_cores.shape[2]
    width = mid_cores.shape[4]
    total_slices = slices * lax.axis_size("mode")
    low = lax.axis_size("rep") // members
    member = lax.axis_index("rep") // low
    here = member[None].astype(jnp.int32)
    masks = (jnp.arange(rank_size, dtype=jnp.int32)[None, :] < ranks[:, None]).astype(jnp.float32)
    masks = jnp.concatenate([masks, masks], axis=1)[:, None, :]
    height = 2 * count * 32
    rows = slices * 32
    inner, outer = radices(lax.axis_size("mode"))

    def half_of(position, index):
        part = lax.dynamic_slice(
            mid_cores, (index, 0, position, 0, 0), (1, count, 1, slices, width)
        )
        return in_rows(part.reshape(count, slices, width))

    keep, send = kernel_call(
        start_kernel,
        [shape(count * 32 + slices, LANES), shape(count * 32 + 2 * slices, LANES)],
        [scratch(2 * height, LANES)],
        here,
        last_cores,
        first_cores,
        sketch_last,
    )
    keeps, sends = [keep], []
    sends.append(flip(send, "rep", low))
    for step in range(1, inner[0]):
        bits = step * inner[1]
        keeps.append(flip(keep, "mode", bits))
        pairs = [
            ((m * 2 * low + r), ((m ^ bits) * 2 * low + (r ^ low)))
            for m in range(lax.axis_size("mode"))
            for r in range(2 * low)
        ]
        sends.append(lax.ppermute(send, ("mode", "rep"), pairs))
    traded = sends[0][count * 32 + slices :]
    (part,) = kernel_call(
        functools.partial(merge_kernel, len(keeps), count * 32, slices),
        [shape(height + 2 * len(keeps) * slices, LANES)],
        [],
        *keeps,
        *sends,
    )
    cores = [None] * middle
    for position in range(middle - 1, -1, -1):
        sent = half_of(position, 1 - member)
        cores[position] = (
            half_of(position, member),
            flip(sent, "rep", low),
        )
    sketch_rows = in_rows(sketch_mid)
    mixed = [None] * middle
    heads = None
    for position in range(middle - 1, -1, -1):
        parts = exchanged(part, "mode") if heads else spread(part, "mode", outer)
        heads = heads or parts
        wide = shape(slices, height, LANES, dtype=jnp.bfloat16)
        part, *mixed[position] = kernel_call(
            functools.partial(sketch_kernel, len(parts)),
            [shape(height, LANES), wide, wide],
            [
                scratch(2 * height, LANES),
                scratch(height * slices, LANES),
                scratch(slices, HALF, LANES),
            ],
            *parts,
            masks[position + 1],
            *cores[position],
            sketch_rows[position],
        )
    parts = exchanged(part, "mode")
    (part,) = kernel_call(
        functools.partial(first_kernel, len(parts)),
        [shape(total_slices, LANES)],
        [scratch(2 * height, LANES)],
        *parts,
        *heads,
        masks[0],
    )
    square = scratch(count * HALF, LANES)
    near = flip(part, "rep", 1)
    inverse, carried, basis, part = kernel_call(
        functools.partial(bond_one_kernel, float(total_slices), len(heads)),
        [shape(HALF, LANES), shape(height, LANES), shape(slices, LANES), shape(rows, LANES)],
        [square],
        part,
        near,
        *heads,
        masks[0],
        *mixed[0],
    )
    row_count = float(total_slices * rank_size)
    whole = shape(members, middle, rows, LANES)
    blocks = ()
    for position in range(middle):
        near = flip(part, "rep", 1)
        mixture, part = kernel_call(
            gram_kernel,
            [shape(rows, LANES), shape(2 * HALF + 32, LANES)],
            [scratch(height * slices, LANES)],
            part,
            near,
            carried,
            *cores[position],
        )
        parts = exchanged(part, "mode")
        mask = masks[position + 1]
        if position < middle - 1:
            inverse, carried, part = kernel_call(
                functools.partial(bond_kernel, row_count, len(parts)),
                [shape(HALF, LANES), shape(height, LANES), shape(rows, LANES)],
                [square],
                *parts,
                mask,
                *mixed[position + 1],
            )
            (own,) = kernel_call(basis_kernel, [shape(rows, LANES)], [], mixture, inverse)
            other = flip(own, "rep", low)
            blocks = kernel_call(
                functools.partial(place_kernel, position),
                [whole],
                [pltpu.SemaphoreType.DMA((2,))],
                here,
                own,
                other,
                *blocks,
                aliases={3: 0} if blocks else None,
                in_hbm=(3, 4),
            )
    away = flip(mixture, "rep", low)
    (last,) = kernel_call(
        functools.partial(last_kernel, row_count, len(parts)),
        [shape(slices + HALF, LANES)],
        [],
        *parts,
        mask,
        here,
        last_cores,
        traded,
        basis,
    )
    near, far, across = (flip(last, "rep", bits) for bits in (1, low, low + 1))
    rounded_first, rounded_last, blocks = kernel_call(
        functools.partial(final_kernel, middle - 1),
        [shape(members, slices, rank_size), shape(members, slices, rank_size), whole],
        [pltpu.VMEM((2, rows, LANES), jnp.float32), pltpu.SemaphoreType.DMA((2,))],
        here,
        last,
        near,
        far,
        across,
        mixture,
        away,
        *blocks,
        aliases={7: 2},
        in_hbm=(7, 10),
    )
    return (rounded_first, out_of_rows(blocks, slices), rounded_last)


def per_device(*arguments):
    members, count, slices, rank_size = arguments[0].shape
    steps = radices(lax.axis_size("mode"))
    fits = (
        members == 2
        and count == 2
        and rank_size == HALF
        and slices % SUBLANES == 0
        and slices * lax.axis_size("mode") == LANES
        and lax.axis_size("rep") == 2 * members
        and len(steps) == 2
    )
    return tiled(*arguments) if fits else general(*arguments)


def solution(mesh):
    return jax.shard_map(
        per_device,
        mesh=mesh,
        in_specs=(
            P(None, "rep", "mode", None),
            P(None, "rep", None, "mode", None),
            P(None, "rep", "mode", None),
            P(None, "mode", None),
            P("mode", None),
            P(),
        ),
        out_specs=(P(None, "mode", None), P(None, None, "mode", None), P(None, "mode", None)),
        check_vma=False,
    )
```

```python
import functools

import jax
import jax.numpy as jnp
from jax import lax
from jax.experimental import pallas as pl
from jax.experimental.pallas import tpu as pltpu
from jax.sharding import PartitionSpec as P

PRECISE = lax.Precision.HIGHEST
FAST = lax.Precision.HIGH


def lower_inverse(gram_matrix):
    factor = jnp.linalg.cholesky(gram_matrix)
    identity = jnp.eye(gram_matrix.shape[-1], dtype=gram_matrix.dtype)
    return jax.scipy.linalg.solve_triangular(factor, identity, lower=True)


def flip(value, axis, bits):
    size = lax.axis_size(axis)
    return lax.ppermute(value, axis, [(index, index ^ bits) for index in range(size)])


def radices(size):
    stride, out = 1, []
    if (size.bit_length() - 1) % 2:
        out.append((2, stride))
        stride *= 2
    while stride < size:
        out.append((4, stride))
        stride *= 4
    return out


def total(value, axis, size=None):
    for radix, stride in radices(size or lax.axis_size(axis)):
        parts = [flip(value, axis, step * stride) for step in range(1, radix)]
        value = sum(parts, value)
    return value


def gathered(value, axis, dim):
    for radix, stride in radices(lax.axis_size(axis)):
        parts = [flip(value, axis, step * stride) for step in range(1, radix)]
        value = jnp.concatenate([value] + parts, axis=dim)
    return value


def general(first_cores, mid_cores, last_cores, sketch_mid, sketch_last, ranks):
    members, _, slices, rank_size = first_cores.shape
    middle = mid_cores.shape[2]
    total_slices = slices * lax.axis_size("mode")
    low = lax.axis_size("rep") // members
    member = lax.axis_index("rep") // low
    masks = (jnp.arange(rank_size, dtype=jnp.int32)[None, :] < ranks[:, None]).astype(jnp.float32)

    def own_and_other(value):
        kept = lax.dynamic_index_in_dim(value, member, 0, keepdims=False)
        sent = lax.dynamic_index_in_dim(value, 1 - member, 0, keepdims=False)
        return jnp.concatenate([kept, flip(sent, "rep", low)], axis=0)

    def both_members(value):
        other = flip(value, "rep", low)
        return jnp.stack(
            [jnp.where(member == 0, value, other), jnp.where(member == 0, other, value)]
        )

    last = own_and_other(last_cores)
    first = own_and_other(first_cores)
    cores = [None] * middle
    for position in range(middle - 1, -1, -1):
        cores[position] = own_and_other(
            mid_cores[:, :, position].reshape(members, -1, slices, rank_size, rank_size)
        )
    sketch_cores = sketch_mid.reshape(middle, slices, rank_size, rank_size)
    sketches = [None] * (middle + 1)
    mixed = [None] * middle
    sketches[middle] = (
        total(jnp.einsum("sic,ie->sce", last, sketch_last, precision=FAST), "mode") * masks[middle]
    )
    for position in range(middle - 1, -1, -1):
        mixed[position] = jnp.einsum(
            "sicd,sde->sice", cores[position], sketches[position + 1], precision=FAST
        )
        folded = jnp.einsum(
            "sice,ife->scf", mixed[position], sketch_cores[position], precision=FAST
        )
        sketches[position] = total(folded, "mode") * masks[position]

    everything = gathered(first, "mode", 1)
    mixture = total(
        jnp.einsum("sid,sde->ie", everything, sketches[0], precision=PRECISE), "rep", low
    )
    gram = jnp.einsum("ie,if->ef", mixture, mixture, precision=PRECISE)
    raw = jnp.einsum("ie,sid->sed", mixture, everything, precision=PRECISE)
    inverse = lower_inverse(gram / total_slices + jnp.diag(1.0 - masks[0]))
    carried = jnp.einsum("fe,sed->sfd", inverse, raw, precision=PRECISE) / total_slices
    basis = jnp.einsum("ie,fe->if", mixture[:slices], inverse, precision=PRECISE)
    rounded_first = both_members(basis)

    rows = total_slices * rank_size
    blocks = []
    for position in range(middle):
        mixture = total(
            jnp.einsum("sac,sice->iae", carried, mixed[position], precision=FAST), "rep", low
        )
        gram = jnp.einsum("iae,iaf->ef", mixture, mixture, precision=PRECISE)
        spread = jnp.einsum("sac,iae->sice", carried, mixture, precision=FAST)
        raw = jnp.einsum("sice,sicd->sed", spread, cores[position], precision=FAST)
        both = total(jnp.concatenate([raw, gram[None]], axis=0), "mode")
        raw, gram = both[:-1], both[-1]
        inverse = lower_inverse(gram / rows + jnp.diag(1.0 - masks[position + 1]))
        carried = jnp.einsum("fe,sed->sfd", inverse, raw, precision=PRECISE) / rows
        basis = jnp.einsum("iae,fe->iaf", mixture, inverse, precision=FAST)
        blocks.append(both_members(basis.reshape(slices, rank_size * rank_size)))
    rounded_mid = jnp.stack(blocks, axis=1)
    local_last = jnp.einsum("sac,sic->ia", carried, last, precision=PRECISE)
    rounded_last = both_members(total(local_last, "rep", low))
    return (rounded_first, rounded_mid, rounded_last)


LANES = 128
SUBLANES = 8
HALF = 64
NN = (((1,), (0,)), ((), ()))
NT = (((1,), (1,)), ((), ()))
TN = (((0,), (0,)), ((), ()))


def left_half(rows):
    return lax.broadcasted_iota(jnp.int32, (rows, LANES), 1) < HALF


def swap(value):
    return pltpu.roll(value, HALF, 1)


def pick(left, right):
    return jnp.where(left_half(left.shape[0]), left, right)


def split(value):
    high = value.astype(jnp.bfloat16)
    return high, (value - high.astype(jnp.float32)).astype(jnp.bfloat16)


def dot(left, right, dims=NN):
    return lax.dot_general(left, right, dims, preferred_element_type=jnp.float32)


def dot3(left, right, dims=NN):
    (lh, ll), (rh, rl) = left, right
    return dot(lh, rh, dims) + dot(lh, rl, dims) + dot(ll, rh, dims)


def exact(left, right, dims=NN):
    return lax.dot_general(
        left, right, dims, precision=PRECISE, preferred_element_type=jnp.float32
    )


def block_diagonal(value):
    zero = jnp.zeros_like(value)
    return jnp.concatenate([pick(value, zero), pick(zero, swap(value))], axis=0)


def spread_rows(packed, scratch):
    count = packed.shape[0]
    scratch[pl.ds(0, count, stride=2), :] = packed
    scratch[pl.ds(1, count, stride=2), :] = swap(packed)
    return scratch[pl.ds(0, 2 * count), :]


def start_kernel(member, *refs):
    sources, (keep, send), (*local, sems, scratch) = refs[:3], refs[3:5], refs[5:]
    copies = [
        pltpu.make_async_copy(source, target, sems.at[at])
        for at, (source, target) in enumerate(zip(sources, local))
    ]
    for copy in copies:
        copy.start()
    for copy in copies:
        copy.wait()
    last, first, sketch = local
    count = last.shape[1]
    for out, index in ((keep, member[0]), (send, 1 - member[0])):
        cores, heads = last[index], first[index]
        for s in range(count):
            scratch[pl.ds(s * HALF, HALF), pl.ds(0, HALF)] = exact(cores[s], sketch[...], TN)
        rows = count * 32
        even = scratch[pl.ds(0, rows, stride=2), :]
        odd = scratch[pl.ds(1, rows, stride=2), :]
        out[pl.ds(0, rows), :] = pick(even, swap(odd))
        slices = heads.shape[1]
        out[pl.ds(rows, slices), :] = jnp.concatenate([heads[0], heads[1]], axis=1)
        if out.shape[0] > rows + slices:
            out[pl.ds(rows + slices, slices), :] = jnp.concatenate([cores[0], cores[1]], axis=1)


def merge_kernel(n_parts, rows, slices, *refs):
    keeps, sends, out = refs[:n_parts], refs[n_parts : 2 * n_parts], refs[-1]
    for pair, parts in enumerate((keeps, sends)):
        out[pl.ds(pair * rows, rows), :] = added([part.at[pl.ds(0, rows)] for part in parts])
        for at, part in enumerate(parts):
            out[pl.ds(2 * rows + (pair * n_parts + at) * slices, slices), :] = part[
                pl.ds(rows, slices), :
            ]


def heads_of(parts, pair):
    rows = (parts[0].shape[0] - LANES) // 2
    return jnp.concatenate(
        [part[pl.ds(LANES + pair * rows, rows), :] for part in parts], axis=0
    )


def added(parts):
    value = parts[0][...]
    for part in parts[1:]:
        value = value + part[...]
    return value


def sketch_kernel(n_parts, *refs):
    parts, refs = refs[:n_parts], refs[n_parts:]
    mask, kept, other, sketch, out, high, low, wide, product, narrow = refs
    count = kept.shape[0]
    rows = kept.shape[1]
    tiles = rows // 256
    value = added([part.at[pl.ds(0, LANES)] for part in parts])
    natural = spread_rows(value * mask[...], wide)
    for half, cores in enumerate((kept, other)):
        for index in range(count):
            s = half * count + index
            weight = split(block_diagonal(natural[s * HALF : (s + 1) * HALF]))
            result = dot3(split(cores[index]), weight)
            for tile in range(tiles):
                product[pl.ds((tile * 2 * count + s) * 256, 256), :] = result[
                    tile * 256 : (tile + 1) * 256
                ]
    height = 2 * count * 32
    total_value = jnp.zeros(out.shape, jnp.float32)
    for tile in range(tiles):
        for sub in range(SUBLANES):
            i = tile * SUBLANES + sub
            packed = sketch[pl.ds(tile * 256 + sub, 32, stride=SUBLANES), :]
            weight = split(block_diagonal(spread_rows(packed, narrow.at[i])))
            own = split(product[pl.ds(tile * height * SUBLANES + sub, height, stride=SUBLANES), :])
            high[i] = own[0]
            low[i] = own[1]
            total_value = total_value + dot3(own, weight, NT)
    out[...] = total_value


def first_kernel(n_parts, *refs):
    parts, refs = refs[:n_parts], refs[n_parts:]
    heads, (mask, out, wide) = refs[:n_parts], refs[n_parts:]
    natural = spread_rows(added(parts) * mask[...], wide)
    natural = pick(natural, jnp.zeros_like(natural))
    value = exact(heads_of(heads, 0), natural[:LANES])
    out[...] = value + exact(heads_of(heads, 1), natural[LANES:])


def eliminate(gram, mask, row_count):
    size = gram.shape[0]
    row = lax.broadcasted_iota(jnp.int32, (size, LANES), 0)
    lane = lax.broadcasted_iota(jnp.int32, (size, LANES), 1)
    scaled = gram * (1.0 / row_count)
    diagonal = jnp.where(lane == row, 1.0 - mask, 0.0)
    work = jnp.where(lane < HALF, scaled + diagonal, jnp.where(lane - HALF == row, 1.0, 0.0))
    step = 4
    done = []
    for base in range(0, size, step):
        start = base - base % SUBLANES
        if base % SUBLANES == 0 and base:
            work = work[SUBLANES:]
        live = size - start
        offset = base - start
        columns = [
            jnp.broadcast_to(work[:, base + k : base + k + 1], (live, LANES)) for k in range(step)
        ]
        factors, pivots = [], []
        for k in range(step):
            at = offset + k
            column, pivot = columns[k], work[at : at + 1]
            for m in range(k):
                weight = factors[m][at : at + 1]
                column = column - factors[m] * weight
                pivot = pivot - pivots[m] * weight
            scale = lax.rsqrt(column[at : at + 1])
            factors.append(column * scale)
            pivots.append(pivot * scale)
        update = work
        for k in range(step):
            update = update - factors[k] * pivots[k]
        place = lax.broadcasted_iota(jnp.int32, (live, LANES), 0)
        work = jnp.where(place >= offset + step, update, work)
        for k in range(step):
            work = jnp.where(place == offset + k, pivots[k], work)
        if offset + step == SUBLANES:
            done.append(work[:SUBLANES])
    return jnp.concatenate(done, axis=0)


def project(raw, gram, mask, row_count, square):
    solved = eliminate(gram, mask, row_count)
    square[pl.ds(0, HALF), :] = solved
    planar = jnp.concatenate(
        [square[pl.ds(0, HALF // 2, stride=2), :], square[pl.ds(1, HALF // 2, stride=2), :]], axis=0
    )
    carried = exact(raw, block_diagonal(swap(planar)), NT) * (1.0 / row_count)
    square[...] = carried
    pairs = carried.shape[0] // HALF
    even = square[pl.ds(0, pairs * 32, stride=2), :]
    odd = square[pl.ds(1, pairs * 32, stride=2), :]
    first, second = pick(even, swap(odd)), pick(swap(even), odd)
    blocks = []
    for pair in range(pairs):
        blocks += [first[pair * 32 : (pair + 1) * 32], second[pair * 32 : (pair + 1) * 32]]
    return swap(solved), jnp.concatenate(blocks, axis=0)


def mix(carried, high, low, out):
    weight = split(carried.T)
    for i in range(high.shape[0]):
        tile, sub = i // SUBLANES, i % SUBLANES
        value = dot3(weight, (high[i], low[i]))
        straight = pick(value[0:32], value[96:128])
        crossed = pick(value[32:64], value[64:96])
        out[pl.ds(tile * 256 + sub, 32, stride=SUBLANES), :] = straight + swap(crossed)


def unpack_gram(packed):
    return jnp.concatenate([packed, swap(packed)], axis=0)


def bond_one_kernel(row_count, n_parts, kept, other, *refs):
    heads, (mask, high, low, *refs) = refs[:n_parts], refs[n_parts:]
    inverse, carried, basis, out, square = refs
    mixture = kept[...] + other[...]
    gram = exact(mixture, mixture, TN)[:HALF]
    raw = []
    for pair in range(2):
        value = exact(heads_of(heads, pair), mixture, TN)
        raw.append(pick(value[:HALF], swap(value[HALF:])))
    solved, moved = project(jnp.concatenate(raw, axis=0), gram, mask[...], row_count, square)
    inverse[...] = solved
    carried[...] = moved
    slices = basis.shape[0]
    full = jnp.concatenate([pick(solved, jnp.zeros_like(solved)), jnp.zeros_like(solved)], axis=0)
    basis[...] = exact(mixture[:slices], full, NT)
    mix(moved, high, low, out)


def bond_kernel(row_count, n_parts, *refs):
    parts, refs = refs[:n_parts], refs[n_parts:]
    mask, high, low, inverse, carried, out, square = refs
    value = added(parts)
    solved, moved = project(
        value[:LANES], unpack_gram(value[LANES:]), mask[...], row_count, square
    )
    inverse[...] = solved
    carried[...] = moved
    mix(moved, high, low, out)


def last_kernel(row_count, n_parts, *refs):
    parts, refs = refs[:n_parts], refs[n_parts:]
    mask, member, kept, traded, basis, out = refs
    value = added(parts)
    solved = swap(eliminate(unpack_gram(value[LANES:]), mask[...], row_count))
    carried = exact(value[:LANES], block_diagonal(solved), NT) * (1.0 / row_count)
    cores = kept[member[0]]
    slices = cores.shape[1]
    own = jnp.concatenate([cores[0], cores[1]], axis=1)
    term = None
    for pair, both in enumerate((own, traded[...])):
        side = carried[pair * HALF : (pair + 1) * HALF]
        zero = jnp.zeros_like(side)
        both = exact(both, jnp.concatenate([pick(side, zero), pick(swap(side), zero)], axis=0))
        term = both if term is None else term + both
    out[pl.ds(0, slices), :] = pick(term, swap(basis[...]))
    out[pl.ds(slices, HALF), :] = solved


def place_kernel(position, member, mine, theirs, *refs):
    out, sems = refs[-2:]
    here = member[0]
    copies = [
        pltpu.make_async_copy(mine, out.at[here, position], sems.at[0]),
        pltpu.make_async_copy(theirs, out.at[1 - here, position], sems.at[1]),
    ]
    for copy in copies:
        copy.start()
    for copy in copies:
        copy.wait()


def final_kernel(position, member, mine, near, far, across, mixture, away, before, *refs):
    first, last, out, blocks, sems = refs
    here = member[0]
    slices = first.shape[1]
    copies = []
    for at, (place, value, terms) in enumerate(
        ((here, mixture, (mine, near)), (1 - here, away, (far, across)))
    ):
        weight = split(block_diagonal(terms[0][pl.ds(slices, HALF), :]))
        blocks[at] = dot3(split(value[...]), weight, NT)
        copy = pltpu.make_async_copy(blocks.at[at], out.at[place, position], sems.at[at])
        copy.start()
        copies.append(copy)
        head = terms[0][pl.ds(0, slices), :]
        first[place] = swap(head)[:, :HALF]
        last[place] = (head + terms[1][pl.ds(0, slices), :])[:, :HALF]
    for copy in copies:
        copy.wait()


def gram_kernel(mine, theirs, carried, kept, other, mixture, out, spread):
    count, rows = kept.shape[0], kept.shape[1]
    tiles = rows // 256
    mixture[...] = mine[...] + theirs[...]
    everything = mixture[...]
    gram = exact(everything, everything, TN)
    weight = split(carried[...])
    height = 2 * count * 32
    for tile in range(tiles):
        for sub in range(SUBLANES):
            packed = mixture[pl.ds(tile * 256 + sub, 32, stride=SUBLANES), :]
            crossed = swap(packed)
            zero = jnp.zeros_like(packed)
            blocks = jnp.concatenate(
                [pick(packed, zero), pick(crossed, zero), pick(zero, crossed), pick(zero, packed)],
                axis=0,
            )
            spread[pl.ds(tile * height * SUBLANES + sub, height, stride=SUBLANES), :] = dot3(
                weight, split(blocks)
            )
    raw = []
    for half, cores in enumerate((kept, other)):
        for index in range(count):
            s = half * count + index
            own = jnp.concatenate(
                [spread[pl.ds((tile * 2 * count + s) * 256, 256), :] for tile in range(tiles)],
                axis=0,
            )
            raw.append(dot3(split(cores[index]), split(own), TN))
    for pair in range(count):
        even, odd = raw[2 * pair], raw[2 * pair + 1]
        out[pl.ds(pair * HALF, HALF), :] = pick(even[:HALF], odd[HALF:]) + swap(
            pick(odd[:HALF], even[HALF:])
        )
    gram = gram[:HALF] + swap(gram[HALF:])
    out[pl.ds(2 * HALF, 32), :] = pick(gram[:32], swap(gram[32:]))


def basis_kernel(mixture, inverse, out):
    weight = split(block_diagonal(inverse[...]))
    out[...] = dot3(split(mixture[...]), weight, NT)


def kernel_call(body, outs, scratch, *operands, aliases=None, in_hbm=(), limit=24 << 20):
    moved = sum(x.size * x.dtype.itemsize for x in (*operands, *outs))
    specs = []
    for at, x in enumerate((*operands, *outs)):
        space = pltpu.VMEM
        if at in in_hbm:
            space = pltpu.HBM
        elif x.dtype == jnp.int32:
            space = pltpu.SMEM
        specs.append(pl.BlockSpec(memory_space=space))
    return pl.pallas_call(
        body,
        out_shape=outs,
        in_specs=specs[: len(operands)],
        out_specs=specs[len(operands) :],
        scratch_shapes=scratch,
        input_output_aliases=aliases or {},
        compiler_params=pltpu.CompilerParams(vmem_limit_bytes=limit),
        cost_estimate=pl.CostEstimate(flops=0, bytes_accessed=moved, transcendentals=0),
    )(*operands)


def shape(*dims, dtype=jnp.float32):
    return jax.ShapeDtypeStruct(dims, dtype)


def scratch(*dims):
    return pltpu.VMEM(dims, jnp.float32)


def in_rows(value):
    lead, (slices, width) = value.shape[:-2], value.shape[-2:]
    value = value.reshape(*lead, slices // SUBLANES, SUBLANES, width // LANES, LANES)
    value = jnp.swapaxes(value, -2, -3)
    return value.reshape(*lead, slices * width // LANES, LANES)


def out_of_rows(value, slices):
    lead, (rows, _) = value.shape[:-2], value.shape[-2:]
    value = value.reshape(*lead, slices // SUBLANES, rows // slices, SUBLANES, LANES)
    value = jnp.swapaxes(value, -2, -3)
    return value.reshape(*lead, slices, rows // slices * LANES)


def spread(value, axis, step):
    radix, stride = step
    return [value] + [flip(value, axis, other * stride) for other in range(1, radix)]


def exchanged(value, axis):
    steps = radices(lax.axis_size(axis))
    for at, (radix, stride) in enumerate(steps):
        parts = spread(value, axis, (radix, stride))
        if at < len(steps) - 1:
            value = sum(parts[1:], parts[0])
    return parts


def tiled(first_cores, mid_cores, last_cores, sketch_mid, sketch_last, ranks):
    members, count, slices, rank_size = first_cores.shape
    middle = mid_cores.shape[2]
    width = mid_cores.shape[4]
    total_slices = slices * lax.axis_size("mode")
    low = lax.axis_size("rep") // members
    member = lax.axis_index("rep") // low
    here = member[None].astype(jnp.int32)
    masks = (jnp.arange(rank_size, dtype=jnp.int32)[None, :] < ranks[:, None]).astype(jnp.float32)
    masks = jnp.concatenate([masks, masks], axis=1)[:, None, :]
    height = 2 * count * 32
    rows = slices * 32
    inner, outer = radices(lax.axis_size("mode"))

    def half_of(source, position, index):
        part = lax.dynamic_slice(
            source, (index, 0, position, 0, 0), (1, count, 1, slices, width)
        )
        return in_rows(part.reshape(count, slices, width))

    keep, send = kernel_call(
        start_kernel,
        [shape(count * 32 + slices, LANES), shape(count * 32 + 2 * slices, LANES)],
        [
            scratch(*last_cores.shape),
            scratch(*first_cores.shape),
            scratch(*sketch_last.shape),
            pltpu.SemaphoreType.DMA((3,)),
            scratch(2 * height, LANES),
        ],
        here,
        last_cores,
        first_cores,
        sketch_last,
        in_hbm=(1, 2, 3),
        limit=None,
    )
    keeps, sends = [keep], []
    sends.append(flip(send, "rep", low))
    for step in range(1, inner[0]):
        bits = step * inner[1]
        keeps.append(flip(keep, "mode", bits))
        pairs = [
            ((m * 2 * low + r), ((m ^ bits) * 2 * low + (r ^ low)))
            for m in range(lax.axis_size("mode"))
            for r in range(2 * low)
        ]
        sends.append(lax.ppermute(send, ("mode", "rep"), pairs))
    traded = sends[0][count * 32 + slices :]
    (part,) = kernel_call(
        functools.partial(merge_kernel, len(keeps), count * 32, slices),
        [shape(height + 2 * len(keeps) * slices, LANES)],
        [],
        *keeps,
        *sends,
    )
    cores = [None] * middle
    late_cores, part = lax.optimization_barrier((mid_cores, part))
    for position in range(middle - 1, -1, -1):
        if position == middle - 1:
            sent = half_of(mid_cores, position, 1 - member)
        else:
            sent = half_of(late_cores, position, 1 - member)
        cores[position] = (half_of(late_cores, position, member), flip(sent, "rep", low))
    sketch_rows = in_rows(sketch_mid)
    mixed = [None] * middle
    heads = None
    for position in range(middle - 1, -1, -1):
        parts = exchanged(part, "mode") if heads else spread(part, "mode", outer)
        heads = heads or parts
        wide = shape(slices, height, LANES, dtype=jnp.bfloat16)
        part, *mixed[position] = kernel_call(
            functools.partial(sketch_kernel, len(parts)),
            [shape(height, LANES), wide, wide],
            [
                scratch(2 * height, LANES),
                scratch(height * slices, LANES),
                scratch(slices, HALF, LANES),
            ],
            *parts,
            masks[position + 1],
            *cores[position],
            sketch_rows[position],
        )
    parts = exchanged(part, "mode")
    (part,) = kernel_call(
        functools.partial(first_kernel, len(parts)),
        [shape(total_slices, LANES)],
        [scratch(2 * height, LANES)],
        *parts,
        *heads,
        masks[0],
    )
    square = scratch(count * HALF, LANES)
    near = flip(part, "rep", 1)
    inverse, carried, basis, part = kernel_call(
        functools.partial(bond_one_kernel, float(total_slices), len(heads)),
        [shape(HALF, LANES), shape(height, LANES), shape(slices, LANES), shape(rows, LANES)],
        [square],
        part,
        near,
        *heads,
        masks[0],
        *mixed[0],
    )
    row_count = float(total_slices * rank_size)
    whole = shape(members, middle, rows, LANES)
    blocks = ()
    for position in range(middle):
        near = flip(part, "rep", 1)
        mixture, part = kernel_call(
            gram_kernel,
            [shape(rows, LANES), shape(2 * HALF + 32, LANES)],
            [scratch(height * slices, LANES)],
            part,
            near,
            carried,
            *cores[position],
        )
        parts = exchanged(part, "mode")
        mask = masks[position + 1]
        if position < middle - 1:
            inverse, carried, part = kernel_call(
                functools.partial(bond_kernel, row_count, len(parts)),
                [shape(HALF, LANES), shape(height, LANES), shape(rows, LANES)],
                [square],
                *parts,
                mask,
                *mixed[position + 1],
            )
            (own,) = kernel_call(basis_kernel, [shape(rows, LANES)], [], mixture, inverse)
            other = flip(own, "rep", low)
            blocks = kernel_call(
                functools.partial(place_kernel, position),
                [whole],
                [pltpu.SemaphoreType.DMA((2,))],
                here,
                own,
                other,
                *blocks,
                aliases={3: 0} if blocks else None,
                in_hbm=(3, 4),
            )
    away = flip(mixture, "rep", low)
    (last,) = kernel_call(
        functools.partial(last_kernel, row_count, len(parts)),
        [shape(slices + HALF, LANES)],
        [],
        *parts,
        mask,
        here,
        last_cores,
        traded,
        basis,
    )
    near, far, across = (flip(last, "rep", bits) for bits in (1, low, low + 1))
    rounded_first, rounded_last, blocks = kernel_call(
        functools.partial(final_kernel, middle - 1),
        [shape(members, slices, rank_size), shape(members, slices, rank_size), whole],
        [pltpu.VMEM((2, rows, LANES), jnp.float32), pltpu.SemaphoreType.DMA((2,))],
        here,
        last,
        near,
        far,
        across,
        mixture,
        away,
        *blocks,
        aliases={7: 2},
        in_hbm=(7, 10),
    )
    return (rounded_first, out_of_rows(blocks, slices), rounded_last)


def per_device(*arguments):
    members, count, slices, rank_size = arguments[0].shape
    steps = radices(lax.axis_size("mode"))
    fits = (
        members == 2
        and count == 2
        and rank_size == HALF
        and slices % SUBLANES == 0
        and slices * lax.axis_size("mode") == LANES
        and lax.axis_size("rep") == 2 * members
        and len(steps) == 2
    )
    return tiled(*arguments) if fits else general(*arguments)


def solution(mesh):
    return jax.shard_map(
        per_device,
        mesh=mesh,
        in_specs=(
            P(None, "rep", "mode", None),
            P(None, "rep", None, "mode", None),
            P(None, "rep", "mode", None),
            P(None, "mode", None),
            P("mode", None),
            P(),
        ),
        out_specs=(P(None, "mode", None), P(None, None, "mode", None), P(None, "mode", None)),
        check_vma=False,
    )
```

```python
import functools

import jax
import jax.numpy as jnp
from jax import lax
from jax.experimental import pallas as pl
from jax.experimental.pallas import tpu as pltpu
from jax.sharding import PartitionSpec as P

PRECISE = lax.Precision.HIGHEST
FAST = lax.Precision.HIGH


def lower_inverse(gram_matrix):
    factor = jnp.linalg.cholesky(gram_matrix)
    identity = jnp.eye(gram_matrix.shape[-1], dtype=gram_matrix.dtype)
    return jax.scipy.linalg.solve_triangular(factor, identity, lower=True)


def flip(value, axis, bits):
    size = lax.axis_size(axis)
    return lax.ppermute(value, axis, [(index, index ^ bits) for index in range(size)])


def radices(size):
    stride, out = 1, []
    if (size.bit_length() - 1) % 2:
        out.append((2, stride))
        stride *= 2
    while stride < size:
        out.append((4, stride))
        stride *= 4
    return out


def total(value, axis, size=None):
    for radix, stride in radices(size or lax.axis_size(axis)):
        parts = [flip(value, axis, step * stride) for step in range(1, radix)]
        value = sum(parts, value)
    return value


def gathered(value, axis, dim):
    for radix, stride in radices(lax.axis_size(axis)):
        parts = [flip(value, axis, step * stride) for step in range(1, radix)]
        value = jnp.concatenate([value] + parts, axis=dim)
    return value


def general(first_cores, mid_cores, last_cores, sketch_mid, sketch_last, ranks):
    members, _, slices, rank_size = first_cores.shape
    middle = mid_cores.shape[2]
    total_slices = slices * lax.axis_size("mode")
    low = lax.axis_size("rep") // members
    member = lax.axis_index("rep") // low
    masks = (jnp.arange(rank_size, dtype=jnp.int32)[None, :] < ranks[:, None]).astype(jnp.float32)

    def own_and_other(value):
        kept = lax.dynamic_index_in_dim(value, member, 0, keepdims=False)
        sent = lax.dynamic_index_in_dim(value, 1 - member, 0, keepdims=False)
        return jnp.concatenate([kept, flip(sent, "rep", low)], axis=0)

    def both_members(value):
        other = flip(value, "rep", low)
        return jnp.stack(
            [jnp.where(member == 0, value, other), jnp.where(member == 0, other, value)]
        )

    last = own_and_other(last_cores)
    first = own_and_other(first_cores)
    cores = [None] * middle
    for position in range(middle - 1, -1, -1):
        cores[position] = own_and_other(
            mid_cores[:, :, position].reshape(members, -1, slices, rank_size, rank_size)
        )
    sketch_cores = sketch_mid.reshape(middle, slices, rank_size, rank_size)
    sketches = [None] * (middle + 1)
    mixed = [None] * middle
    sketches[middle] = (
        total(jnp.einsum("sic,ie->sce", last, sketch_last, precision=FAST), "mode") * masks[middle]
    )
    for position in range(middle - 1, -1, -1):
        mixed[position] = jnp.einsum(
            "sicd,sde->sice", cores[position], sketches[position + 1], precision=FAST
        )
        folded = jnp.einsum(
            "sice,ife->scf", mixed[position], sketch_cores[position], precision=FAST
        )
        sketches[position] = total(folded, "mode") * masks[position]

    everything = gathered(first, "mode", 1)
    mixture = total(
        jnp.einsum("sid,sde->ie", everything, sketches[0], precision=PRECISE), "rep", low
    )
    gram = jnp.einsum("ie,if->ef", mixture, mixture, precision=PRECISE)
    raw = jnp.einsum("ie,sid->sed", mixture, everything, precision=PRECISE)
    inverse = lower_inverse(gram / total_slices + jnp.diag(1.0 - masks[0]))
    carried = jnp.einsum("fe,sed->sfd", inverse, raw, precision=PRECISE) / total_slices
    basis = jnp.einsum("ie,fe->if", mixture[:slices], inverse, precision=PRECISE)
    rounded_first = both_members(basis)

    rows = total_slices * rank_size
    blocks = []
    for position in range(middle):
        mixture = total(
            jnp.einsum("sac,sice->iae", carried, mixed[position], precision=FAST), "rep", low
        )
        gram = jnp.einsum("iae,iaf->ef", mixture, mixture, precision=PRECISE)
        spread = jnp.einsum("sac,iae->sice", carried, mixture, precision=FAST)
        raw = jnp.einsum("sice,sicd->sed", spread, cores[position], precision=FAST)
        both = total(jnp.concatenate([raw, gram[None]], axis=0), "mode")
        raw, gram = both[:-1], both[-1]
        inverse = lower_inverse(gram / rows + jnp.diag(1.0 - masks[position + 1]))
        carried = jnp.einsum("fe,sed->sfd", inverse, raw, precision=PRECISE) / rows
        basis = jnp.einsum("iae,fe->iaf", mixture, inverse, precision=FAST)
        blocks.append(both_members(basis.reshape(slices, rank_size * rank_size)))
    rounded_mid = jnp.stack(blocks, axis=1)
    local_last = jnp.einsum("sac,sic->ia", carried, last, precision=PRECISE)
    rounded_last = both_members(total(local_last, "rep", low))
    return (rounded_first, rounded_mid, rounded_last)


LANES = 128
SUBLANES = 8
HALF = 64
NN = (((1,), (0,)), ((), ()))
NT = (((1,), (1,)), ((), ()))
TN = (((0,), (0,)), ((), ()))


def left_half(rows):
    return lax.broadcasted_iota(jnp.int32, (rows, LANES), 1) < HALF


def swap(value):
    return pltpu.roll(value, HALF, 1)


def pick(left, right):
    return jnp.where(left_half(left.shape[0]), left, right)


def split(value):
    high = value.astype(jnp.bfloat16)
    return high, (value - high.astype(jnp.float32)).astype(jnp.bfloat16)


def dot(left, right, dims=NN):
    return lax.dot_general(left, right, dims, preferred_element_type=jnp.float32)


def dot3(left, right, dims=NN):
    (lh, ll), (rh, rl) = left, right
    at_left, at_right = dims[0][0][0], dims[0][1][0]
    zero = jnp.zeros_like(rl)
    wide = jnp.concatenate(
        [
            jnp.concatenate([rh, rh], axis=at_right),
            jnp.concatenate([rl, zero], axis=at_right),
        ],
        axis=1 - at_right,
    )
    value = dot(jnp.concatenate([lh, ll], axis=at_left), wide, dims)
    return value[:, :LANES] + value[:, LANES:]


def exact(left, right, dims=NN):
    return lax.dot_general(
        left, right, dims, precision=PRECISE, preferred_element_type=jnp.float32
    )


def block_diagonal(value):
    zero = jnp.zeros_like(value)
    return jnp.concatenate([pick(value, zero), pick(zero, swap(value))], axis=0)


def spread_rows(packed, scratch):
    count = packed.shape[0]
    scratch[pl.ds(0, count, stride=2), :] = packed
    scratch[pl.ds(1, count, stride=2), :] = swap(packed)
    return scratch[pl.ds(0, 2 * count), :]


def start_kernel(member, *refs):
    sources, (keep, send), (*local, sems, scratch) = refs[:3], refs[3:5], refs[5:]
    copies = [
        pltpu.make_async_copy(source, target, sems.at[at])
        for at, (source, target) in enumerate(zip(sources, local))
    ]
    for copy in copies:
        copy.start()
    for copy in copies:
        copy.wait()
    last, first, sketch = local
    count = last.shape[1]
    for out, index in ((keep, member[0]), (send, 1 - member[0])):
        cores, heads = last[index], first[index]
        for s in range(count):
            scratch[pl.ds(s * HALF, HALF), pl.ds(0, HALF)] = exact(cores[s], sketch[...], TN)
        rows = count * 32
        even = scratch[pl.ds(0, rows, stride=2), :]
        odd = scratch[pl.ds(1, rows, stride=2), :]
        out[pl.ds(0, rows), :] = pick(even, swap(odd))
        slices = heads.shape[1]
        out[pl.ds(rows, slices), :] = jnp.concatenate([heads[0], heads[1]], axis=1)
        if out.shape[0] > rows + slices:
            out[pl.ds(rows + slices, slices), :] = jnp.concatenate([cores[0], cores[1]], axis=1)


def merge_kernel(n_parts, rows, slices, *refs):
    keeps, sends, out = refs[:n_parts], refs[n_parts : 2 * n_parts], refs[-1]
    for pair, parts in enumerate((keeps, sends)):
        out[pl.ds(pair * rows, rows), :] = added([part.at[pl.ds(0, rows)] for part in parts])
        for at, part in enumerate(parts):
            out[pl.ds(2 * rows + (pair * n_parts + at) * slices, slices), :] = part[
                pl.ds(rows, slices), :
            ]


def heads_of(parts, pair):
    rows = (parts[0].shape[0] - LANES) // 2
    return jnp.concatenate(
        [part[pl.ds(LANES + pair * rows, rows), :] for part in parts], axis=0
    )


def added(parts):
    value = parts[0][...]
    for part in parts[1:]:
        value = value + part[...]
    return value


def sketch_kernel(n_parts, *refs):
    parts, refs = refs[:n_parts], refs[n_parts:]
    mask, kept, other, sketch, out, high, low, wide, product, narrow = refs
    count = kept.shape[0]
    rows = kept.shape[1]
    tiles = rows // 256
    value = added([part.at[pl.ds(0, LANES)] for part in parts])
    natural = spread_rows(value * mask[...], wide)
    for half, cores in enumerate((kept, other)):
        for index in range(count):
            s = half * count + index
            weight = split(block_diagonal(natural[s * HALF : (s + 1) * HALF]))
            result = dot3(split(cores[index]), weight)
            for tile in range(tiles):
                product[pl.ds((tile * 2 * count + s) * 256, 256), :] = result[
                    tile * 256 : (tile + 1) * 256
                ]
    height = 2 * count * 32
    total_value = jnp.zeros(out.shape, jnp.float32)
    for tile in range(tiles):
        for sub in range(SUBLANES):
            i = tile * SUBLANES + sub
            packed = sketch[pl.ds(tile * 256 + sub, 32, stride=SUBLANES), :]
            weight = split(block_diagonal(spread_rows(packed, narrow.at[i])))
            own = split(product[pl.ds(tile * height * SUBLANES + sub, height, stride=SUBLANES), :])
            high[i] = own[0]
            low[i] = own[1]
            total_value = total_value + dot3(own, weight, NT)
    out[...] = total_value


def first_kernel(n_parts, *refs):
    parts, refs = refs[:n_parts], refs[n_parts:]
    heads, (mask, out, wide) = refs[:n_parts], refs[n_parts:]
    natural = spread_rows(added(parts) * mask[...], wide)
    natural = pick(natural, jnp.zeros_like(natural))
    value = exact(heads_of(heads, 0), natural[:LANES])
    out[...] = value + exact(heads_of(heads, 1), natural[LANES:])


def eliminate(gram, mask, row_count):
    size = gram.shape[0]
    row = lax.broadcasted_iota(jnp.int32, (size, LANES), 0)
    lane = lax.broadcasted_iota(jnp.int32, (size, LANES), 1)
    scaled = gram * (1.0 / row_count)
    unit = lax.rsqrt(jnp.broadcast_to(scaled[0:1, 0:1], (1, LANES)))
    scaled = scaled * unit * unit
    diagonal = jnp.where(lane == row, 1.0 - mask, 0.0)
    work = jnp.where(lane < HALF, scaled + diagonal, jnp.where(lane - HALF == row, 1.0, 0.0))
    done = []
    for base in range(0, size, SUBLANES):
        live = size - base
        columns = [
            jnp.broadcast_to(work[:, base + k : base + k + 1], (live, LANES))
            for k in range(SUBLANES)
        ]
        pivots = [work[k : k + 1] for k in range(SUBLANES)]
        for k in range(0, SUBLANES, 2):
            first, second = columns[k], columns[k + 1]
            a, b, c = first[k : k + 1], first[k + 1 : k + 2], second[k + 1 : k + 2]
            root = lax.rsqrt(a)
            next_root = lax.rsqrt(a * c - b * b) * (a * root)
            ratio = b * (root * root)
            columns[k : k + 2] = first * root, (second - first * ratio) * next_root
            pivots[k : k + 2] = pivots[k] * root, (pivots[k + 1] - pivots[k] * ratio) * next_root
            for m in range(k + 2, SUBLANES):
                for at in (k, k + 1):
                    weight = columns[at][m : m + 1]
                    columns[m] = columns[m] - columns[at] * weight
                    pivots[m] = pivots[m] - pivots[at] * weight
        done.append(jnp.concatenate(pivots, axis=0))
        work = work[SUBLANES:]
        for k in range(SUBLANES):
            work = work - columns[k][SUBLANES:] * pivots[k]
    return jnp.concatenate(done, axis=0) * unit


def project(raw, gram, mask, row_count, square):
    solved = eliminate(gram, mask, row_count)
    square[pl.ds(0, HALF), :] = solved
    planar = jnp.concatenate(
        [square[pl.ds(0, HALF // 2, stride=2), :], square[pl.ds(1, HALF // 2, stride=2), :]], axis=0
    )
    carried = exact(raw, block_diagonal(swap(planar)), NT) * (1.0 / row_count)
    square[...] = carried
    pairs = carried.shape[0] // HALF
    even = square[pl.ds(0, pairs * 32, stride=2), :]
    odd = square[pl.ds(1, pairs * 32, stride=2), :]
    first, second = pick(even, swap(odd)), pick(swap(even), odd)
    blocks = []
    for pair in range(pairs):
        blocks += [first[pair * 32 : (pair + 1) * 32], second[pair * 32 : (pair + 1) * 32]]
    return swap(solved), jnp.concatenate(blocks, axis=0)


def mix(carried, high, low, out):
    weight = split(carried.T)
    for i in range(high.shape[0]):
        tile, sub = i // SUBLANES, i % SUBLANES
        value = dot3(weight, (high[i], low[i]))
        straight = pick(value[0:32], value[96:128])
        crossed = pick(value[32:64], value[64:96])
        out[pl.ds(tile * 256 + sub, 32, stride=SUBLANES), :] = straight + swap(crossed)


def unpack_gram(packed):
    return jnp.concatenate([packed, swap(packed)], axis=0)


def bond_one_kernel(row_count, n_parts, kept, other, *refs):
    heads, (mask, high, low, *refs) = refs[:n_parts], refs[n_parts:]
    inverse, carried, basis, out, square = refs
    mixture = kept[...] + other[...]
    gram = exact(mixture, mixture, TN)[:HALF]
    raw = []
    for pair in range(2):
        value = exact(heads_of(heads, pair), mixture, TN)
        raw.append(pick(value[:HALF], swap(value[HALF:])))
    solved, moved = project(jnp.concatenate(raw, axis=0), gram, mask[...], row_count, square)
    inverse[...] = solved
    carried[...] = moved
    slices = basis.shape[0]
    full = jnp.concatenate([pick(solved, jnp.zeros_like(solved)), jnp.zeros_like(solved)], axis=0)
    basis[...] = exact(mixture[:slices], full, NT)
    mix(moved, high, low, out)


def bond_kernel(row_count, n_parts, *refs):
    parts, refs = refs[:n_parts], refs[n_parts:]
    mask, high, low, inverse, carried, out, square = refs
    value = added(parts)
    solved, moved = project(
        value[:LANES], unpack_gram(value[LANES:]), mask[...], row_count, square
    )
    inverse[...] = solved
    carried[...] = moved
    mix(moved, high, low, out)


def last_kernel(row_count, n_parts, *refs):
    parts, refs = refs[:n_parts], refs[n_parts:]
    mask, member, kept, traded, basis, out = refs
    value = added(parts)
    solved = swap(eliminate(unpack_gram(value[LANES:]), mask[...], row_count))
    carried = exact(value[:LANES], block_diagonal(solved), NT) * (1.0 / row_count)
    cores = kept[member[0]]
    slices = cores.shape[1]
    own = jnp.concatenate([cores[0], cores[1]], axis=1)
    term = None
    for pair, both in enumerate((own, traded[...])):
        side = carried[pair * HALF : (pair + 1) * HALF]
        zero = jnp.zeros_like(side)
        both = exact(both, jnp.concatenate([pick(side, zero), pick(swap(side), zero)], axis=0))
        term = both if term is None else term + both
    out[pl.ds(0, slices), :] = pick(term, swap(basis[...]))
    out[pl.ds(slices, HALF), :] = solved


def place_kernel(position, member, mine, theirs, *refs):
    out, sems = refs[-2:]
    here = member[0]
    copies = [
        pltpu.make_async_copy(mine, out.at[here, position], sems.at[0]),
        pltpu.make_async_copy(theirs, out.at[1 - here, position], sems.at[1]),
    ]
    for copy in copies:
        copy.start()
    for copy in copies:
        copy.wait()


def final_kernel(position, member, mine, near, far, across, mixture, away, before, *refs):
    first, last, out, blocks, sems = refs
    here = member[0]
    slices = first.shape[1]
    copies = []
    for at, (place, value, terms) in enumerate(
        ((here, mixture, (mine, near)), (1 - here, away, (far, across)))
    ):
        weight = split(block_diagonal(terms[0][pl.ds(slices, HALF), :]))
        blocks[at] = dot3(split(value[...]), weight, NT)
        copy = pltpu.make_async_copy(blocks.at[at], out.at[place, position], sems.at[at])
        copy.start()
        copies.append(copy)
        head = terms[0][pl.ds(0, slices), :]
        first[place] = swap(head)[:, :HALF]
        last[place] = (head + terms[1][pl.ds(0, slices), :])[:, :HALF]
    for copy in copies:
        copy.wait()


def gram_kernel(mine, theirs, carried, kept, other, mixture, out, spread):
    count, rows = kept.shape[0], kept.shape[1]
    tiles = rows // 256
    mixture[...] = mine[...] + theirs[...]
    everything = mixture[...]
    gram = exact(everything, everything, TN)
    weight = split(carried[...])
    height = 2 * count * 32
    for tile in range(tiles):
        for sub in range(SUBLANES):
            packed = mixture[pl.ds(tile * 256 + sub, 32, stride=SUBLANES), :]
            crossed = swap(packed)
            zero = jnp.zeros_like(packed)
            blocks = jnp.concatenate(
                [pick(packed, zero), pick(crossed, zero), pick(zero, crossed), pick(zero, packed)],
                axis=0,
            )
            spread[pl.ds(tile * height * SUBLANES + sub, height, stride=SUBLANES), :] = dot3(
                weight, split(blocks)
            )
    raw = []
    for half, cores in enumerate((kept, other)):
        for index in range(count):
            s = half * count + index
            own = jnp.concatenate(
                [spread[pl.ds((tile * 2 * count + s) * 256, 256), :] for tile in range(tiles)],
                axis=0,
            )
            raw.append(dot3(split(cores[index]), split(own), TN))
    for pair in range(count):
        even, odd = raw[2 * pair], raw[2 * pair + 1]
        out[pl.ds(pair * HALF, HALF), :] = pick(even[:HALF], odd[HALF:]) + swap(
            pick(odd[:HALF], even[HALF:])
        )
    gram = gram[:HALF] + swap(gram[HALF:])
    out[pl.ds(2 * HALF, 32), :] = pick(gram[:32], swap(gram[32:]))


def basis_kernel(mixture, inverse, out):
    weight = split(block_diagonal(inverse[...]))
    out[...] = dot3(split(mixture[...]), weight, NT)


def kernel_call(body, outs, scratch, *operands, aliases=None, in_hbm=(), limit=24 << 20):
    moved = sum(x.size * x.dtype.itemsize for x in (*operands, *outs))
    specs = []
    for at, x in enumerate((*operands, *outs)):
        space = pltpu.VMEM
        if at in in_hbm:
            space = pltpu.HBM
        elif x.dtype == jnp.int32:
            space = pltpu.SMEM
        specs.append(pl.BlockSpec(memory_space=space))
    return pl.pallas_call(
        body,
        out_shape=outs,
        in_specs=specs[: len(operands)],
        out_specs=specs[len(operands) :],
        scratch_shapes=scratch,
        input_output_aliases=aliases or {},
        compiler_params=pltpu.CompilerParams(vmem_limit_bytes=limit),
        cost_estimate=pl.CostEstimate(flops=0, bytes_accessed=moved, transcendentals=0),
    )(*operands)


def shape(*dims, dtype=jnp.float32):
    return jax.ShapeDtypeStruct(dims, dtype)


def scratch(*dims):
    return pltpu.VMEM(dims, jnp.float32)


def in_rows(value):
    lead, (slices, width) = value.shape[:-2], value.shape[-2:]
    value = value.reshape(*lead, slices // SUBLANES, SUBLANES, width // LANES, LANES)
    value = jnp.swapaxes(value, -2, -3)
    return value.reshape(*lead, slices * width // LANES, LANES)


def out_of_rows(value, slices):
    lead, (rows, _) = value.shape[:-2], value.shape[-2:]
    value = value.reshape(*lead, slices // SUBLANES, rows // slices, SUBLANES, LANES)
    value = jnp.swapaxes(value, -2, -3)
    return value.reshape(*lead, slices, rows // slices * LANES)


def spread(value, axis, step):
    radix, stride = step
    return [value] + [flip(value, axis, other * stride) for other in range(1, radix)]


def exchanged(value, axis):
    steps = radices(lax.axis_size(axis))
    for at, (radix, stride) in enumerate(steps):
        parts = spread(value, axis, (radix, stride))
        if at < len(steps) - 1:
            value = sum(parts[1:], parts[0])
    return parts


def tiled(first_cores, mid_cores, last_cores, sketch_mid, sketch_last, ranks):
    members, count, slices, rank_size = first_cores.shape
    middle = mid_cores.shape[2]
    width = mid_cores.shape[4]
    total_slices = slices * lax.axis_size("mode")
    low = lax.axis_size("rep") // members
    member = lax.axis_index("rep") // low
    here = member[None].astype(jnp.int32)
    masks = (jnp.arange(rank_size, dtype=jnp.int32)[None, :] < ranks[:, None]).astype(jnp.float32)
    masks = jnp.concatenate([masks, masks], axis=1)[:, None, :]
    height = 2 * count * 32
    rows = slices * 32
    inner, outer = radices(lax.axis_size("mode"))

    def half_of(source, position, index):
        part = lax.dynamic_slice(
            source, (index, 0, position, 0, 0), (1, count, 1, slices, width)
        )
        return in_rows(part.reshape(count, slices, width))

    keep, send = kernel_call(
        start_kernel,
        [shape(count * 32 + slices, LANES), shape(count * 32 + 2 * slices, LANES)],
        [
            scratch(*last_cores.shape),
            scratch(*first_cores.shape),
            scratch(*sketch_last.shape),
            pltpu.SemaphoreType.DMA((3,)),
            scratch(2 * height, LANES),
        ],
        here,
        last_cores,
        first_cores,
        sketch_last,
        in_hbm=(1, 2, 3),
        limit=None,
    )
    keeps, sends = [keep], []
    sends.append(flip(send, "rep", low))
    for step in range(1, inner[0]):
        bits = step * inner[1]
        keeps.append(flip(keep, "mode", bits))
        pairs = [
            ((m * 2 * low + r), ((m ^ bits) * 2 * low + (r ^ low)))
            for m in range(lax.axis_size("mode"))
            for r in range(2 * low)
        ]
        sends.append(lax.ppermute(send, ("mode", "rep"), pairs))
    traded = sends[0][count * 32 + slices :]
    (part,) = kernel_call(
        functools.partial(merge_kernel, len(keeps), count * 32, slices),
        [shape(height + 2 * len(keeps) * slices, LANES)],
        [],
        *keeps,
        *sends,
    )
    cores = [None] * middle
    late_cores, part = lax.optimization_barrier((mid_cores, part))
    for position in range(middle - 1, -1, -1):
        if position == middle - 1:
            sent = half_of(mid_cores, position, 1 - member)
        else:
            sent = half_of(late_cores, position, 1 - member)
        cores[position] = (half_of(late_cores, position, member), flip(sent, "rep", low))
    sketch_rows = in_rows(sketch_mid)
    mixed = [None] * middle
    heads = None
    for position in range(middle - 1, -1, -1):
        parts = exchanged(part, "mode") if heads else spread(part, "mode", outer)
        heads = heads or parts
        wide = shape(slices, height, LANES, dtype=jnp.bfloat16)
        part, *mixed[position] = kernel_call(
            functools.partial(sketch_kernel, len(parts)),
            [shape(height, LANES), wide, wide],
            [
                scratch(2 * height, LANES),
                scratch(height * slices, LANES),
                scratch(slices, HALF, LANES),
            ],
            *parts,
            masks[position + 1],
            *cores[position],
            sketch_rows[position],
        )
    parts = exchanged(part, "mode")
    (part,) = kernel_call(
        functools.partial(first_kernel, len(parts)),
        [shape(total_slices, LANES)],
        [scratch(2 * height, LANES)],
        *parts,
        *heads,
        masks[0],
    )
    square = scratch(count * HALF, LANES)
    near = flip(part, "rep", 1)
    inverse, carried, basis, part = kernel_call(
        functools.partial(bond_one_kernel, float(total_slices), len(heads)),
        [shape(HALF, LANES), shape(height, LANES), shape(slices, LANES), shape(rows, LANES)],
        [square],
        part,
        near,
        *heads,
        masks[0],
        *mixed[0],
    )
    row_count = float(total_slices * rank_size)
    whole = shape(members, middle, rows, LANES)
    blocks = ()
    for position in range(middle):
        near = flip(part, "rep", 1)
        mixture, part = kernel_call(
            gram_kernel,
            [shape(rows, LANES), shape(2 * HALF + 32, LANES)],
            [scratch(height * slices, LANES)],
            part,
            near,
            carried,
            *cores[position],
        )
        parts = exchanged(part, "mode")
        mask = masks[position + 1]
        if position < middle - 1:
            inverse, carried, part = kernel_call(
                functools.partial(bond_kernel, row_count, len(parts)),
                [shape(HALF, LANES), shape(height, LANES), shape(rows, LANES)],
                [square],
                *parts,
                mask,
                *mixed[position + 1],
            )
            (own,) = kernel_call(basis_kernel, [shape(rows, LANES)], [], mixture, inverse)
            other = flip(own, "rep", low)
            blocks = kernel_call(
                functools.partial(place_kernel, position),
                [whole],
                [pltpu.SemaphoreType.DMA((2,))],
                here,
                own,
                other,
                *blocks,
                aliases={3: 0} if blocks else None,
                in_hbm=(3, 4),
            )
    away = flip(mixture, "rep", low)
    (last,) = kernel_call(
        functools.partial(last_kernel, row_count, len(parts)),
        [shape(slices + HALF, LANES)],
        [],
        *parts,
        mask,
        here,
        last_cores,
        traded,
        basis,
    )
    near, far, across = (flip(last, "rep", bits) for bits in (1, low, low + 1))
    rounded_first, rounded_last, blocks = kernel_call(
        functools.partial(final_kernel, middle - 1),
        [shape(members, slices, rank_size), shape(members, slices, rank_size), whole],
        [pltpu.VMEM((2, rows, LANES), jnp.float32), pltpu.SemaphoreType.DMA((2,))],
        here,
        last,
        near,
        far,
        across,
        mixture,
        away,
        *blocks,
        aliases={7: 2},
        in_hbm=(7, 10),
    )
    return (rounded_first, out_of_rows(blocks, slices), rounded_last)


def per_device(*arguments):
    members, count, slices, rank_size = arguments[0].shape
    steps = radices(lax.axis_size("mode"))
    fits = (
        members == 2
        and count == 2
        and rank_size == HALF
        and slices % SUBLANES == 0
        and slices * lax.axis_size("mode") == LANES
        and lax.axis_size("rep") == 2 * members
        and len(steps) == 2
    )
    return tiled(*arguments) if fits else general(*arguments)


def solution(mesh):
    return jax.shard_map(
        per_device,
        mesh=mesh,
        in_specs=(
            P(None, "rep", "mode", None),
            P(None, "rep", None, "mode", None),
            P(None, "rep", "mode", None),
            P(None, "mode", None),
            P("mode", None),
            P(),
        ),
        out_specs=(P(None, "mode", None), P(None, None, "mode", None), P(None, "mode", None)),
        check_vma=False,
    )
```

```python
import functools

import jax
import jax.numpy as jnp
from jax import lax
from jax.experimental import pallas as pl
from jax.experimental.pallas import tpu as pltpu
from jax.sharding import PartitionSpec as P

PRECISE = lax.Precision.HIGHEST
FAST = lax.Precision.HIGH


def lower_inverse(gram_matrix):
    factor = jnp.linalg.cholesky(gram_matrix)
    identity = jnp.eye(gram_matrix.shape[-1], dtype=gram_matrix.dtype)
    return jax.scipy.linalg.solve_triangular(factor, identity, lower=True)


def flip(value, axis, bits):
    size = lax.axis_size(axis)
    return lax.ppermute(value, axis, [(index, index ^ bits) for index in range(size)])


def radices(size):
    stride, out = 1, []
    if (size.bit_length() - 1) % 2:
        out.append((2, stride))
        stride *= 2
    while stride < size:
        out.append((4, stride))
        stride *= 4
    return out


def total(value, axis, size=None):
    for radix, stride in radices(size or lax.axis_size(axis)):
        parts = [flip(value, axis, step * stride) for step in range(1, radix)]
        value = sum(parts, value)
    return value


def gathered(value, axis, dim):
    for radix, stride in radices(lax.axis_size(axis)):
        parts = [flip(value, axis, step * stride) for step in range(1, radix)]
        value = jnp.concatenate([value] + parts, axis=dim)
    return value


def general(first_cores, mid_cores, last_cores, sketch_mid, sketch_last, ranks):
    members, _, slices, rank_size = first_cores.shape
    middle = mid_cores.shape[2]
    total_slices = slices * lax.axis_size("mode")
    low = lax.axis_size("rep") // members
    member = lax.axis_index("rep") // low
    masks = (jnp.arange(rank_size, dtype=jnp.int32)[None, :] < ranks[:, None]).astype(jnp.float32)

    def own_and_other(value):
        kept = lax.dynamic_index_in_dim(value, member, 0, keepdims=False)
        sent = lax.dynamic_index_in_dim(value, 1 - member, 0, keepdims=False)
        return jnp.concatenate([kept, flip(sent, "rep", low)], axis=0)

    def both_members(value):
        other = flip(value, "rep", low)
        return jnp.stack(
            [jnp.where(member == 0, value, other), jnp.where(member == 0, other, value)]
        )

    last = own_and_other(last_cores)
    first = own_and_other(first_cores)
    cores = [None] * middle
    for position in range(middle - 1, -1, -1):
        cores[position] = own_and_other(
            mid_cores[:, :, position].reshape(members, -1, slices, rank_size, rank_size)
        )
    sketch_cores = sketch_mid.reshape(middle, slices, rank_size, rank_size)
    sketches = [None] * (middle + 1)
    mixed = [None] * middle
    sketches[middle] = (
        total(jnp.einsum("sic,ie->sce", last, sketch_last, precision=FAST), "mode") * masks[middle]
    )
    for position in range(middle - 1, -1, -1):
        mixed[position] = jnp.einsum(
            "sicd,sde->sice", cores[position], sketches[position + 1], precision=FAST
        )
        folded = jnp.einsum(
            "sice,ife->scf", mixed[position], sketch_cores[position], precision=FAST
        )
        sketches[position] = total(folded, "mode") * masks[position]

    everything = gathered(first, "mode", 1)
    mixture = total(
        jnp.einsum("sid,sde->ie", everything, sketches[0], precision=PRECISE), "rep", low
    )
    gram = jnp.einsum("ie,if->ef", mixture, mixture, precision=PRECISE)
    raw = jnp.einsum("ie,sid->sed", mixture, everything, precision=PRECISE)
    inverse = lower_inverse(gram / total_slices + jnp.diag(1.0 - masks[0]))
    carried = jnp.einsum("fe,sed->sfd", inverse, raw, precision=PRECISE) / total_slices
    basis = jnp.einsum("ie,fe->if", mixture[:slices], inverse, precision=PRECISE)
    rounded_first = both_members(basis)

    rows = total_slices * rank_size
    blocks = []
    for position in range(middle):
        mixture = total(
            jnp.einsum("sac,sice->iae", carried, mixed[position], precision=FAST), "rep", low
        )
        gram = jnp.einsum("iae,iaf->ef", mixture, mixture, precision=PRECISE)
        spread = jnp.einsum("sac,iae->sice", carried, mixture, precision=FAST)
        raw = jnp.einsum("sice,sicd->sed", spread, cores[position], precision=FAST)
        both = total(jnp.concatenate([raw, gram[None]], axis=0), "mode")
        raw, gram = both[:-1], both[-1]
        inverse = lower_inverse(gram / rows + jnp.diag(1.0 - masks[position + 1]))
        carried = jnp.einsum("fe,sed->sfd", inverse, raw, precision=PRECISE) / rows
        basis = jnp.einsum("iae,fe->iaf", mixture, inverse, precision=FAST)
        blocks.append(both_members(basis.reshape(slices, rank_size * rank_size)))
    rounded_mid = jnp.stack(blocks, axis=1)
    local_last = jnp.einsum("sac,sic->ia", carried, last, precision=PRECISE)
    rounded_last = both_members(total(local_last, "rep", low))
    return (rounded_first, rounded_mid, rounded_last)


LANES = 128
SUBLANES = 8
HALF = 64
NN = (((1,), (0,)), ((), ()))
NT = (((1,), (1,)), ((), ()))
TN = (((0,), (0,)), ((), ()))


def left_half(rows):
    return lax.broadcasted_iota(jnp.int32, (rows, LANES), 1) < HALF


def swap(value):
    return pltpu.roll(value, HALF, 1)


def pick(left, right):
    return jnp.where(left_half(left.shape[0]), left, right)


def split(value):
    high = value.astype(jnp.bfloat16)
    return high, (value - high.astype(jnp.float32)).astype(jnp.bfloat16)


def dot(left, right, dims=NN):
    return lax.dot_general(left, right, dims, preferred_element_type=jnp.float32)


def dot3(left, right, dims=NN):
    (lh, ll), (rh, rl) = left, right
    at_left, at_right = dims[0][0][0], dims[0][1][0]
    zero = jnp.zeros_like(rl)
    wide = jnp.concatenate(
        [
            jnp.concatenate([rh, rh], axis=at_right),
            jnp.concatenate([rl, zero], axis=at_right),
        ],
        axis=1 - at_right,
    )
    value = dot(jnp.concatenate([lh, ll], axis=at_left), wide, dims)
    return value[:, :LANES] + value[:, LANES:]


def exact(left, right, dims=NN):
    return lax.dot_general(
        left, right, dims, precision=PRECISE, preferred_element_type=jnp.float32
    )


def block_diagonal(value):
    zero = jnp.zeros_like(value)
    return jnp.concatenate([pick(value, zero), pick(zero, swap(value))], axis=0)


def spread_rows(packed, scratch):
    count = packed.shape[0]
    scratch[pl.ds(0, count, stride=2), :] = packed
    scratch[pl.ds(1, count, stride=2), :] = swap(packed)
    return scratch[pl.ds(0, 2 * count), :]


def start_kernel(member, *refs):
    sources, (keep, send), (*local, sems, scratch) = refs[:3], refs[3:5], refs[5:]
    copies = [
        pltpu.make_async_copy(source, target, sems.at[at])
        for at, (source, target) in enumerate(zip(sources, local))
    ]
    for copy in copies:
        copy.start()
    for copy in copies:
        copy.wait()
    last, first, sketch = local
    count = last.shape[1]
    for out, index in ((keep, member[0]), (send, 1 - member[0])):
        cores, heads = last[index], first[index]
        for s in range(count):
            scratch[pl.ds(s * HALF, HALF), pl.ds(0, HALF)] = exact(cores[s], sketch[...], TN)
        rows = count * 32
        even = scratch[pl.ds(0, rows, stride=2), :]
        odd = scratch[pl.ds(1, rows, stride=2), :]
        out[pl.ds(0, rows), :] = pick(even, swap(odd))
        slices = heads.shape[1]
        out[pl.ds(rows, slices), :] = jnp.concatenate([heads[0], heads[1]], axis=1)
        if out.shape[0] > rows + slices:
            out[pl.ds(rows + slices, slices), :] = jnp.concatenate([cores[0], cores[1]], axis=1)


def merge_kernel(n_parts, rows, slices, *refs):
    keeps, sends, out = refs[:n_parts], refs[n_parts : 2 * n_parts], refs[-1]
    for pair, parts in enumerate((keeps, sends)):
        out[pl.ds(pair * rows, rows), :] = added([part.at[pl.ds(0, rows)] for part in parts])
        for at, part in enumerate(parts):
            out[pl.ds(2 * rows + (pair * n_parts + at) * slices, slices), :] = part[
                pl.ds(rows, slices), :
            ]


def heads_of(parts, pair):
    rows = (parts[0].shape[0] - LANES) // 2
    return jnp.concatenate(
        [part[pl.ds(LANES + pair * rows, rows), :] for part in parts], axis=0
    )


def added(parts):
    value = parts[0][...]
    for part in parts[1:]:
        value = value + part[...]
    return value


def sketch_step(parts, mask, kept, other, sketch, high, low, wide, product, narrow):
    count = kept.shape[0]
    rows = kept.shape[1]
    tiles = rows // 256
    value = added([part.at[pl.ds(0, LANES)] for part in parts])
    natural = spread_rows(value * mask[...], wide)
    for half, cores in enumerate((kept, other)):
        for index in range(count):
            s = half * count + index
            weight = split(block_diagonal(natural[s * HALF : (s + 1) * HALF]))
            result = dot3(split(cores[index]), weight)
            for tile in range(tiles):
                product[pl.ds((tile * 2 * count + s) * 256, 256), :] = result[
                    tile * 256 : (tile + 1) * 256
                ]
    height = 2 * count * 32
    total_value = None
    for tile in range(tiles):
        for sub in range(SUBLANES):
            i = tile * SUBLANES + sub
            packed = sketch[pl.ds(tile * 256 + sub, 32, stride=SUBLANES), :]
            weight = split(block_diagonal(spread_rows(packed, narrow.at[i])))
            own = split(product[pl.ds(tile * height * SUBLANES + sub, height, stride=SUBLANES), :])
            high[i] = own[0]
            low[i] = own[1]
            term = dot3(own, weight, NT)
            total_value = term if total_value is None else total_value + term
    return total_value


def sketch_kernel(n_parts, *refs):
    parts, refs = refs[:n_parts], refs[n_parts:]
    mask, kept, other, sketch, out, *rest = refs
    out[...] = sketch_step(parts, mask, kept, other, sketch, *rest)


SHIFTS = (1, 3, 2)


def slice_blocks(spot, n_inner, n_outer):
    inner, outer = spot % n_inner, spot // n_inner
    return [
        (outer + n_outer - by) % n_outer * n_inner + (inner ^ step)
        for by in (0,) + SHIFTS
        for step in range(n_inner)
    ]


def block_rows(block, count):
    return pl.ds(pl.multiple_of(block * count, SUBLANES), count)


def first_kernel(n_parts, *refs, slices):
    parts, heads, refs = refs[:n_parts], refs[n_parts : 2 * n_parts], refs[2 * n_parts :]
    spot, mask, next_mask, kept, other, sketch, out, *rest = refs
    value = sketch_step(parts, mask, kept, other, sketch, *rest)
    natural = spread_rows(value * next_mask[...], rest[2])
    natural = pick(natural, jnp.zeros_like(natural))
    value = exact(heads_of(heads, 0), natural[:LANES])
    value = value + exact(heads_of(heads, 1), natural[LANES:])
    shared = rest[2]
    blocks = slice_blocks(spot[0], LANES // slices // n_parts, n_parts)
    for at, block in enumerate(blocks):
        shared[block_rows(block, slices), :] = value[at * slices : (at + 1) * slices]
    value = shared[pl.ds(0, LANES), :]
    out[...] = pick(value[:HALF], swap(value[HALF:]))


def eliminate(gram, mask, row_count):
    size = gram.shape[0]
    row = lax.broadcasted_iota(jnp.int32, (size, LANES), 0)
    lane = lax.broadcasted_iota(jnp.int32, (size, LANES), 1)
    scaled = gram * (1.0 / row_count)
    unit = lax.rsqrt(jnp.broadcast_to(scaled[0:1, 0:1], (1, LANES)))
    scaled = scaled * unit * unit
    diagonal = jnp.where(lane == row, 1.0 - mask, 0.0)
    work = jnp.where(lane < HALF, scaled + diagonal, jnp.where(lane - HALF == row, 1.0, 0.0))
    done = []
    for base in range(0, size, SUBLANES):
        live = size - base
        columns = [
            jnp.broadcast_to(work[:, base + k : base + k + 1], (live, LANES))
            for k in range(SUBLANES)
        ]
        pivots = [work[k : k + 1] for k in range(SUBLANES)]
        for k in range(0, SUBLANES, 2):
            first, second = columns[k], columns[k + 1]
            a, b, c = first[k : k + 1], first[k + 1 : k + 2], second[k + 1 : k + 2]
            root = lax.rsqrt(a)
            next_root = lax.rsqrt(a * c - b * b) * (a * root)
            ratio = b * (root * root)
            columns[k : k + 2] = first * root, (second - first * ratio) * next_root
            pivots[k : k + 2] = pivots[k] * root, (pivots[k + 1] - pivots[k] * ratio) * next_root
            for m in range(k + 2, SUBLANES):
                for at in (k, k + 1):
                    weight = columns[at][m : m + 1]
                    columns[m] = columns[m] - columns[at] * weight
                    pivots[m] = pivots[m] - pivots[at] * weight
        done.append(jnp.concatenate(pivots, axis=0))
        work = work[SUBLANES:]
        for k in range(SUBLANES):
            work = work - columns[k][SUBLANES:] * pivots[k]
    return jnp.concatenate(done, axis=0) * unit


def project(raw, gram, mask, row_count, square):
    solved = eliminate(gram, mask, row_count)
    square[pl.ds(0, HALF), :] = solved
    planar = jnp.concatenate(
        [square[pl.ds(0, HALF // 2, stride=2), :], square[pl.ds(1, HALF // 2, stride=2), :]], axis=0
    )
    carried = exact(raw, block_diagonal(swap(planar)), NT) * (1.0 / row_count)
    square[...] = carried
    pairs = carried.shape[0] // HALF
    even = square[pl.ds(0, pairs * 32, stride=2), :]
    odd = square[pl.ds(1, pairs * 32, stride=2), :]
    first, second = pick(even, swap(odd)), pick(swap(even), odd)
    blocks = []
    for pair in range(pairs):
        blocks += [first[pair * 32 : (pair + 1) * 32], second[pair * 32 : (pair + 1) * 32]]
    return swap(solved), jnp.concatenate(blocks, axis=0)


def mix(carried, high, low, out):
    weight = split(carried.T)
    for i in range(high.shape[0]):
        tile, sub = i // SUBLANES, i % SUBLANES
        value = dot3(weight, (high[i], low[i]))
        straight = pick(value[0:32], value[96:128])
        crossed = pick(value[32:64], value[64:96])
        out[pl.ds(tile * 256 + sub, 32, stride=SUBLANES), :] = straight + swap(crossed)


def unpack_gram(packed):
    return jnp.concatenate([packed, swap(packed)], axis=0)


def bond_one_kernel(row_count, n_parts, *refs):
    parts, heads, refs = refs[:n_parts], refs[n_parts : 2 * n_parts], refs[2 * n_parts :]
    spot, mask, high, low, inverse, carried, basis, out, square = refs
    packed = added(parts)
    zero = jnp.zeros_like(packed)
    square[...] = jnp.concatenate([pick(packed, zero), pick(swap(packed), zero)], axis=0)
    slices = basis.shape[0]
    blocks = slice_blocks(spot[0], LANES // slices // n_parts, n_parts)
    mixture = jnp.concatenate([square[block_rows(block, slices), :] for block in blocks], axis=0)
    gram = exact(mixture, mixture, TN)[:HALF]
    raw = []
    for pair in range(2):
        value = exact(heads_of(heads, pair), mixture, TN)
        raw.append(pick(value[:HALF], swap(value[HALF:])))
    solved, moved = project(jnp.concatenate(raw, axis=0), gram, mask[...], row_count, square)
    inverse[...] = solved
    carried[...] = moved
    full = jnp.concatenate([pick(solved, jnp.zeros_like(solved)), jnp.zeros_like(solved)], axis=0)
    basis[...] = exact(mixture[:slices], full, NT)
    mix(moved, high, low, out)


def bond_kernel(row_count, n_parts, *refs):
    parts, refs = refs[:n_parts], refs[n_parts:]
    mask, high, low, inverse, carried, out, square = refs
    value = added(parts)
    solved, moved = project(
        value[:LANES], unpack_gram(value[LANES:]), mask[...], row_count, square
    )
    inverse[...] = solved
    carried[...] = moved
    mix(moved, high, low, out)


def last_kernel(row_count, n_parts, *refs):
    parts, refs = refs[:n_parts], refs[n_parts:]
    mask, member, kept, traded, basis, out = refs
    value = added(parts)
    solved = swap(eliminate(unpack_gram(value[LANES:]), mask[...], row_count))
    carried = exact(value[:LANES], block_diagonal(solved), NT) * (1.0 / row_count)
    cores = kept[member[0]]
    slices = cores.shape[1]
    own = jnp.concatenate([cores[0], cores[1]], axis=1)
    term = None
    for pair, both in enumerate((own, traded[...])):
        side = carried[pair * HALF : (pair + 1) * HALF]
        zero = jnp.zeros_like(side)
        both = exact(both, jnp.concatenate([pick(side, zero), pick(swap(side), zero)], axis=0))
        term = both if term is None else term + both
    out[pl.ds(0, slices), :] = pick(term, swap(basis[...]))
    out[pl.ds(slices, HALF), :] = solved


def place_kernel(position, member, mine, theirs, *refs):
    out, sems = refs[-2:]
    here = member[0]
    copies = [
        pltpu.make_async_copy(mine, out.at[here, position], sems.at[0]),
        pltpu.make_async_copy(theirs, out.at[1 - here, position], sems.at[1]),
    ]
    for copy in copies:
        copy.start()
    for copy in copies:
        copy.wait()


def own_kernel(position, member, mine, mixture, before, *refs):
    out, block, sem = refs
    slices = mine.shape[0] - HALF
    weight = split(block_diagonal(mine[pl.ds(slices, HALF), :]))
    block[...] = dot3(split(mixture[...]), weight, NT)
    copy = pltpu.make_async_copy(block, out.at[member[0], position], sem)
    copy.start()
    copy.wait()


def final_kernel(position, member, mine, near, far, across, away, before, *refs):
    first, last, out, blocks, sems = refs
    here = member[0]
    slices = first.shape[1]
    weight = split(block_diagonal(far[pl.ds(slices, HALF), :]))
    count = blocks.shape[0]
    height = away.shape[0] // count
    copies = []
    for at in range(count):
        value = away[pl.ds(at * height, height), :]
        blocks[at] = dot3(split(value), weight, NT)
        place = out.at[1 - here, position, pl.ds(at * height, height), :]
        copies.append(pltpu.make_async_copy(blocks.at[at], place, sems.at[at]))
        copies[-1].start()
    for place, terms in ((here, (mine, near)), (1 - here, (far, across))):
        head = terms[0][pl.ds(0, slices), :]
        first[place] = swap(head)[:, :HALF]
        last[place] = (head + terms[1][pl.ds(0, slices), :])[:, :HALF]
    for copy in copies:
        copy.wait()


def gram_kernel(mine, theirs, carried, kept, other, mixture, out, spread):
    count, rows = kept.shape[0], kept.shape[1]
    tiles = rows // 256
    mixture[...] = mine[...] + theirs[...]
    everything = mixture[...]
    gram = exact(everything, everything, TN)
    weight = split(carried[...])
    height = 2 * count * 32
    for tile in range(tiles):
        for sub in range(SUBLANES):
            packed = mixture[pl.ds(tile * 256 + sub, 32, stride=SUBLANES), :]
            crossed = swap(packed)
            zero = jnp.zeros_like(packed)
            blocks = jnp.concatenate(
                [pick(packed, zero), pick(crossed, zero), pick(zero, crossed), pick(zero, packed)],
                axis=0,
            )
            spread[pl.ds(tile * height * SUBLANES + sub, height, stride=SUBLANES), :] = dot3(
                weight, split(blocks)
            )
    raw = []
    for half, cores in enumerate((kept, other)):
        for index in range(count):
            s = half * count + index
            own = jnp.concatenate(
                [spread[pl.ds((tile * 2 * count + s) * 256, 256), :] for tile in range(tiles)],
                axis=0,
            )
            raw.append(dot3(split(cores[index]), split(own), TN))
    for pair in range(count):
        even, odd = raw[2 * pair], raw[2 * pair + 1]
        out[pl.ds(pair * HALF, HALF), :] = pick(even[:HALF], odd[HALF:]) + swap(
            pick(odd[:HALF], even[HALF:])
        )
    gram = gram[:HALF] + swap(gram[HALF:])
    out[pl.ds(2 * HALF, 32), :] = pick(gram[:32], swap(gram[32:]))


def basis_kernel(mixture, inverse, out):
    weight = split(block_diagonal(inverse[...]))
    out[...] = dot3(split(mixture[...]), weight, NT)


def kernel_call(body, outs, scratch, *operands, aliases=None, in_hbm=(), limit=24 << 20):
    moved = sum(x.size * x.dtype.itemsize for x in (*operands, *outs))
    specs = []
    for at, x in enumerate((*operands, *outs)):
        space = pltpu.VMEM
        if at in in_hbm:
            space = pltpu.HBM
        elif x.dtype == jnp.int32:
            space = pltpu.SMEM
        specs.append(pl.BlockSpec(memory_space=space))
    return pl.pallas_call(
        body,
        out_shape=outs,
        in_specs=specs[: len(operands)],
        out_specs=specs[len(operands) :],
        scratch_shapes=scratch,
        input_output_aliases=aliases or {},
        compiler_params=pltpu.CompilerParams(vmem_limit_bytes=limit),
        cost_estimate=pl.CostEstimate(flops=0, bytes_accessed=moved, transcendentals=0),
    )(*operands)


def shape(*dims, dtype=jnp.float32):
    return jax.ShapeDtypeStruct(dims, dtype)


def scratch(*dims):
    return pltpu.VMEM(dims, jnp.float32)


def in_rows(value):
    lead, (slices, width) = value.shape[:-2], value.shape[-2:]
    value = value.reshape(*lead, slices // SUBLANES, SUBLANES, width // LANES, LANES)
    value = jnp.swapaxes(value, -2, -3)
    return value.reshape(*lead, slices * width // LANES, LANES)


def out_of_rows(value, slices):
    lead, (rows, _) = value.shape[:-2], value.shape[-2:]
    value = value.reshape(*lead, slices // SUBLANES, rows // slices, SUBLANES, LANES)
    value = jnp.swapaxes(value, -2, -3)
    return value.reshape(*lead, slices, rows // slices * LANES)


def spread(value, axis, step):
    radix, stride = step
    if radix == 2:
        return [value, flip(value, axis, stride)]
    size = lax.axis_size(axis)
    parts = [value]
    for by in SHIFTS:
        pairs = [
            (index, index + ((index // stride + by) % 4 - index // stride % 4) * stride)
            for index in range(size)
        ]
        parts.append(lax.ppermute(value, axis, pairs))
    return parts


def exchanged(value, axis):
    steps = radices(lax.axis_size(axis))
    for at, (radix, stride) in enumerate(steps):
        parts = spread(value, axis, (radix, stride))
        if at < len(steps) - 1:
            value = sum(parts[1:], parts[0])
    return parts


def tiled(first_cores, mid_cores, last_cores, sketch_mid, sketch_last, ranks):
    members, count, slices, rank_size = first_cores.shape
    middle = mid_cores.shape[2]
    width = mid_cores.shape[4]
    total_slices = slices * lax.axis_size("mode")
    low = lax.axis_size("rep") // members
    member = lax.axis_index("rep") // low
    here = member[None].astype(jnp.int32)
    spot = lax.axis_index("mode")[None].astype(jnp.int32)
    height = 2 * count * 32
    rows = slices * 32
    inner, outer = radices(lax.axis_size("mode"))

    def half_of(source, position, index):
        part = lax.dynamic_slice(
            source, (index, 0, position, 0, 0), (1, count, 1, slices, width)
        )
        return in_rows(part.reshape(count, slices, width))

    keep, send = kernel_call(
        start_kernel,
        [shape(count * 32 + slices, LANES), shape(count * 32 + 2 * slices, LANES)],
        [
            scratch(*last_cores.shape),
            scratch(*first_cores.shape),
            scratch(*sketch_last.shape),
            pltpu.SemaphoreType.DMA((3,)),
            scratch(2 * height, LANES),
        ],
        here,
        last_cores,
        first_cores,
        sketch_last,
        in_hbm=(1, 2, 3),
        limit=None,
    )
    keeps, sends = [keep], []
    sends.append(flip(send, "rep", low))
    for step in range(1, inner[0]):
        bits = step * inner[1]
        keeps.append(flip(keep, "mode", bits))
        pairs = [
            ((m * 2 * low + r), ((m ^ bits) * 2 * low + (r ^ low)))
            for m in range(lax.axis_size("mode"))
            for r in range(2 * low)
        ]
        sends.append(lax.ppermute(send, ("mode", "rep"), pairs))
    traded = sends[0][count * 32 + slices :]
    (part,) = kernel_call(
        functools.partial(merge_kernel, len(keeps), count * 32, slices),
        [shape(height + 2 * len(keeps) * slices, LANES)],
        [],
        *keeps,
        *sends,
    )
    cores = [None] * middle
    late_cores, late_sketch, late_ranks, part = lax.optimization_barrier(
        (mid_cores, sketch_mid, ranks, part)
    )
    masks = (jnp.arange(rank_size, dtype=jnp.int32)[None, :] < late_ranks[:, None]).astype(
        jnp.float32
    )
    masks = jnp.concatenate([masks, masks], axis=1)[:, None, :]
    sketch_rows = in_rows(late_sketch)
    sketch_rows = [sketch_rows[position] for position in range(middle)]
    for position in range(middle - 1, -1, -1):
        if position == middle - 1:
            sent = half_of(mid_cores, position, 1 - member)
        else:
            sent = half_of(late_cores, position, 1 - member)
        cores[position] = (half_of(late_cores, position, member), flip(sent, "rep", low))
    mixed = [None] * middle
    heads = None
    wide = shape(slices, height, LANES, dtype=jnp.bfloat16)
    for position in range(middle - 1, -1, -1):
        parts = exchanged(part, "mode") if heads else spread(part, "mode", outer)
        heads = heads or parts
        body, more, result = sketch_kernel, (), shape(height, LANES)
        if position == 0:
            body = functools.partial(first_kernel, slices=slices)
            more, result = (*heads, spot), shape(total_slices // 2, LANES)
        part, *mixed[position] = kernel_call(
            functools.partial(body, len(parts)),
            [result, wide, wide],
            [
                scratch(2 * height, LANES),
                scratch(height * slices, LANES),
                scratch(slices, HALF, LANES),
            ],
            *parts,
            *more,
            *((masks[1], masks[0]) if position == 0 else (masks[position + 1],)),
            *cores[position],
            sketch_rows[position],
        )
    square = scratch(count * HALF, LANES)
    part = part + flip(part, "rep", 1)
    parts = exchanged(part, "mode")
    inverse, carried, basis, part = kernel_call(
        functools.partial(bond_one_kernel, float(total_slices), len(parts)),
        [shape(HALF, LANES), shape(height, LANES), shape(slices, LANES), shape(rows, LANES)],
        [square],
        *parts,
        *heads,
        spot,
        masks[0],
        *mixed[0],
    )
    row_count = float(total_slices * rank_size)
    whole = shape(members, middle, rows, LANES)
    blocks = ()
    for position in range(middle):
        near = flip(part, "rep", 1)
        mixture, part = kernel_call(
            gram_kernel,
            [shape(rows, LANES), shape(2 * HALF + 32, LANES)],
            [scratch(height * slices, LANES)],
            part,
            near,
            carried,
            *cores[position],
        )
        parts = exchanged(part, "mode")
        mask = masks[position + 1]
        if position < middle - 1:
            inverse, carried, part = kernel_call(
                functools.partial(bond_kernel, row_count, len(parts)),
                [shape(HALF, LANES), shape(height, LANES), shape(rows, LANES)],
                [square],
                *parts,
                mask,
                *mixed[position + 1],
            )
            (own,) = kernel_call(basis_kernel, [shape(rows, LANES)], [], mixture, inverse)
            other = flip(own, "rep", low)
            blocks = kernel_call(
                functools.partial(place_kernel, position),
                [whole],
                [pltpu.SemaphoreType.DMA((2,))],
                here,
                own,
                other,
                *blocks,
                aliases={3: 0} if blocks else None,
                in_hbm=(3, 4),
            )
    away = flip(mixture, "rep", low)
    (last,) = kernel_call(
        functools.partial(last_kernel, row_count, len(parts)),
        [shape(slices + HALF, LANES)],
        [],
        *parts,
        mask,
        here,
        last_cores,
        traded,
        basis,
    )
    near, far, across = (flip(last, "rep", bits) for bits in (1, low, low + 1))
    blocks = kernel_call(
        functools.partial(own_kernel, middle - 1),
        [whole],
        [scratch(rows, LANES), pltpu.SemaphoreType.DMA],
        here,
        last,
        mixture,
        *blocks,
        aliases={3: 0},
        in_hbm=(3, 4),
    )
    pieces = slices // SUBLANES
    rounded_first, rounded_last, blocks = kernel_call(
        functools.partial(final_kernel, middle - 1),
        [shape(members, slices, rank_size), shape(members, slices, rank_size), whole],
        [scratch(pieces, rows // pieces, LANES), pltpu.SemaphoreType.DMA((pieces,))],
        here,
        last,
        near,
        far,
        across,
        away,
        *blocks,
        aliases={6: 2},
        in_hbm=(6, 9),
    )
    return (rounded_first, out_of_rows(blocks, slices), rounded_last)


def per_device(*arguments):
    members, count, slices, rank_size = arguments[0].shape
    steps = radices(lax.axis_size("mode"))
    fits = (
        members == 2
        and count == 2
        and rank_size == HALF
        and slices % SUBLANES == 0
        and slices * lax.axis_size("mode") == LANES
        and lax.axis_size("rep") == 2 * members
        and len(steps) == 2
    )
    return tiled(*arguments) if fits else general(*arguments)


def solution(mesh):
    return jax.shard_map(
        per_device,
        mesh=mesh,
        in_specs=(
            P(None, "rep", "mode", None),
            P(None, "rep", None, "mode", None),
            P(None, "rep", "mode", None),
            P(None, "mode", None),
            P("mode", None),
            P(),
        ),
        out_specs=(P(None, "mode", None), P(None, None, "mode", None), P(None, "mode", None)),
        check_vma=False,
    )
```

```python
import functools

import jax
import jax.numpy as jnp
from jax import lax
from jax.experimental import pallas as pl
from jax.experimental.pallas import tpu as pltpu
from jax.sharding import PartitionSpec as P

PRECISE = lax.Precision.HIGHEST
FAST = lax.Precision.HIGH


def lower_inverse(gram_matrix):
    factor = jnp.linalg.cholesky(gram_matrix)
    identity = jnp.eye(gram_matrix.shape[-1], dtype=gram_matrix.dtype)
    return jax.scipy.linalg.solve_triangular(factor, identity, lower=True)


def flip(value, axis, bits):
    size = lax.axis_size(axis)
    return lax.ppermute(value, axis, [(index, index ^ bits) for index in range(size)])


def radices(size):
    stride, out = 1, []
    if (size.bit_length() - 1) % 2:
        out.append((2, stride))
        stride *= 2
    while stride < size:
        out.append((4, stride))
        stride *= 4
    return out


def total(value, axis, size=None):
    for radix, stride in radices(size or lax.axis_size(axis)):
        parts = [flip(value, axis, step * stride) for step in range(1, radix)]
        value = sum(parts, value)
    return value


def gathered(value, axis, dim):
    for radix, stride in radices(lax.axis_size(axis)):
        parts = [flip(value, axis, step * stride) for step in range(1, radix)]
        value = jnp.concatenate([value] + parts, axis=dim)
    return value


def general(first_cores, mid_cores, last_cores, sketch_mid, sketch_last, ranks):
    members, _, slices, rank_size = first_cores.shape
    middle = mid_cores.shape[2]
    total_slices = slices * lax.axis_size("mode")
    low = lax.axis_size("rep") // members
    member = lax.axis_index("rep") // low
    masks = (jnp.arange(rank_size, dtype=jnp.int32)[None, :] < ranks[:, None]).astype(jnp.float32)

    def own_and_other(value):
        kept = lax.dynamic_index_in_dim(value, member, 0, keepdims=False)
        sent = lax.dynamic_index_in_dim(value, 1 - member, 0, keepdims=False)
        return jnp.concatenate([kept, flip(sent, "rep", low)], axis=0)

    def both_members(value):
        other = flip(value, "rep", low)
        return jnp.stack(
            [jnp.where(member == 0, value, other), jnp.where(member == 0, other, value)]
        )

    last = own_and_other(last_cores)
    first = own_and_other(first_cores)
    cores = [None] * middle
    for position in range(middle - 1, -1, -1):
        cores[position] = own_and_other(
            mid_cores[:, :, position].reshape(members, -1, slices, rank_size, rank_size)
        )
    sketch_cores = sketch_mid.reshape(middle, slices, rank_size, rank_size)
    sketches = [None] * (middle + 1)
    mixed = [None] * middle
    sketches[middle] = (
        total(jnp.einsum("sic,ie->sce", last, sketch_last, precision=FAST), "mode") * masks[middle]
    )
    for position in range(middle - 1, -1, -1):
        mixed[position] = jnp.einsum(
            "sicd,sde->sice", cores[position], sketches[position + 1], precision=FAST
        )
        folded = jnp.einsum(
            "sice,ife->scf", mixed[position], sketch_cores[position], precision=FAST
        )
        sketches[position] = total(folded, "mode") * masks[position]

    everything = gathered(first, "mode", 1)
    mixture = total(
        jnp.einsum("sid,sde->ie", everything, sketches[0], precision=PRECISE), "rep", low
    )
    gram = jnp.einsum("ie,if->ef", mixture, mixture, precision=PRECISE)
    raw = jnp.einsum("ie,sid->sed", mixture, everything, precision=PRECISE)
    inverse = lower_inverse(gram / total_slices + jnp.diag(1.0 - masks[0]))
    carried = jnp.einsum("fe,sed->sfd", inverse, raw, precision=PRECISE) / total_slices
    basis = jnp.einsum("ie,fe->if", mixture[:slices], inverse, precision=PRECISE)
    rounded_first = both_members(basis)

    rows = total_slices * rank_size
    blocks = []
    for position in range(middle):
        mixture = total(
            jnp.einsum("sac,sice->iae", carried, mixed[position], precision=FAST), "rep", low
        )
        gram = jnp.einsum("iae,iaf->ef", mixture, mixture, precision=PRECISE)
        spread = jnp.einsum("sac,iae->sice", carried, mixture, precision=FAST)
        raw = jnp.einsum("sice,sicd->sed", spread, cores[position], precision=FAST)
        both = total(jnp.concatenate([raw, gram[None]], axis=0), "mode")
        raw, gram = both[:-1], both[-1]
        inverse = lower_inverse(gram / rows + jnp.diag(1.0 - masks[position + 1]))
        carried = jnp.einsum("fe,sed->sfd", inverse, raw, precision=PRECISE) / rows
        basis = jnp.einsum("iae,fe->iaf", mixture, inverse, precision=FAST)
        blocks.append(both_members(basis.reshape(slices, rank_size * rank_size)))
    rounded_mid = jnp.stack(blocks, axis=1)
    local_last = jnp.einsum("sac,sic->ia", carried, last, precision=PRECISE)
    rounded_last = both_members(total(local_last, "rep", low))
    return (rounded_first, rounded_mid, rounded_last)


LANES = 128
SUBLANES = 8
HALF = 64
NN = (((1,), (0,)), ((), ()))
NT = (((1,), (1,)), ((), ()))
TN = (((0,), (0,)), ((), ()))


def left_half(rows):
    return lax.broadcasted_iota(jnp.int32, (rows, LANES), 1) < HALF


def swap(value):
    return pltpu.roll(value, HALF, 1)


def pick(left, right):
    return jnp.where(left_half(left.shape[0]), left, right)


def split(value):
    high = value.astype(jnp.bfloat16)
    return high, (value - high.astype(jnp.float32)).astype(jnp.bfloat16)


def dot(left, right, dims=NN):
    return lax.dot_general(left, right, dims, preferred_element_type=jnp.float32)


def dot3(left, right, dims=NN):
    (lh, ll), (rh, rl) = left, right
    at_left, at_right = dims[0][0][0], dims[0][1][0]
    zero = jnp.zeros_like(rl)
    wide = jnp.concatenate(
        [
            jnp.concatenate([rh, rh], axis=at_right),
            jnp.concatenate([rl, zero], axis=at_right),
        ],
        axis=1 - at_right,
    )
    value = dot(jnp.concatenate([lh, ll], axis=at_left), wide, dims)
    return value[:, :LANES] + value[:, LANES:]


def exact(left, right, dims=NN):
    return lax.dot_general(
        left, right, dims, precision=PRECISE, preferred_element_type=jnp.float32
    )


def block_diagonal(value):
    zero = jnp.zeros_like(value)
    return jnp.concatenate([pick(value, zero), pick(zero, swap(value))], axis=0)


def spread_rows(packed, scratch):
    count = packed.shape[0]
    scratch[pl.ds(0, count, stride=2), :] = packed
    scratch[pl.ds(1, count, stride=2), :] = swap(packed)
    return scratch[pl.ds(0, 2 * count), :]


def start_kernel(member, _, *refs):
    sources, (keep, send), (*local, sems, scratch) = refs[:3], refs[3:5], refs[5:]
    copies = [
        pltpu.make_async_copy(source, target, sems.at[at])
        for at, (source, target) in enumerate(zip(sources, local))
    ]
    for copy in copies:
        copy.start()
    for copy in copies:
        copy.wait()
    last, first, sketch = local
    count = last.shape[1]
    for out, index in ((keep, member[0]), (send, 1 - member[0])):
        cores, heads = last[index], first[index]
        for s in range(count):
            scratch[pl.ds(s * HALF, HALF), pl.ds(0, HALF)] = exact(cores[s], sketch[...], TN)
        rows = count * 32
        even = scratch[pl.ds(0, rows, stride=2), :]
        odd = scratch[pl.ds(1, rows, stride=2), :]
        out[pl.ds(0, rows), :] = pick(even, swap(odd))
        slices = heads.shape[1]
        out[pl.ds(rows, slices), :] = jnp.concatenate([heads[0], heads[1]], axis=1)
        if out.shape[0] > rows + slices:
            out[pl.ds(rows + slices, slices), :] = jnp.concatenate([cores[0], cores[1]], axis=1)


def merge_kernel(n_parts, rows, slices, *refs):
    keeps, sends, out = refs[:n_parts], refs[n_parts : 2 * n_parts], refs[-1]
    for pair, parts in enumerate((keeps, sends)):
        out[pl.ds(pair * rows, rows), :] = added([part.at[pl.ds(0, rows)] for part in parts])
        for at, part in enumerate(parts):
            out[pl.ds(2 * rows + (pair * n_parts + at) * slices, slices), :] = part[
                pl.ds(rows, slices), :
            ]


def heads_of(parts, pair):
    rows = (parts[0].shape[0] - LANES) // 2
    return jnp.concatenate(
        [part[pl.ds(LANES + pair * rows, rows), :] for part in parts], axis=0
    )


def added(parts):
    value = parts[0][...]
    for part in parts[1:]:
        value = value + part[...]
    return value


def sketch_step(parts, mask, kept, other, sketch, high, low, wide, product, narrow):
    count = kept.shape[0]
    rows = kept.shape[1]
    tiles = rows // 256
    value = added([part.at[pl.ds(0, LANES)] for part in parts])
    natural = spread_rows(value * mask[...], wide)
    for half, cores in enumerate((kept, other)):
        for index in range(count):
            s = half * count + index
            weight = split(block_diagonal(natural[s * HALF : (s + 1) * HALF]))
            result = dot3(split(cores[index]), weight)
            for tile in range(tiles):
                product[pl.ds((tile * 2 * count + s) * 256, 256), :] = result[
                    tile * 256 : (tile + 1) * 256
                ]
    height = 2 * count * 32
    total_value = None
    for tile in range(tiles):
        for sub in range(SUBLANES):
            i = tile * SUBLANES + sub
            packed = sketch[pl.ds(tile * 256 + sub, 32, stride=SUBLANES), :]
            weight = split(block_diagonal(spread_rows(packed, narrow.at[i])))
            own = split(product[pl.ds(tile * height * SUBLANES + sub, height, stride=SUBLANES), :])
            high[i] = own[0]
            low[i] = own[1]
            term = dot3(own, weight, NT)
            total_value = term if total_value is None else total_value + term
    return total_value


def sketch_kernel(n_parts, *refs):
    parts, refs = refs[:n_parts], refs[n_parts:]
    mask, kept, other, sketch, out, *rest = refs
    out[...] = sketch_step(parts, mask, kept, other, sketch, *rest)


SHIFTS = (1, 3, 2)


def slice_blocks(spot, n_inner, n_outer):
    inner, outer = spot % n_inner, spot // n_inner
    return [
        (outer + n_outer - by) % n_outer * n_inner + (inner ^ step)
        for by in (0,) + SHIFTS
        for step in range(n_inner)
    ]


def block_rows(block, count):
    return pl.ds(pl.multiple_of(block * count, SUBLANES), count)


def first_kernel(n_parts, *refs, slices):
    parts, heads, refs = refs[:n_parts], refs[n_parts : 2 * n_parts], refs[2 * n_parts :]
    spot, mask, next_mask, kept, other, sketch, out, *rest = refs
    value = sketch_step(parts, mask, kept, other, sketch, *rest)
    natural = spread_rows(value * next_mask[...], rest[2])
    natural = pick(natural, jnp.zeros_like(natural))
    value = exact(heads_of(heads, 0), natural[:LANES])
    value = value + exact(heads_of(heads, 1), natural[LANES:])
    shared = rest[2]
    blocks = slice_blocks(spot[0], LANES // slices // n_parts, n_parts)
    for at, block in enumerate(blocks):
        shared[block_rows(block, slices), :] = value[at * slices : (at + 1) * slices]
    value = shared[pl.ds(0, LANES), :]
    out[...] = pick(value[:HALF], swap(value[HALF:]))


def eliminate(gram, mask, row_count):
    size = gram.shape[0]
    row = lax.broadcasted_iota(jnp.int32, (size, LANES), 0)
    lane = lax.broadcasted_iota(jnp.int32, (size, LANES), 1)
    scaled = gram * (1.0 / row_count)
    unit = lax.rsqrt(jnp.broadcast_to(scaled[0:1, 0:1], (1, LANES)))
    scaled = scaled * unit * unit
    diagonal = jnp.where(lane == row, 1.0 - mask, 0.0)
    work = jnp.where(lane < HALF, scaled + diagonal, jnp.where(lane - HALF == row, 1.0, 0.0))
    done = []
    for base in range(0, size, SUBLANES):
        live = size - base
        columns = [
            jnp.broadcast_to(work[:, base + k : base + k + 1], (live, LANES))
            for k in range(SUBLANES)
        ]
        pivots = [work[k : k + 1] for k in range(SUBLANES)]
        for k in range(0, SUBLANES, 2):
            first, second = columns[k], columns[k + 1]
            a, b, c = first[k : k + 1], first[k + 1 : k + 2], second[k + 1 : k + 2]
            root = lax.rsqrt(a)
            next_root = lax.rsqrt(a * c - b * b) * (a * root)
            ratio = b * (root * root)
            columns[k : k + 2] = first * root, (second - first * ratio) * next_root
            pivots[k : k + 2] = pivots[k] * root, (pivots[k + 1] - pivots[k] * ratio) * next_root
            for m in range(k + 2, SUBLANES):
                for at in (k, k + 1):
                    weight = columns[at][m : m + 1]
                    columns[m] = columns[m] - columns[at] * weight
                    pivots[m] = pivots[m] - pivots[at] * weight
        done.append(jnp.concatenate(pivots, axis=0))
        work = work[SUBLANES:]
        for k in range(SUBLANES):
            work = work - columns[k][SUBLANES:] * pivots[k]
    return jnp.concatenate(done, axis=0) * unit


def project(raw, gram, mask, row_count, square):
    solved = eliminate(gram, mask, row_count)
    square[pl.ds(0, HALF), :] = solved
    planar = jnp.concatenate(
        [square[pl.ds(0, HALF // 2, stride=2), :], square[pl.ds(1, HALF // 2, stride=2), :]], axis=0
    )
    carried = exact(raw, block_diagonal(swap(planar)), NT) * (1.0 / row_count)
    square[...] = carried
    pairs = carried.shape[0] // HALF
    even = square[pl.ds(0, pairs * 32, stride=2), :]
    odd = square[pl.ds(1, pairs * 32, stride=2), :]
    first, second = pick(even, swap(odd)), pick(swap(even), odd)
    blocks = []
    for pair in range(pairs):
        blocks += [first[pair * 32 : (pair + 1) * 32], second[pair * 32 : (pair + 1) * 32]]
    return swap(solved), jnp.concatenate(blocks, axis=0)


def mix(carried, high, low, out):
    weight = split(carried.T)
    for i in range(high.shape[0]):
        tile, sub = i // SUBLANES, i % SUBLANES
        value = dot3(weight, (high[i], low[i]))
        straight = pick(value[0:32], value[96:128])
        crossed = pick(value[32:64], value[64:96])
        out[pl.ds(tile * 256 + sub, 32, stride=SUBLANES), :] = straight + swap(crossed)


def unpack_gram(packed):
    return jnp.concatenate([packed, swap(packed)], axis=0)


def bond_one_kernel(row_count, n_parts, *refs):
    parts, heads, refs = refs[:n_parts], refs[n_parts : 2 * n_parts], refs[2 * n_parts :]
    spot, mask, high, low, inverse, carried, basis, out, square = refs
    packed = added(parts)
    zero = jnp.zeros_like(packed)
    square[...] = jnp.concatenate([pick(packed, zero), pick(swap(packed), zero)], axis=0)
    slices = basis.shape[0]
    blocks = slice_blocks(spot[0], LANES // slices // n_parts, n_parts)
    mixture = jnp.concatenate([square[block_rows(block, slices), :] for block in blocks], axis=0)
    gram = exact(mixture, mixture, TN)[:HALF]
    raw = []
    for pair in range(2):
        value = exact(heads_of(heads, pair), mixture, TN)
        raw.append(pick(value[:HALF], swap(value[HALF:])))
    solved, moved = project(jnp.concatenate(raw, axis=0), gram, mask[...], row_count, square)
    inverse[...] = solved
    carried[...] = moved
    full = jnp.concatenate([pick(solved, jnp.zeros_like(solved)), jnp.zeros_like(solved)], axis=0)
    basis[...] = exact(mixture[:slices], full, NT)
    mix(moved, high, low, out)


def bond_kernel(row_count, n_parts, *refs):
    parts, refs = refs[:n_parts], refs[n_parts:]
    mask, high, low, inverse, carried, out, square = refs
    value = added(parts)
    solved, moved = project(
        value[:LANES], unpack_gram(value[LANES:]), mask[...], row_count, square
    )
    inverse[...] = solved
    carried[...] = moved
    mix(moved, high, low, out)


def last_kernel(row_count, n_parts, *refs):
    parts, refs = refs[:n_parts], refs[n_parts:]
    mask, member, kept, traded, basis, out = refs
    value = added(parts)
    solved = swap(eliminate(unpack_gram(value[LANES:]), mask[...], row_count))
    carried = exact(value[:LANES], block_diagonal(solved), NT) * (1.0 / row_count)
    cores = kept[member[0]]
    slices = cores.shape[1]
    own = jnp.concatenate([cores[0], cores[1]], axis=1)
    term = None
    for pair, both in enumerate((own, traded[...])):
        side = carried[pair * HALF : (pair + 1) * HALF]
        zero = jnp.zeros_like(side)
        both = exact(both, jnp.concatenate([pick(side, zero), pick(swap(side), zero)], axis=0))
        term = both if term is None else term + both
    out[pl.ds(0, slices), :] = pick(term, swap(basis[...]))
    out[pl.ds(slices, HALF), :] = solved


def place_kernel(position, member, mine, theirs, *refs):
    out, sems = refs[-2:]
    here = member[0]
    copies = [
        pltpu.make_async_copy(mine, out.at[here, position], sems.at[0]),
        pltpu.make_async_copy(theirs, out.at[1 - here, position], sems.at[1]),
    ]
    for copy in copies:
        copy.start()
    for copy in copies:
        copy.wait()


def own_kernel(position, member, mine, mixture, before, *refs):
    out, block, sem = refs
    slices = mine.shape[0] - HALF
    weight = split(block_diagonal(mine[pl.ds(slices, HALF), :]))
    block[...] = dot3(split(mixture[...]), weight, NT)
    copy = pltpu.make_async_copy(block, out.at[member[0], position], sem)
    copy.start()
    copy.wait()


def final_kernel(position, member, mine, near, far, across, away, before, *refs):
    first, last, out, blocks, sems = refs
    here = member[0]
    slices = first.shape[1]
    weight = split(block_diagonal(far[pl.ds(slices, HALF), :]))
    count = blocks.shape[0]
    height = away.shape[0] // count
    copies = []
    for at in range(count):
        value = away[pl.ds(at * height, height), :]
        blocks[at] = dot3(split(value), weight, NT)
        place = out.at[1 - here, position, pl.ds(at * height, height), :]
        copies.append(pltpu.make_async_copy(blocks.at[at], place, sems.at[at]))
        copies[-1].start()
    for place, terms in ((here, (mine, near)), (1 - here, (far, across))):
        head = terms[0][pl.ds(0, slices), :]
        first[place] = swap(head)[:, :HALF]
        last[place] = (head + terms[1][pl.ds(0, slices), :])[:, :HALF]
    for copy in copies:
        copy.wait()


def gram_kernel(mine, theirs, carried, kept, other, mixture, out, spread):
    count, rows = kept.shape[0], kept.shape[1]
    tiles = rows // 256
    mixture[...] = mine[...] + theirs[...]
    everything = mixture[...]
    gram = exact(everything, everything, TN)
    weight = split(carried[...])
    height = 2 * count * 32
    for tile in range(tiles):
        for sub in range(SUBLANES):
            packed = mixture[pl.ds(tile * 256 + sub, 32, stride=SUBLANES), :]
            crossed = swap(packed)
            zero = jnp.zeros_like(packed)
            blocks = jnp.concatenate(
                [pick(packed, zero), pick(crossed, zero), pick(zero, crossed), pick(zero, packed)],
                axis=0,
            )
            spread[pl.ds(tile * height * SUBLANES + sub, height, stride=SUBLANES), :] = dot3(
                weight, split(blocks)
            )
    raw = []
    for half, cores in enumerate((kept, other)):
        for index in range(count):
            s = half * count + index
            own = jnp.concatenate(
                [spread[pl.ds((tile * 2 * count + s) * 256, 256), :] for tile in range(tiles)],
                axis=0,
            )
            raw.append(dot3(split(cores[index]), split(own), TN))
    for pair in range(count):
        even, odd = raw[2 * pair], raw[2 * pair + 1]
        out[pl.ds(pair * HALF, HALF), :] = pick(even[:HALF], odd[HALF:]) + swap(
            pick(odd[:HALF], even[HALF:])
        )
    gram = gram[:HALF] + swap(gram[HALF:])
    out[pl.ds(2 * HALF, 32), :] = pick(gram[:32], swap(gram[32:]))


def basis_kernel(mixture, inverse, out):
    weight = split(block_diagonal(inverse[...]))
    out[...] = dot3(split(mixture[...]), weight, NT)


def kernel_call(body, outs, scratch, *operands, aliases=None, in_hbm=(), limit=24 << 20):
    moved = sum(x.size * x.dtype.itemsize for x in (*operands, *outs))
    specs = []
    for at, x in enumerate((*operands, *outs)):
        space = pltpu.VMEM
        if at in in_hbm:
            space = pltpu.HBM
        elif x.dtype == jnp.int32:
            space = pltpu.SMEM
        specs.append(pl.BlockSpec(memory_space=space))
    return pl.pallas_call(
        body,
        out_shape=outs,
        in_specs=specs[: len(operands)],
        out_specs=specs[len(operands) :],
        scratch_shapes=scratch,
        input_output_aliases=aliases or {},
        compiler_params=pltpu.CompilerParams(vmem_limit_bytes=limit),
        cost_estimate=pl.CostEstimate(flops=0, bytes_accessed=moved, transcendentals=0),
    )(*operands)


def shape(*dims, dtype=jnp.float32):
    return jax.ShapeDtypeStruct(dims, dtype)


def scratch(*dims):
    return pltpu.VMEM(dims, jnp.float32)


def in_rows(value):
    lead, (slices, width) = value.shape[:-2], value.shape[-2:]
    value = value.reshape(*lead, slices // SUBLANES, SUBLANES, width // LANES, LANES)
    value = jnp.swapaxes(value, -2, -3)
    return value.reshape(*lead, slices * width // LANES, LANES)


def out_of_rows(value, slices):
    lead, (rows, _) = value.shape[:-2], value.shape[-2:]
    value = value.reshape(*lead, slices // SUBLANES, rows // slices, SUBLANES, LANES)
    value = jnp.swapaxes(value, -2, -3)
    return value.reshape(*lead, slices, rows // slices * LANES)


def spread(value, axis, step):
    radix, stride = step
    if radix == 2:
        return [value, flip(value, axis, stride)]
    size = lax.axis_size(axis)
    parts = [value]
    for by in SHIFTS:
        pairs = [
            (index, index + ((index // stride + by) % 4 - index // stride % 4) * stride)
            for index in range(size)
        ]
        parts.append(lax.ppermute(value, axis, pairs))
    return parts


def exchanged(value, axis):
    steps = radices(lax.axis_size(axis))
    for at, (radix, stride) in enumerate(steps):
        parts = spread(value, axis, (radix, stride))
        if at < len(steps) - 1:
            value = sum(parts[1:], parts[0])
    return parts


def tiled(first_cores, mid_cores, last_cores, sketch_mid, sketch_last, ranks):
    members, count, slices, rank_size = first_cores.shape
    middle = mid_cores.shape[2]
    width = mid_cores.shape[4]
    total_slices = slices * lax.axis_size("mode")
    low = lax.axis_size("rep") // members
    member = lax.axis_index("rep") // low
    here = member[None].astype(jnp.int32)
    spot = lax.axis_index("mode")[None].astype(jnp.int32)
    height = 2 * count * 32
    rows = slices * 32
    inner, outer = radices(lax.axis_size("mode"))

    def half_of(source, position, index):
        part = lax.dynamic_slice(
            source, (index, 0, position, 0, 0), (1, count, 1, slices, width)
        )
        return in_rows(part.reshape(count, slices, width))

    keep, send = kernel_call(
        start_kernel,
        [shape(count * 32 + slices, LANES), shape(count * 32 + 2 * slices, LANES)],
        [
            scratch(*last_cores.shape),
            scratch(*first_cores.shape),
            scratch(*sketch_last.shape),
            pltpu.SemaphoreType.DMA((3,)),
            scratch(2 * height, LANES),
        ],
        here,
        spot,
        last_cores,
        first_cores,
        sketch_last,
        in_hbm=(2, 3, 4),
        limit=None,
    )
    keeps, sends = [keep], []
    sends.append(flip(send, "rep", low))
    for step in range(1, inner[0]):
        bits = step * inner[1]
        keeps.append(flip(keep, "mode", bits))
        pairs = [
            ((m * 2 * low + r), ((m ^ bits) * 2 * low + (r ^ low)))
            for m in range(lax.axis_size("mode"))
            for r in range(2 * low)
        ]
        sends.append(lax.ppermute(send, ("mode", "rep"), pairs))
    traded = sends[0][count * 32 + slices :]
    (part,) = kernel_call(
        functools.partial(merge_kernel, len(keeps), count * 32, slices),
        [shape(height + 2 * len(keeps) * slices, LANES)],
        [],
        *keeps,
        *sends,
    )
    cores = [None] * middle
    late_cores, late_sketch, late_ranks, part = lax.optimization_barrier(
        (mid_cores, sketch_mid, ranks, part)
    )
    masks = (jnp.arange(rank_size, dtype=jnp.int32)[None, :] < late_ranks[:, None]).astype(
        jnp.float32
    )
    masks = jnp.concatenate([masks, masks], axis=1)[:, None, :]
    sketch_rows = in_rows(late_sketch)
    sketch_rows = [sketch_rows[position] for position in range(middle)]
    for position in range(middle - 1, -1, -1):
        if position == middle - 1:
            sent = half_of(mid_cores, position, 1 - member)
        else:
            sent = half_of(late_cores, position, 1 - member)
        cores[position] = (half_of(late_cores, position, member), flip(sent, "rep", low))
    mixed = [None] * middle
    heads = None
    wide = shape(slices, height, LANES, dtype=jnp.bfloat16)
    for position in range(middle - 1, -1, -1):
        parts = exchanged(part, "mode") if heads else spread(part, "mode", outer)
        heads = heads or parts
        body, more, result = sketch_kernel, (), shape(height, LANES)
        if position == 0:
            body = functools.partial(first_kernel, slices=slices)
            more, result = (*heads, spot), shape(total_slices // 2, LANES)
        part, *mixed[position] = kernel_call(
            functools.partial(body, len(parts)),
            [result, wide, wide],
            [
                scratch(2 * height, LANES),
                scratch(height * slices, LANES),
                scratch(slices, HALF, LANES),
            ],
            *parts,
            *more,
            *((masks[1], masks[0]) if position == 0 else (masks[position + 1],)),
            *cores[position],
            sketch_rows[position],
        )
    square = scratch(count * HALF, LANES)
    part = part + flip(part, "rep", 1)
    parts = exchanged(part, "mode")
    inverse, carried, basis, part = kernel_call(
        functools.partial(bond_one_kernel, float(total_slices), len(parts)),
        [shape(HALF, LANES), shape(height, LANES), shape(slices, LANES), shape(rows, LANES)],
        [square],
        *parts,
        *heads,
        spot,
        masks[0],
        *mixed[0],
    )
    row_count = float(total_slices * rank_size)
    whole = shape(members, middle, rows, LANES)
    blocks = ()
    for position in range(middle):
        near = flip(part, "rep", 1)
        mixture, part = kernel_call(
            gram_kernel,
            [shape(rows, LANES), shape(2 * HALF + 32, LANES)],
            [scratch(height * slices, LANES)],
            part,
            near,
            carried,
            *cores[position],
        )
        parts = exchanged(part, "mode")
        mask = masks[position + 1]
        if position < middle - 1:
            inverse, carried, part = kernel_call(
                functools.partial(bond_kernel, row_count, len(parts)),
                [shape(HALF, LANES), shape(height, LANES), shape(rows, LANES)],
                [square],
                *parts,
                mask,
                *mixed[position + 1],
            )
            (own,) = kernel_call(basis_kernel, [shape(rows, LANES)], [], mixture, inverse)
            other = flip(own, "rep", low)
            blocks = kernel_call(
                functools.partial(place_kernel, position),
                [whole],
                [pltpu.SemaphoreType.DMA((2,))],
                here,
                own,
                other,
                *blocks,
                aliases={3: 0} if blocks else None,
                in_hbm=(3, 4),
            )
    away = flip(mixture, "rep", low)
    (last,) = kernel_call(
        functools.partial(last_kernel, row_count, len(parts)),
        [shape(slices + HALF, LANES)],
        [],
        *parts,
        mask,
        here,
        last_cores,
        traded,
        basis,
    )
    near, far, across = (flip(last, "rep", bits) for bits in (1, low, low + 1))
    blocks = kernel_call(
        functools.partial(own_kernel, middle - 1),
        [whole],
        [scratch(rows, LANES), pltpu.SemaphoreType.DMA],
        here,
        last,
        mixture,
        *blocks,
        aliases={3: 0},
        in_hbm=(3, 4),
    )
    pieces = slices // SUBLANES
    rounded_first, rounded_last, blocks = kernel_call(
        functools.partial(final_kernel, middle - 1),
        [shape(members, slices, rank_size), shape(members, slices, rank_size), whole],
        [scratch(pieces, rows // pieces, LANES), pltpu.SemaphoreType.DMA((pieces,))],
        here,
        last,
        near,
        far,
        across,
        away,
        *blocks,
        aliases={6: 2},
        in_hbm=(6, 9),
    )
    return (rounded_first, out_of_rows(blocks, slices), rounded_last)


def per_device(*arguments):
    members, count, slices, rank_size = arguments[0].shape
    steps = radices(lax.axis_size("mode"))
    fits = (
        members == 2
        and count == 2
        and rank_size == HALF
        and slices % SUBLANES == 0
        and slices * lax.axis_size("mode") == LANES
        and lax.axis_size("rep") == 2 * members
        and len(steps) == 2
    )
    return tiled(*arguments) if fits else general(*arguments)


def solution(mesh):
    return jax.shard_map(
        per_device,
        mesh=mesh,
        in_specs=(
            P(None, "rep", "mode", None),
            P(None, "rep", None, "mode", None),
            P(None, "rep", "mode", None),
            P(None, "mode", None),
            P("mode", None),
            P(),
        ),
        out_specs=(P(None, "mode", None), P(None, None, "mode", None), P(None, "mode", None)),
        check_vma=False,
    )
```

```python
import functools

import jax
import jax.numpy as jnp
from jax import lax
from jax.experimental import pallas as pl
from jax.experimental.pallas import tpu as pltpu
from jax.sharding import PartitionSpec as P

PRECISE = lax.Precision.HIGHEST
FAST = lax.Precision.HIGH


def lower_inverse(gram_matrix):
    factor = jnp.linalg.cholesky(gram_matrix)
    identity = jnp.eye(gram_matrix.shape[-1], dtype=gram_matrix.dtype)
    return jax.scipy.linalg.solve_triangular(factor, identity, lower=True)


def flip(value, axis, bits):
    size = lax.axis_size(axis)
    return lax.ppermute(value, axis, [(index, index ^ bits) for index in range(size)])


def radices(size):
    stride, out = 1, []
    if (size.bit_length() - 1) % 2:
        out.append((2, stride))
        stride *= 2
    while stride < size:
        out.append((4, stride))
        stride *= 4
    return out


def total(value, axis, size=None):
    for radix, stride in radices(size or lax.axis_size(axis)):
        parts = [flip(value, axis, step * stride) for step in range(1, radix)]
        value = sum(parts, value)
    return value


def gathered(value, axis, dim):
    for radix, stride in radices(lax.axis_size(axis)):
        parts = [flip(value, axis, step * stride) for step in range(1, radix)]
        value = jnp.concatenate([value] + parts, axis=dim)
    return value


def general(first_cores, mid_cores, last_cores, sketch_mid, sketch_last, ranks):
    members, _, slices, rank_size = first_cores.shape
    middle = mid_cores.shape[2]
    total_slices = slices * lax.axis_size("mode")
    low = lax.axis_size("rep") // members
    member = lax.axis_index("rep") // low
    masks = (jnp.arange(rank_size, dtype=jnp.int32)[None, :] < ranks[:, None]).astype(jnp.float32)

    def own_and_other(value):
        kept = lax.dynamic_index_in_dim(value, member, 0, keepdims=False)
        sent = lax.dynamic_index_in_dim(value, 1 - member, 0, keepdims=False)
        return jnp.concatenate([kept, flip(sent, "rep", low)], axis=0)

    def both_members(value):
        other = flip(value, "rep", low)
        return jnp.stack(
            [jnp.where(member == 0, value, other), jnp.where(member == 0, other, value)]
        )

    last = own_and_other(last_cores)
    first = own_and_other(first_cores)
    cores = [None] * middle
    for position in range(middle - 1, -1, -1):
        cores[position] = own_and_other(
            mid_cores[:, :, position].reshape(members, -1, slices, rank_size, rank_size)
        )
    sketch_cores = sketch_mid.reshape(middle, slices, rank_size, rank_size)
    sketches = [None] * (middle + 1)
    mixed = [None] * middle
    sketches[middle] = (
        total(jnp.einsum("sic,ie->sce", last, sketch_last, precision=FAST), "mode") * masks[middle]
    )
    for position in range(middle - 1, -1, -1):
        mixed[position] = jnp.einsum(
            "sicd,sde->sice", cores[position], sketches[position + 1], precision=FAST
        )
        folded = jnp.einsum(
            "sice,ife->scf", mixed[position], sketch_cores[position], precision=FAST
        )
        sketches[position] = total(folded, "mode") * masks[position]

    everything = gathered(first, "mode", 1)
    mixture = total(
        jnp.einsum("sid,sde->ie", everything, sketches[0], precision=PRECISE), "rep", low
    )
    gram = jnp.einsum("ie,if->ef", mixture, mixture, precision=PRECISE)
    raw = jnp.einsum("ie,sid->sed", mixture, everything, precision=PRECISE)
    inverse = lower_inverse(gram / total_slices + jnp.diag(1.0 - masks[0]))
    carried = jnp.einsum("fe,sed->sfd", inverse, raw, precision=PRECISE) / total_slices
    basis = jnp.einsum("ie,fe->if", mixture[:slices], inverse, precision=PRECISE)
    rounded_first = both_members(basis)

    rows = total_slices * rank_size
    blocks = []
    for position in range(middle):
        mixture = total(
            jnp.einsum("sac,sice->iae", carried, mixed[position], precision=FAST), "rep", low
        )
        gram = jnp.einsum("iae,iaf->ef", mixture, mixture, precision=PRECISE)
        spread = jnp.einsum("sac,iae->sice", carried, mixture, precision=FAST)
        raw = jnp.einsum("sice,sicd->sed", spread, cores[position], precision=FAST)
        both = total(jnp.concatenate([raw, gram[None]], axis=0), "mode")
        raw, gram = both[:-1], both[-1]
        inverse = lower_inverse(gram / rows + jnp.diag(1.0 - masks[position + 1]))
        carried = jnp.einsum("fe,sed->sfd", inverse, raw, precision=PRECISE) / rows
        basis = jnp.einsum("iae,fe->iaf", mixture, inverse, precision=FAST)
        blocks.append(both_members(basis.reshape(slices, rank_size * rank_size)))
    rounded_mid = jnp.stack(blocks, axis=1)
    local_last = jnp.einsum("sac,sic->ia", carried, last, precision=PRECISE)
    rounded_last = both_members(total(local_last, "rep", low))
    return (rounded_first, rounded_mid, rounded_last)


LANES = 128
SUBLANES = 8
HALF = 64
NN = (((1,), (0,)), ((), ()))
NT = (((1,), (1,)), ((), ()))
TN = (((0,), (0,)), ((), ()))


def left_half(rows):
    return lax.broadcasted_iota(jnp.int32, (rows, LANES), 1) < HALF


def swap(value):
    return pltpu.roll(value, HALF, 1)


def pick(left, right):
    return jnp.where(left_half(left.shape[0]), left, right)


def split(value):
    high = value.astype(jnp.bfloat16)
    return high, (value - high.astype(jnp.float32)).astype(jnp.bfloat16)


def dot(left, right, dims=NN):
    return lax.dot_general(left, right, dims, preferred_element_type=jnp.float32)


def dot3(left, right, dims=NN):
    (lh, ll), (rh, rl) = left, right
    at_left, at_right = dims[0][0][0], dims[0][1][0]
    zero = jnp.zeros_like(rl)
    wide = jnp.concatenate(
        [
            jnp.concatenate([rh, rh], axis=at_right),
            jnp.concatenate([rl, zero], axis=at_right),
        ],
        axis=1 - at_right,
    )
    value = dot(jnp.concatenate([lh, ll], axis=at_left), wide, dims)
    return value[:, :LANES] + value[:, LANES:]


def exact(left, right, dims=NN):
    return lax.dot_general(
        left, right, dims, precision=PRECISE, preferred_element_type=jnp.float32
    )


def block_diagonal(value):
    zero = jnp.zeros_like(value)
    return jnp.concatenate([pick(value, zero), pick(zero, swap(value))], axis=0)


def spread_rows(packed, scratch):
    count = packed.shape[0]
    scratch[pl.ds(0, count, stride=2), :] = packed
    scratch[pl.ds(1, count, stride=2), :] = swap(packed)
    return scratch[pl.ds(0, 2 * count), :]


def start_kernel(member, _, *refs):
    sources, (part, heads, tail), (*local, sems, scratch) = refs[:3], refs[3:6], refs[6:]
    copies = [
        pltpu.make_async_copy(source, target, sems.at[at])
        for at, (source, target) in enumerate(zip(sources, local))
    ]
    for copy in copies:
        copy.start()
    for copy in copies:
        copy.wait()
    last, first, sketch = local
    count, slices = last.shape[1:3]
    for half, index in enumerate((member[0], 1 - member[0])):
        cores, fronts = last[index], first[index]
        for s in range(count):
            scratch[pl.ds((half * count + s) * HALF, HALF), pl.ds(0, HALF)] = exact(
                cores[s], sketch[...], TN
            )
        heads[pl.ds(half * slices, slices), :] = jnp.concatenate([fronts[0], fronts[1]], axis=1)
        if half:
            tail[...] = jnp.concatenate([cores[0], cores[1]], axis=1)
    rows = part.shape[0]
    even = scratch[pl.ds(0, rows, stride=2), :]
    odd = scratch[pl.ds(1, rows, stride=2), :]
    part[...] = pick(even, swap(odd))


def merge_kernel(n_parts, rows, *refs):
    keeps, sends, (part, heads) = refs[:n_parts], refs[n_parts : 2 * n_parts], refs[2 * n_parts :]
    height = keeps[0].shape[0] - rows
    for pair, terms in enumerate((keeps, sends)):
        part[pl.ds(pair * rows, rows), :] = added([term.at[pl.ds(0, rows)] for term in terms])
        for at, term in enumerate(terms):
            heads[pair, pl.ds(at * height, height), :] = term[pl.ds(rows, height), :]


def added(parts):
    value = parts[0][...]
    for part in parts[1:]:
        value = value + part[...]
    return value


def sketch_step(parts, mask, kept, other, sketch, high, low, wide, product, narrow):
    count = kept.shape[0]
    rows = kept.shape[1]
    tiles = rows // 256
    natural = spread_rows(added(parts) * mask[...], wide)
    for half, cores in enumerate((kept, other)):
        for index in range(count):
            s = half * count + index
            weight = split(block_diagonal(natural[s * HALF : (s + 1) * HALF]))
            result = dot3(split(cores[index]), weight)
            for tile in range(tiles):
                product[pl.ds((tile * 2 * count + s) * 256, 256), :] = result[
                    tile * 256 : (tile + 1) * 256
                ]
    height = 2 * count * 32
    total_value = None
    for tile in range(tiles):
        for sub in range(SUBLANES):
            i = tile * SUBLANES + sub
            packed = sketch[pl.ds(tile * 256 + sub, 32, stride=SUBLANES), :]
            weight = split(block_diagonal(spread_rows(packed, narrow.at[i])))
            own = split(product[pl.ds(tile * height * SUBLANES + sub, height, stride=SUBLANES), :])
            high[i] = own[0]
            low[i] = own[1]
            term = dot3(own, weight, NT)
            total_value = term if total_value is None else total_value + term
    return total_value


def sketch_kernel(n_parts, *refs):
    parts, refs = refs[:n_parts], refs[n_parts:]
    mask, kept, other, sketch, out, *rest = refs
    out[...] = sketch_step(parts, mask, kept, other, sketch, *rest)


def meet_kernel(n_parts, n_heads, *refs):
    parts, heads, refs = refs[:n_parts], refs[n_parts : n_parts + n_heads], refs[n_parts + n_heads :]
    mask, tail, kept, other, sketch, keep, send, relay, *rest = refs
    value = sketch_step(parts, mask, kept, other, sketch, *rest)
    rows = value.shape[0] // 2
    slices = tail.shape[0]
    keep[pl.ds(0, rows), :] = value[:rows]
    send[pl.ds(0, rows), :] = value[rows:]
    for at, head in enumerate(heads):
        keep[pl.ds(rows + at * slices, slices), :] = head[pl.ds(0, slices), :]
        send[pl.ds(rows + at * slices, slices), :] = head[pl.ds(slices, slices), :]
    relay[pl.ds(0, rows), :] = added([part.at[pl.ds(rows, rows)] for part in parts]) * mask[...]
    relay[pl.ds(rows, slices), :] = tail[...]


def mixed_kernel(relay, cores, own_high, own_low, high, low, wide, product):
    count, rows = cores.shape[:2]
    tiles = rows // 256
    height = count * 32
    natural = spread_rows(relay[pl.ds(0, height), :], wide)
    for index in range(count):
        weight = split(block_diagonal(natural[index * HALF : (index + 1) * HALF]))
        result = dot3(split(cores[index]), weight)
        for tile in range(tiles):
            product[pl.ds((tile * count + index) * 256, 256), :] = result[
                tile * 256 : (tile + 1) * 256
            ]
    for i in range(high.shape[0]):
        start = i // SUBLANES * height * SUBLANES + i % SUBLANES
        value = split(product[pl.ds(start, height, stride=SUBLANES), :])
        high[i] = jnp.concatenate([own_high[i][:height], value[0]], axis=0)
        low[i] = jnp.concatenate([own_low[i][:height], value[1]], axis=0)


SHIFTS = (1, 3, 2)


def slice_blocks(spot, n_inner, n_outer):
    inner, outer = spot % n_inner, spot // n_inner
    return [
        (outer + n_outer - by) % n_outer * n_inner + (inner ^ step)
        for step in range(n_inner)
        for by in (0,) + SHIFTS
    ]


def block_rows(block, count):
    return pl.ds(pl.multiple_of(block * count, SUBLANES), count)


def first_kernel(n_parts, *refs, slices):
    parts, (heads, *refs) = refs[:n_parts], refs[n_parts:]
    spot, mask, next_mask, kept, other, sketch, out, *rest = refs
    value = sketch_step(parts, mask, kept, other, sketch, *rest)
    natural = spread_rows(value * next_mask[...], rest[2])
    natural = pick(natural, jnp.zeros_like(natural))
    value = exact(heads[0], natural[:LANES])
    value = value + exact(heads[1], natural[LANES:])
    shared = rest[2]
    blocks = slice_blocks(spot[0], LANES // slices // n_parts, n_parts)
    for at, block in enumerate(blocks):
        shared[block_rows(block, slices), :] = value[at * slices : (at + 1) * slices]
    value = shared[pl.ds(0, LANES), :]
    out[...] = pick(value[:HALF], swap(value[HALF:]))


def eliminate(gram, mask, row_count):
    size = gram.shape[0]
    row = lax.broadcasted_iota(jnp.int32, (size, LANES), 0)
    lane = lax.broadcasted_iota(jnp.int32, (size, LANES), 1)
    scaled = gram * (1.0 / row_count)
    unit = lax.rsqrt(jnp.broadcast_to(scaled[0:1, 0:1], (1, LANES)))
    scaled = scaled * unit * unit
    diagonal = jnp.where(lane == row, 1.0 - mask, 0.0)
    work = jnp.where(lane < HALF, scaled + diagonal, jnp.where(lane - HALF == row, 1.0, 0.0))
    done = []
    for base in range(0, size, SUBLANES):
        live = size - base
        columns = [
            jnp.broadcast_to(work[:, base + k : base + k + 1], (live, LANES))
            for k in range(SUBLANES)
        ]
        pivots = [work[k : k + 1] for k in range(SUBLANES)]
        for k in range(0, SUBLANES, 2):
            first, second = columns[k], columns[k + 1]
            a, b, c = first[k : k + 1], first[k + 1 : k + 2], second[k + 1 : k + 2]
            root = lax.rsqrt(a)
            next_root = lax.rsqrt(a * c - b * b) * (a * root)
            ratio = b * (root * root)
            columns[k : k + 2] = first * root, (second - first * ratio) * next_root
            pivots[k : k + 2] = pivots[k] * root, (pivots[k + 1] - pivots[k] * ratio) * next_root
            for m in range(k + 2, SUBLANES):
                for at in (k, k + 1):
                    weight = columns[at][m : m + 1]
                    columns[m] = columns[m] - columns[at] * weight
                    pivots[m] = pivots[m] - pivots[at] * weight
        done.append(jnp.concatenate(pivots, axis=0))
        work = work[SUBLANES:]
        for k in range(SUBLANES):
            work = work - columns[k][SUBLANES:] * pivots[k]
    return jnp.concatenate(done, axis=0) * unit


def project(raw, gram, mask, row_count, square):
    solved = eliminate(gram, mask, row_count)
    square[pl.ds(0, HALF), :] = solved
    planar = jnp.concatenate(
        [square[pl.ds(0, HALF // 2, stride=2), :], square[pl.ds(1, HALF // 2, stride=2), :]], axis=0
    )
    carried = exact(raw, block_diagonal(swap(planar)), NT) * (1.0 / row_count)
    square[...] = carried
    pairs = carried.shape[0] // HALF
    even = square[pl.ds(0, pairs * 32, stride=2), :]
    odd = square[pl.ds(1, pairs * 32, stride=2), :]
    first, second = pick(even, swap(odd)), pick(swap(even), odd)
    blocks = []
    for pair in range(pairs):
        blocks += [first[pair * 32 : (pair + 1) * 32], second[pair * 32 : (pair + 1) * 32]]
    return swap(solved), jnp.concatenate(blocks, axis=0)


def mix(carried, high, low, out):
    weight = split(carried.T)
    for i in range(high.shape[0]):
        tile, sub = i // SUBLANES, i % SUBLANES
        value = dot3(weight, (high[i], low[i]))
        straight = pick(value[0:32], value[96:128])
        crossed = pick(value[32:64], value[64:96])
        out[pl.ds(tile * 256 + sub, 32, stride=SUBLANES), :] = straight + swap(crossed)


def unpack_gram(packed):
    return jnp.concatenate([packed, swap(packed)], axis=0)


def bond_one_kernel(row_count, n_parts, *refs):
    parts, (heads, *refs) = refs[:n_parts], refs[n_parts:]
    spot, mask, high, low, inverse, carried, basis, out, square = refs
    packed = added(parts)
    zero = jnp.zeros_like(packed)
    square[...] = jnp.concatenate([pick(packed, zero), pick(swap(packed), zero)], axis=0)
    slices = basis.shape[0]
    blocks = slice_blocks(spot[0], LANES // slices // n_parts, n_parts)
    mixture = jnp.concatenate([square[block_rows(block, slices), :] for block in blocks], axis=0)
    gram = exact(mixture, mixture, TN)[:HALF]
    raw = []
    for pair in range(2):
        value = exact(heads[pair], mixture, TN)
        raw.append(pick(value[:HALF], swap(value[HALF:])))
    solved, moved = project(jnp.concatenate(raw, axis=0), gram, mask[...], row_count, square)
    inverse[...] = solved
    carried[...] = moved
    full = jnp.concatenate([pick(solved, jnp.zeros_like(solved)), jnp.zeros_like(solved)], axis=0)
    basis[...] = exact(mixture[:slices], full, NT)
    mix(moved, high, low, out)


def bond_kernel(row_count, n_parts, *refs):
    parts, refs = refs[:n_parts], refs[n_parts:]
    mask, high, low, inverse, carried, out, square = refs
    value = added(parts)
    solved, moved = project(
        value[:LANES], unpack_gram(value[LANES:]), mask[...], row_count, square
    )
    inverse[...] = solved
    carried[...] = moved
    mix(moved, high, low, out)


def last_kernel(row_count, n_parts, *refs):
    parts, refs = refs[:n_parts], refs[n_parts:]
    mask, member, kept, relay, basis, out = refs
    value = added(parts)
    solved = swap(eliminate(unpack_gram(value[LANES:]), mask[...], row_count))
    carried = exact(value[:LANES], block_diagonal(solved), NT) * (1.0 / row_count)
    cores = kept[member[0]]
    slices = cores.shape[1]
    own = jnp.concatenate([cores[0], cores[1]], axis=1)
    term = None
    for pair, both in enumerate((own, relay[pl.ds(HALF, slices), :])):
        side = carried[pair * HALF : (pair + 1) * HALF]
        zero = jnp.zeros_like(side)
        both = exact(both, jnp.concatenate([pick(side, zero), pick(swap(side), zero)], axis=0))
        term = both if term is None else term + both
    out[pl.ds(0, slices), :] = pick(term, swap(basis[...]))
    out[pl.ds(slices, HALF), :] = solved


def place_kernel(position, member, mine, theirs, *refs):
    out, sems = refs[-2:]
    here = member[0]
    copies = [
        pltpu.make_async_copy(mine, out.at[here, position], sems.at[0]),
        pltpu.make_async_copy(theirs, out.at[1 - here, position], sems.at[1]),
    ]
    for copy in copies:
        copy.start()
    for copy in copies:
        copy.wait()


def own_kernel(position, member, mine, mixture, before, *refs):
    out, block, sem = refs
    slices = mine.shape[0] - HALF
    weight = split(block_diagonal(mine[pl.ds(slices, HALF), :]))
    block[...] = dot3(split(mixture[...]), weight, NT)
    copy = pltpu.make_async_copy(block, out.at[member[0], position], sem)
    copy.start()
    copy.wait()


def final_kernel(position, member, mine, near, far, across, away, before, *refs):
    first, last, out, blocks, sems = refs
    here = member[0]
    slices = first.shape[1]
    weight = split(block_diagonal(far[pl.ds(slices, HALF), :]))
    count = blocks.shape[0]
    height = away.shape[0] // count
    copies = []
    for at in range(count):
        value = away[pl.ds(at * height, height), :]
        blocks[at] = dot3(split(value), weight, NT)
        place = out.at[1 - here, position, pl.ds(at * height, height), :]
        copies.append(pltpu.make_async_copy(blocks.at[at], place, sems.at[at]))
        copies[-1].start()
    for place, terms in ((here, (mine, near)), (1 - here, (far, across))):
        head = terms[0][pl.ds(0, slices), :]
        first[place] = swap(head)[:, :HALF]
        last[place] = (head + terms[1][pl.ds(0, slices), :])[:, :HALF]
    for copy in copies:
        copy.wait()


def gram_kernel(mine, theirs, carried, kept, other, mixture, out, spread):
    count, rows = kept.shape[0], kept.shape[1]
    tiles = rows // 256
    mixture[...] = mine[...] + theirs[...]
    everything = mixture[...]
    gram = exact(everything, everything, TN)
    weight = split(carried[...])
    height = 2 * count * 32
    for tile in range(tiles):
        for sub in range(SUBLANES):
            packed = mixture[pl.ds(tile * 256 + sub, 32, stride=SUBLANES), :]
            crossed = swap(packed)
            zero = jnp.zeros_like(packed)
            blocks = jnp.concatenate(
                [pick(packed, zero), pick(crossed, zero), pick(zero, crossed), pick(zero, packed)],
                axis=0,
            )
            spread[pl.ds(tile * height * SUBLANES + sub, height, stride=SUBLANES), :] = dot3(
                weight, split(blocks)
            )
    raw = []
    for half, cores in enumerate((kept, other)):
        for index in range(count):
            s = half * count + index
            own = jnp.concatenate(
                [spread[pl.ds((tile * 2 * count + s) * 256, 256), :] for tile in range(tiles)],
                axis=0,
            )
            raw.append(dot3(split(cores[index]), split(own), TN))
    for pair in range(count):
        even, odd = raw[2 * pair], raw[2 * pair + 1]
        out[pl.ds(pair * HALF, HALF), :] = pick(even[:HALF], odd[HALF:]) + swap(
            pick(odd[:HALF], even[HALF:])
        )
    gram = gram[:HALF] + swap(gram[HALF:])
    out[pl.ds(2 * HALF, 32), :] = pick(gram[:32], swap(gram[32:]))


def basis_kernel(mixture, inverse, out):
    weight = split(block_diagonal(inverse[...]))
    out[...] = dot3(split(mixture[...]), weight, NT)


def kernel_call(body, outs, scratch, *operands, aliases=None, in_hbm=(), limit=24 << 20):
    moved = sum(x.size * x.dtype.itemsize for x in (*operands, *outs))
    specs = []
    for at, x in enumerate((*operands, *outs)):
        space = pltpu.VMEM
        if at in in_hbm:
            space = pltpu.HBM
        elif x.dtype == jnp.int32:
            space = pltpu.SMEM
        specs.append(pl.BlockSpec(memory_space=space))
    return pl.pallas_call(
        body,
        out_shape=outs,
        in_specs=specs[: len(operands)],
        out_specs=specs[len(operands) :],
        scratch_shapes=scratch,
        input_output_aliases=aliases or {},
        compiler_params=pltpu.CompilerParams(vmem_limit_bytes=limit),
        cost_estimate=pl.CostEstimate(flops=0, bytes_accessed=moved, transcendentals=0),
    )(*operands)


def shape(*dims, dtype=jnp.float32):
    return jax.ShapeDtypeStruct(dims, dtype)


def scratch(*dims):
    return pltpu.VMEM(dims, jnp.float32)


def in_rows(value):
    lead, (slices, width) = value.shape[:-2], value.shape[-2:]
    value = value.reshape(*lead, slices // SUBLANES, SUBLANES, width // LANES, LANES)
    value = jnp.swapaxes(value, -2, -3)
    return value.reshape(*lead, slices * width // LANES, LANES)


def out_of_rows(value, slices):
    lead, (rows, _) = value.shape[:-2], value.shape[-2:]
    value = value.reshape(*lead, slices // SUBLANES, rows // slices, SUBLANES, LANES)
    value = jnp.swapaxes(value, -2, -3)
    return value.reshape(*lead, slices, rows // slices * LANES)


def spread(value, axis, step):
    radix, stride = step
    if radix == 2:
        return [value, flip(value, axis, stride)]
    size = lax.axis_size(axis)
    parts = [value]
    for by in SHIFTS:
        pairs = [
            (index, index + ((index // stride + by) % 4 - index // stride % 4) * stride)
            for index in range(size)
        ]
        parts.append(lax.ppermute(value, axis, pairs))
    return parts


def exchanged(value, axis):
    steps = radices(lax.axis_size(axis))
    for at, (radix, stride) in enumerate(steps):
        parts = spread(value, axis, (radix, stride))
        if at < len(steps) - 1:
            value = sum(parts[1:], parts[0])
    return parts


def tiled(first_cores, mid_cores, last_cores, sketch_mid, sketch_last, ranks):
    members, count, slices, rank_size = first_cores.shape
    middle = mid_cores.shape[2]
    width = mid_cores.shape[4]
    total_slices = slices * lax.axis_size("mode")
    low = lax.axis_size("rep") // members
    member = lax.axis_index("rep") // low
    here = member[None].astype(jnp.int32)
    spot = lax.axis_index("mode")[None].astype(jnp.int32)
    height = 2 * count * 32
    rows = slices * 32
    inner, outer = radices(lax.axis_size("mode"))

    def half_of(source, position, index):
        part = lax.dynamic_slice(
            source, (index, 0, position, 0, 0), (1, count, 1, slices, width)
        )
        return in_rows(part.reshape(count, slices, width))

    part, heads, tail = kernel_call(
        start_kernel,
        [shape(height, LANES), shape(2 * slices, LANES), shape(slices, LANES)],
        [
            scratch(*last_cores.shape),
            scratch(*first_cores.shape),
            scratch(*sketch_last.shape),
            pltpu.SemaphoreType.DMA((3,)),
            scratch(2 * height, LANES),
        ],
        here,
        spot,
        last_cores,
        first_cores,
        sketch_last,
        in_hbm=(2, 3, 4),
        limit=None,
    )
    late_cores, late_sketch, late_ranks, part = lax.optimization_barrier(
        (mid_cores, sketch_mid, ranks, part)
    )
    masks = (jnp.arange(rank_size, dtype=jnp.int32)[None, :] < late_ranks[:, None]).astype(
        jnp.float32
    )
    masks = jnp.concatenate([masks, masks], axis=1)[:, None, :]
    sketch_rows = in_rows(late_sketch)
    sketch_rows = [sketch_rows[position] for position in range(middle)]
    kept = [half_of(late_cores, position, member) for position in range(middle)]
    sent = [half_of(late_cores, position, 1 - member) for position in range(middle)]
    sent[middle - 2] = half_of(mid_cores, middle - 2, 1 - member)
    traded = [flip(sent[position], "rep", low) for position in range(middle)]
    cores = list(zip(kept, traded))
    wide = shape(slices, height, LANES, dtype=jnp.bfloat16)
    room = [
        scratch(2 * height, LANES),
        scratch(height * slices, LANES),
        scratch(slices, HALF, LANES),
    ]
    heads = spread(heads, "mode", outer)
    parts = exchanged(part, "mode")
    block = shape(height // 2 + len(heads) * slices, LANES)
    keep, send, relay, *own_mixed = kernel_call(
        functools.partial(meet_kernel, len(parts), len(heads)),
        [block, block, shape(height // 2 + slices, LANES), wide, wide],
        room,
        *parts,
        *heads,
        masks[middle],
        tail,
        kept[-1],
        sent[-1],
        sketch_rows[-1],
    )
    keeps, sends = [keep], []
    sends.append(flip(send, "rep", low))
    for step in range(1, inner[0]):
        bits = step * inner[1]
        keeps.append(flip(keep, "mode", bits))
        pairs = [
            ((m * 2 * low + r), ((m ^ bits) * 2 * low + (r ^ low)))
            for m in range(lax.axis_size("mode"))
            for r in range(2 * low)
        ]
        sends.append(lax.ppermute(send, ("mode", "rep"), pairs))
    part, heads = kernel_call(
        functools.partial(merge_kernel, len(keeps), height // 2),
        [shape(height, LANES), shape(2, total_slices, LANES)],
        [],
        *keeps,
        *sends,
    )
    relay = flip(relay, "rep", low)
    mixed = [None] * middle
    mixed[-1] = kernel_call(
        mixed_kernel,
        [wide, wide],
        [scratch(height, LANES), scratch(height // 2 * slices, LANES)],
        relay,
        traded[-1],
        *own_mixed,
    )
    for position in range(middle - 2, -1, -1):
        if position == middle - 2:
            parts = spread(part, "mode", outer)
        else:
            parts = exchanged(part, "mode")
        body, more, result = sketch_kernel, (), shape(height, LANES)
        if position == 0:
            body = functools.partial(first_kernel, slices=slices)
            more, result = (heads, spot), shape(total_slices // 2, LANES)
        part, *mixed[position] = kernel_call(
            functools.partial(body, len(parts)),
            [result, wide, wide],
            room,
            *parts,
            *more,
            *((masks[1], masks[0]) if position == 0 else (masks[position + 1],)),
            *cores[position],
            sketch_rows[position],
        )
    square = scratch(count * HALF, LANES)
    part = part + flip(part, "rep", 1)
    parts = exchanged(part, "mode")
    inverse, carried, basis, part = kernel_call(
        functools.partial(bond_one_kernel, float(total_slices), len(parts)),
        [shape(HALF, LANES), shape(height, LANES), shape(slices, LANES), shape(rows, LANES)],
        [square],
        *parts,
        heads,
        spot,
        masks[0],
        *mixed[0],
    )
    row_count = float(total_slices * rank_size)
    whole = shape(members, middle, rows, LANES)
    blocks = ()
    for position in range(middle):
        near = flip(part, "rep", 1)
        mixture, part = kernel_call(
            gram_kernel,
            [shape(rows, LANES), shape(2 * HALF + 32, LANES)],
            [scratch(height * slices, LANES)],
            part,
            near,
            carried,
            *cores[position],
        )
        parts = exchanged(part, "mode")
        mask = masks[position + 1]
        if position < middle - 1:
            inverse, carried, part = kernel_call(
                functools.partial(bond_kernel, row_count, len(parts)),
                [shape(HALF, LANES), shape(height, LANES), shape(rows, LANES)],
                [square],
                *parts,
                mask,
                *mixed[position + 1],
            )
            (own,) = kernel_call(basis_kernel, [shape(rows, LANES)], [], mixture, inverse)
            other = flip(own, "rep", low)
            blocks = kernel_call(
                functools.partial(place_kernel, position),
                [whole],
                [pltpu.SemaphoreType.DMA((2,))],
                here,
                own,
                other,
                *blocks,
                aliases={3: 0} if blocks else None,
                in_hbm=(3, 4),
            )
    away = flip(mixture, "rep", low)
    (last,) = kernel_call(
        functools.partial(last_kernel, row_count, len(parts)),
        [shape(slices + HALF, LANES)],
        [],
        *parts,
        mask,
        here,
        last_cores,
        relay,
        basis,
    )
    near, far, across = (flip(last, "rep", bits) for bits in (1, low, low + 1))
    blocks = kernel_call(
        functools.partial(own_kernel, middle - 1),
        [whole],
        [scratch(rows, LANES), pltpu.SemaphoreType.DMA],
        here,
        last,
        mixture,
        *blocks,
        aliases={3: 0},
        in_hbm=(3, 4),
    )
    pieces = slices // SUBLANES
    rounded_first, rounded_last, blocks = kernel_call(
        functools.partial(final_kernel, middle - 1),
        [shape(members, slices, rank_size), shape(members, slices, rank_size), whole],
        [scratch(pieces, rows // pieces, LANES), pltpu.SemaphoreType.DMA((pieces,))],
        here,
        last,
        near,
        far,
        across,
        away,
        *blocks,
        aliases={6: 2},
        in_hbm=(6, 9),
    )
    return (rounded_first, out_of_rows(blocks, slices), rounded_last)


def per_device(*arguments):
    members, count, slices, rank_size = arguments[0].shape
    steps = radices(lax.axis_size("mode"))
    fits = (
        members == 2
        and count == 2
        and rank_size == HALF
        and slices % SUBLANES == 0
        and slices * lax.axis_size("mode") == LANES
        and lax.axis_size("rep") == 2 * members
        and len(steps) == 2
    )
    return tiled(*arguments) if fits else general(*arguments)


def solution(mesh):
    return jax.shard_map(
        per_device,
        mesh=mesh,
        in_specs=(
            P(None, "rep", "mode", None),
            P(None, "rep", None, "mode", None),
            P(None, "rep", "mode", None),
            P(None, "mode", None),
            P("mode", None),
            P(),
        ),
        out_specs=(P(None, "mode", None), P(None, None, "mode", None), P(None, "mode", None)),
        check_vma=False,
    )
```

```python
import functools

import jax
import jax.numpy as jnp
from jax import lax
from jax.experimental import pallas as pl
from jax.experimental.pallas import tpu as pltpu
from jax.sharding import PartitionSpec as P

PRECISE = lax.Precision.HIGHEST
FAST = lax.Precision.HIGH


def lower_inverse(gram_matrix):
    factor = jnp.linalg.cholesky(gram_matrix)
    identity = jnp.eye(gram_matrix.shape[-1], dtype=gram_matrix.dtype)
    return jax.scipy.linalg.solve_triangular(factor, identity, lower=True)


def flip(value, axis, bits):
    size = lax.axis_size(axis)
    return lax.ppermute(value, axis, [(index, index ^ bits) for index in range(size)])


def radices(size):
    stride, out = 1, []
    if (size.bit_length() - 1) % 2:
        out.append((2, stride))
        stride *= 2
    while stride < size:
        out.append((4, stride))
        stride *= 4
    return out


def total(value, axis, size=None):
    for radix, stride in radices(size or lax.axis_size(axis)):
        parts = [flip(value, axis, step * stride) for step in range(1, radix)]
        value = sum(parts, value)
    return value


def gathered(value, axis, dim):
    for radix, stride in radices(lax.axis_size(axis)):
        parts = [flip(value, axis, step * stride) for step in range(1, radix)]
        value = jnp.concatenate([value] + parts, axis=dim)
    return value


def general(first_cores, mid_cores, last_cores, sketch_mid, sketch_last, ranks):
    members, _, slices, rank_size = first_cores.shape
    middle = mid_cores.shape[2]
    total_slices = slices * lax.axis_size("mode")
    low = lax.axis_size("rep") // members
    member = lax.axis_index("rep") // low
    masks = (jnp.arange(rank_size, dtype=jnp.int32)[None, :] < ranks[:, None]).astype(jnp.float32)

    def own_and_other(value):
        kept = lax.dynamic_index_in_dim(value, member, 0, keepdims=False)
        sent = lax.dynamic_index_in_dim(value, 1 - member, 0, keepdims=False)
        return jnp.concatenate([kept, flip(sent, "rep", low)], axis=0)

    def both_members(value):
        other = flip(value, "rep", low)
        return jnp.stack(
            [jnp.where(member == 0, value, other), jnp.where(member == 0, other, value)]
        )

    last = own_and_other(last_cores)
    first = own_and_other(first_cores)
    cores = [None] * middle
    for position in range(middle - 1, -1, -1):
        cores[position] = own_and_other(
            mid_cores[:, :, position].reshape(members, -1, slices, rank_size, rank_size)
        )
    sketch_cores = sketch_mid.reshape(middle, slices, rank_size, rank_size)
    sketches = [None] * (middle + 1)
    mixed = [None] * middle
    sketches[middle] = (
        total(jnp.einsum("sic,ie->sce", last, sketch_last, precision=FAST), "mode") * masks[middle]
    )
    for position in range(middle - 1, -1, -1):
        mixed[position] = jnp.einsum(
            "sicd,sde->sice", cores[position], sketches[position + 1], precision=FAST
        )
        folded = jnp.einsum(
            "sice,ife->scf", mixed[position], sketch_cores[position], precision=FAST
        )
        sketches[position] = total(folded, "mode") * masks[position]

    everything = gathered(first, "mode", 1)
    mixture = total(
        jnp.einsum("sid,sde->ie", everything, sketches[0], precision=PRECISE), "rep", low
    )
    gram = jnp.einsum("ie,if->ef", mixture, mixture, precision=PRECISE)
    raw = jnp.einsum("ie,sid->sed", mixture, everything, precision=PRECISE)
    inverse = lower_inverse(gram / total_slices + jnp.diag(1.0 - masks[0]))
    carried = jnp.einsum("fe,sed->sfd", inverse, raw, precision=PRECISE) / total_slices
    basis = jnp.einsum("ie,fe->if", mixture[:slices], inverse, precision=PRECISE)
    rounded_first = both_members(basis)

    rows = total_slices * rank_size
    blocks = []
    for position in range(middle):
        mixture = total(
            jnp.einsum("sac,sice->iae", carried, mixed[position], precision=FAST), "rep", low
        )
        gram = jnp.einsum("iae,iaf->ef", mixture, mixture, precision=PRECISE)
        spread = jnp.einsum("sac,iae->sice", carried, mixture, precision=FAST)
        raw = jnp.einsum("sice,sicd->sed", spread, cores[position], precision=FAST)
        both = total(jnp.concatenate([raw, gram[None]], axis=0), "mode")
        raw, gram = both[:-1], both[-1]
        inverse = lower_inverse(gram / rows + jnp.diag(1.0 - masks[position + 1]))
        carried = jnp.einsum("fe,sed->sfd", inverse, raw, precision=PRECISE) / rows
        basis = jnp.einsum("iae,fe->iaf", mixture, inverse, precision=FAST)
        blocks.append(both_members(basis.reshape(slices, rank_size * rank_size)))
    rounded_mid = jnp.stack(blocks, axis=1)
    local_last = jnp.einsum("sac,sic->ia", carried, last, precision=PRECISE)
    rounded_last = both_members(total(local_last, "rep", low))
    return (rounded_first, rounded_mid, rounded_last)


LANES = 128
SUBLANES = 8
HALF = 64
NN = (((1,), (0,)), ((), ()))
NT = (((1,), (1,)), ((), ()))
TN = (((0,), (0,)), ((), ()))


def left_half(rows):
    return lax.broadcasted_iota(jnp.int32, (rows, LANES), 1) < HALF


def swap(value):
    return pltpu.roll(value, HALF, 1)


def pick(left, right):
    return jnp.where(left_half(left.shape[0]), left, right)


def split(value):
    high = value.astype(jnp.bfloat16)
    return high, (value - high.astype(jnp.float32)).astype(jnp.bfloat16)


def dot(left, right, dims=NN):
    return lax.dot_general(left, right, dims, preferred_element_type=jnp.float32)


def dot3(left, right, dims=NN):
    (lh, ll), (rh, rl) = left, right
    at_left, at_right = dims[0][0][0], dims[0][1][0]
    zero = jnp.zeros_like(rl)
    wide = jnp.concatenate(
        [
            jnp.concatenate([rh, rh], axis=at_right),
            jnp.concatenate([rl, zero], axis=at_right),
        ],
        axis=1 - at_right,
    )
    value = dot(jnp.concatenate([lh, ll], axis=at_left), wide, dims)
    return value[:, :LANES] + value[:, LANES:]


def exact(left, right, dims=NN):
    return lax.dot_general(
        left, right, dims, precision=PRECISE, preferred_element_type=jnp.float32
    )


def block_diagonal(value):
    zero = jnp.zeros_like(value)
    return jnp.concatenate([pick(value, zero), pick(zero, swap(value))], axis=0)


def spread_rows(packed, scratch):
    count = packed.shape[0]
    scratch[pl.ds(0, count, stride=2), :] = packed
    scratch[pl.ds(1, count, stride=2), :] = swap(packed)
    return scratch[pl.ds(0, 2 * count), :]


def start_kernel(member, _, last, sketch, out, scratch):
    count = last.shape[1]
    for half, index in enumerate((member[0], 1 - member[0])):
        cores = last[index]
        for s in range(count):
            scratch[pl.ds((half * count + s) * HALF, HALF), pl.ds(0, HALF)] = exact(
                cores[s], sketch[...], TN
            )
    rows = out.shape[0]
    even = scratch[pl.ds(0, rows, stride=2), :]
    odd = scratch[pl.ds(1, rows, stride=2), :]
    out[...] = pick(even, swap(odd))


def merge_kernel(n_parts, rows, *refs):
    keeps, sends, (part, heads) = refs[:n_parts], refs[n_parts : 2 * n_parts], refs[2 * n_parts :]
    height = keeps[0].shape[0] - rows
    for pair, terms in enumerate((keeps, sends)):
        part[pl.ds(pair * rows, rows), :] = added([term.at[pl.ds(0, rows)] for term in terms])
        for at, term in enumerate(terms):
            place = pl.ds((pair * n_parts + at) * height, height)
            heads[place, :] = term[pl.ds(rows, height), :]


def heads_of(parts, pair):
    rows = parts[0].shape[0] // 2
    return jnp.concatenate([part[pl.ds(pair * rows, rows), :] for part in parts], axis=0)


def added(parts):
    value = parts[0][...]
    for part in parts[1:]:
        value = value + part[...]
    return value


def sketch_step(parts, mask, kept, other, sketch, high, low, wide, product, narrow):
    count = kept.shape[0]
    rows = kept.shape[1]
    tiles = rows // 256
    natural = spread_rows(added(parts) * mask[...], wide)
    for half, cores in enumerate((kept, other)):
        for index in range(count):
            s = half * count + index
            weight = split(block_diagonal(natural[s * HALF : (s + 1) * HALF]))
            result = dot3(split(cores[index]), weight)
            for tile in range(tiles):
                product[pl.ds((tile * 2 * count + s) * 256, 256), :] = result[
                    tile * 256 : (tile + 1) * 256
                ]
    height = 2 * count * 32
    total_value = None
    for tile in range(tiles):
        for sub in range(SUBLANES):
            i = tile * SUBLANES + sub
            packed = sketch[pl.ds(tile * 256 + sub, 32, stride=SUBLANES), :]
            weight = split(block_diagonal(spread_rows(packed, narrow.at[i])))
            own = split(product[pl.ds(tile * height * SUBLANES + sub, height, stride=SUBLANES), :])
            high[i] = own[0]
            low[i] = own[1]
            term = dot3(own, weight, NT)
            total_value = term if total_value is None else total_value + term
    return total_value


def sketch_kernel(n_parts, *refs):
    parts, refs = refs[:n_parts], refs[n_parts:]
    mask, kept, other, sketch, out, *rest = refs
    out[...] = sketch_step(parts, mask, kept, other, sketch, *rest)


def meet_kernel(n_parts, *refs):
    parts, refs = refs[:n_parts], refs[n_parts:]
    member, first, last, mask, kept, other, sketch, keep, send, relay, *rest = refs
    value = sketch_step(parts, mask, kept, other, sketch, *rest)
    rows = value.shape[0] // 2
    slices = first.shape[2]
    for out, half, index in ((keep, 0, member[0]), (send, 1, 1 - member[0])):
        out[pl.ds(0, rows), :] = value[half * rows : (half + 1) * rows]
        heads = first[index]
        out[pl.ds(rows, slices), :] = jnp.concatenate([heads[0], heads[1]], axis=1)
    tail = last[1 - member[0]]
    relay[pl.ds(0, rows), :] = added([part.at[pl.ds(rows, rows)] for part in parts]) * mask[...]
    relay[pl.ds(rows, slices), :] = jnp.concatenate([tail[0], tail[1]], axis=1)


def mixed_kernel(relay, cores, own_high, own_low, high, low, wide, product):
    count, rows = cores.shape[:2]
    tiles = rows // 256
    height = count * 32
    natural = spread_rows(relay[pl.ds(0, height), :], wide)
    for index in range(count):
        weight = split(block_diagonal(natural[index * HALF : (index + 1) * HALF]))
        result = dot3(split(cores[index]), weight)
        for tile in range(tiles):
            product[pl.ds((tile * count + index) * 256, 256), :] = result[
                tile * 256 : (tile + 1) * 256
            ]
    for i in range(high.shape[0]):
        start = i // SUBLANES * height * SUBLANES + i % SUBLANES
        value = split(product[pl.ds(start, height, stride=SUBLANES), :])
        high[i] = jnp.concatenate([own_high[i][:height], value[0]], axis=0)
        low[i] = jnp.concatenate([own_low[i][:height], value[1]], axis=0)


SHIFTS = (1, 3, 2)


def slice_blocks(spot, n_inner, n_outer):
    inner, outer = spot % n_inner, spot // n_inner
    return [
        (outer + n_outer - by) % n_outer * n_inner + (inner ^ step)
        for by in (0,) + SHIFTS
        for step in range(n_inner)
    ]


def block_rows(block, count):
    return pl.ds(pl.multiple_of(block * count, SUBLANES), count)


def first_kernel(n_parts, *refs, slices):
    parts, heads, refs = refs[:n_parts], refs[n_parts : 2 * n_parts], refs[2 * n_parts :]
    spot, mask, next_mask, kept, other, sketch, out, *rest = refs
    value = sketch_step(parts, mask, kept, other, sketch, *rest)
    natural = spread_rows(value * next_mask[...], rest[2])
    natural = pick(natural, jnp.zeros_like(natural))
    value = dot3(split(heads_of(heads, 0)), split(natural[:LANES]))
    value = value + dot3(split(heads_of(heads, 1)), split(natural[LANES:]))
    shared = rest[2]
    blocks = slice_blocks(spot[0], LANES // slices // n_parts, n_parts)
    for at, block in enumerate(blocks):
        shared[block_rows(block, slices), :] = value[at * slices : (at + 1) * slices]
    value = shared[pl.ds(0, LANES), :]
    out[...] = pick(value[:HALF], swap(value[HALF:]))


def eliminate(gram, mask, row_count):
    size = gram.shape[0]
    row = lax.broadcasted_iota(jnp.int32, (size, LANES), 0)
    lane = lax.broadcasted_iota(jnp.int32, (size, LANES), 1)
    scaled = gram * (1.0 / row_count)
    unit = lax.rsqrt(jnp.broadcast_to(scaled[0:1, 0:1], (1, LANES)))
    scaled = scaled * unit * unit
    diagonal = jnp.where(lane == row, 1.0 - mask, 0.0)
    work = jnp.where(lane < HALF, scaled + diagonal, jnp.where(lane - HALF == row, 1.0, 0.0))
    done = []
    for base in range(0, size, SUBLANES):
        live = size - base
        columns = [
            jnp.broadcast_to(work[:, base + k : base + k + 1], (live, LANES))
            for k in range(SUBLANES)
        ]
        pivots = [work[k : k + 1] for k in range(SUBLANES)]
        for k in range(0, SUBLANES, 2):
            first, second = columns[k], columns[k + 1]
            a, b, c = first[k : k + 1], first[k + 1 : k + 2], second[k + 1 : k + 2]
            root = lax.rsqrt(a)
            next_root = lax.rsqrt(a * c - b * b) * (a * root)
            ratio = b * (root * root)
            columns[k : k + 2] = first * root, (second - first * ratio) * next_root
            pivots[k : k + 2] = pivots[k] * root, (pivots[k + 1] - pivots[k] * ratio) * next_root
            for m in range(k + 2, SUBLANES):
                for at in (k, k + 1):
                    weight = columns[at][m : m + 1]
                    columns[m] = columns[m] - columns[at] * weight
                    pivots[m] = pivots[m] - pivots[at] * weight
        done.append(jnp.concatenate(pivots, axis=0))
        work = work[SUBLANES:]
        for k in range(SUBLANES):
            work = work - columns[k][SUBLANES:] * pivots[k]
    return jnp.concatenate(done, axis=0) * unit


def project(raw, gram, mask, row_count, square):
    solved = eliminate(gram, mask, row_count)
    square[pl.ds(0, HALF), :] = solved
    planar = jnp.concatenate(
        [square[pl.ds(0, HALF // 2, stride=2), :], square[pl.ds(1, HALF // 2, stride=2), :]], axis=0
    )
    carried = dot3(split(raw), split(block_diagonal(swap(planar))), NT) * (1.0 / row_count)
    square[...] = carried
    pairs = carried.shape[0] // HALF
    even = square[pl.ds(0, pairs * 32, stride=2), :]
    odd = square[pl.ds(1, pairs * 32, stride=2), :]
    first, second = pick(even, swap(odd)), pick(swap(even), odd)
    blocks = []
    for pair in range(pairs):
        blocks += [first[pair * 32 : (pair + 1) * 32], second[pair * 32 : (pair + 1) * 32]]
    return swap(solved), jnp.concatenate(blocks, axis=0)


def mix(carried, high, low, out):
    weight = split(carried.T)
    for i in range(high.shape[0]):
        tile, sub = i // SUBLANES, i % SUBLANES
        value = dot3(weight, (high[i], low[i]))
        straight = pick(value[0:32], value[96:128])
        crossed = pick(value[32:64], value[64:96])
        out[pl.ds(tile * 256 + sub, 32, stride=SUBLANES), :] = straight + swap(crossed)


def unpack_gram(packed):
    return jnp.concatenate([packed, swap(packed)], axis=0)


def bond_one_kernel(row_count, n_parts, *refs):
    parts, heads, refs = refs[:n_parts], refs[n_parts : 2 * n_parts], refs[2 * n_parts :]
    spot, mask, high, low, inverse, carried, basis, out, square = refs
    packed = added(parts)
    zero = jnp.zeros_like(packed)
    square[...] = jnp.concatenate([pick(packed, zero), pick(swap(packed), zero)], axis=0)
    slices = basis.shape[0]
    blocks = slice_blocks(spot[0], LANES // slices // n_parts, n_parts)
    mixture = jnp.concatenate([square[block_rows(block, slices), :] for block in blocks], axis=0)
    gram = exact(mixture, mixture, TN)[:HALF]
    raw = []
    for pair in range(2):
        value = dot3(split(heads_of(heads, pair)), split(mixture), TN)
        raw.append(pick(value[:HALF], swap(value[HALF:])))
    solved, moved = project(jnp.concatenate(raw, axis=0), gram, mask[...], row_count, square)
    inverse[...] = solved
    carried[...] = moved
    full = jnp.concatenate([pick(solved, jnp.zeros_like(solved)), jnp.zeros_like(solved)], axis=0)
    basis[...] = exact(mixture[:slices], full, NT)
    mix(moved, high, low, out)


def bond_kernel(row_count, n_parts, *refs):
    parts, refs = refs[:n_parts], refs[n_parts:]
    mask, high, low, inverse, carried, out, square = refs
    value = added(parts)
    solved, moved = project(
        value[:LANES], unpack_gram(value[LANES:]), mask[...], row_count, square
    )
    inverse[...] = solved
    carried[...] = moved
    mix(moved, high, low, out)


def last_kernel(row_count, n_parts, *refs):
    parts, refs = refs[:n_parts], refs[n_parts:]
    mask, member, kept, relay, basis, out = refs
    value = added(parts)
    solved = swap(eliminate(unpack_gram(value[LANES:]), mask[...], row_count))
    carried = exact(value[:LANES], block_diagonal(solved), NT) * (1.0 / row_count)
    cores = kept[member[0]]
    slices = cores.shape[1]
    own = jnp.concatenate([cores[0], cores[1]], axis=1)
    term = None
    for pair, both in enumerate((own, relay[pl.ds(HALF, slices), :])):
        side = carried[pair * HALF : (pair + 1) * HALF]
        zero = jnp.zeros_like(side)
        both = exact(both, jnp.concatenate([pick(side, zero), pick(swap(side), zero)], axis=0))
        term = both if term is None else term + both
    out[pl.ds(0, slices), :] = pick(term, swap(basis[...]))
    out[pl.ds(slices, HALF), :] = solved


def place_kernel(position, member, mine, theirs, *refs):
    out, sems = refs[-2:]
    here = member[0]
    copies = [
        pltpu.make_async_copy(mine, out.at[here, position], sems.at[0]),
        pltpu.make_async_copy(theirs, out.at[1 - here, position], sems.at[1]),
    ]
    for copy in copies:
        copy.start()
    for copy in copies:
        copy.wait()


def own_kernel(position, member, mine, mixture, before, *refs):
    out, block, sem = refs
    slices = mine.shape[0] - HALF
    weight = split(block_diagonal(mine[pl.ds(slices, HALF), :]))
    block[...] = dot3(split(mixture[...]), weight, NT)
    copy = pltpu.make_async_copy(block, out.at[member[0], position], sem)
    copy.start()
    copy.wait()


def final_kernel(position, member, mine, near, far, across, away, before, *refs):
    first, last, out, blocks, sems = refs
    here = member[0]
    slices = first.shape[1]
    weight = split(block_diagonal(far[pl.ds(slices, HALF), :]))
    count = blocks.shape[0]
    height = away.shape[0] // count
    copies = []
    for at in range(count):
        value = away[pl.ds(at * height, height), :]
        blocks[at] = dot3(split(value), weight, NT)
        place = out.at[1 - here, position, pl.ds(at * height, height), :]
        copies.append(pltpu.make_async_copy(blocks.at[at], place, sems.at[at]))
        copies[-1].start()
    for place, terms in ((here, (mine, near)), (1 - here, (far, across))):
        head = terms[0][pl.ds(0, slices), :]
        first[place] = swap(head)[:, :HALF]
        last[place] = (head + terms[1][pl.ds(0, slices), :])[:, :HALF]
    for copy in copies:
        copy.wait()


def gram_kernel(mine, theirs, carried, kept, other, mixture, out, spread):
    count, rows = kept.shape[0], kept.shape[1]
    tiles = rows // 256
    mixture[...] = mine[...] + theirs[...]
    everything = split(mixture[...])
    gram = dot3(everything, everything, TN)
    weight = split(carried[...])
    height = 2 * count * 32
    for tile in range(tiles):
        for sub in range(SUBLANES):
            packed = mixture[pl.ds(tile * 256 + sub, 32, stride=SUBLANES), :]
            crossed = swap(packed)
            zero = jnp.zeros_like(packed)
            blocks = jnp.concatenate(
                [pick(packed, zero), pick(crossed, zero), pick(zero, crossed), pick(zero, packed)],
                axis=0,
            )
            spread[pl.ds(tile * height * SUBLANES + sub, height, stride=SUBLANES), :] = dot3(
                weight, split(blocks)
            )
    raw = []
    for half, cores in enumerate((kept, other)):
        for index in range(count):
            s = half * count + index
            own = jnp.concatenate(
                [spread[pl.ds((tile * 2 * count + s) * 256, 256), :] for tile in range(tiles)],
                axis=0,
            )
            raw.append(dot3(split(cores[index]), split(own), TN))
    for pair in range(count):
        even, odd = raw[2 * pair], raw[2 * pair + 1]
        out[pl.ds(pair * HALF, HALF), :] = pick(even[:HALF], odd[HALF:]) + swap(
            pick(odd[:HALF], even[HALF:])
        )
    gram = gram[:HALF] + swap(gram[HALF:])
    out[pl.ds(2 * HALF, 32), :] = pick(gram[:32], swap(gram[32:]))


def basis_kernel(mixture, inverse, out):
    weight = split(block_diagonal(inverse[...]))
    out[...] = dot3(split(mixture[...]), weight, NT)


def kernel_call(body, outs, scratch, *operands, aliases=None, in_hbm=(), limit=24 << 20):
    moved = sum(x.size * x.dtype.itemsize for x in (*operands, *outs))
    specs = []
    for at, x in enumerate((*operands, *outs)):
        space = pltpu.VMEM
        if at in in_hbm:
            space = pltpu.HBM
        elif x.dtype == jnp.int32:
            space = pltpu.SMEM
        specs.append(pl.BlockSpec(memory_space=space))
    return pl.pallas_call(
        body,
        out_shape=outs,
        in_specs=specs[: len(operands)],
        out_specs=specs[len(operands) :],
        scratch_shapes=scratch,
        input_output_aliases=aliases or {},
        compiler_params=pltpu.CompilerParams(vmem_limit_bytes=limit),
        cost_estimate=pl.CostEstimate(flops=0, bytes_accessed=moved, transcendentals=0),
    )(*operands)


def shape(*dims, dtype=jnp.float32):
    return jax.ShapeDtypeStruct(dims, dtype)


def scratch(*dims):
    return pltpu.VMEM(dims, jnp.float32)


def in_rows(value):
    lead, (slices, width) = value.shape[:-2], value.shape[-2:]
    value = value.reshape(*lead, slices // SUBLANES, SUBLANES, width // LANES, LANES)
    value = jnp.swapaxes(value, -2, -3)
    return value.reshape(*lead, slices * width // LANES, LANES)


def out_of_rows(value, slices):
    lead, (rows, _) = value.shape[:-2], value.shape[-2:]
    value = value.reshape(*lead, slices // SUBLANES, rows // slices, SUBLANES, LANES)
    value = jnp.swapaxes(value, -2, -3)
    return value.reshape(*lead, slices, rows // slices * LANES)


def spread(value, axis, step):
    radix, stride = step
    if radix == 2:
        return [value, flip(value, axis, stride)]
    size = lax.axis_size(axis)
    parts = [value]
    for by in SHIFTS:
        pairs = [
            (index, index + ((index // stride + by) % 4 - index // stride % 4) * stride)
            for index in range(size)
        ]
        parts.append(lax.ppermute(value, axis, pairs))
    return parts


def exchanged(value, axis):
    steps = radices(lax.axis_size(axis))
    for at, (radix, stride) in enumerate(steps):
        parts = spread(value, axis, (radix, stride))
        if at < len(steps) - 1:
            value = sum(parts[1:], parts[0])
    return parts


def tiled(first_cores, mid_cores, last_cores, sketch_mid, sketch_last, ranks):
    members, count, slices, rank_size = first_cores.shape
    middle = mid_cores.shape[2]
    width = mid_cores.shape[4]
    total_slices = slices * lax.axis_size("mode")
    low = lax.axis_size("rep") // members
    member = lax.axis_index("rep") // low
    here = member[None].astype(jnp.int32)
    spot = lax.axis_index("mode")[None].astype(jnp.int32)
    height = 2 * count * 32
    rows = slices * 32
    inner, outer = radices(lax.axis_size("mode"))

    def half_of(source, position, index):
        part = lax.dynamic_slice(
            source, (index, 0, position, 0, 0), (1, count, 1, slices, width)
        )
        return in_rows(part.reshape(count, slices, width))

    (part,) = kernel_call(
        start_kernel,
        [shape(height, LANES)],
        [scratch(2 * height, LANES)],
        here,
        spot,
        last_cores,
        sketch_last,
    )
    late_cores, late_sketch, late_ranks, part = lax.optimization_barrier(
        (mid_cores, sketch_mid, ranks, part)
    )
    masks = (jnp.arange(rank_size, dtype=jnp.int32)[None, :] < late_ranks[:, None]).astype(
        jnp.float32
    )
    masks = jnp.concatenate([masks, masks], axis=1)[:, None, :]
    sketch_rows = in_rows(late_sketch)
    sketch_rows = [sketch_rows[position] for position in range(middle)]
    kept = [None] * (middle - 1) + [half_of(late_cores, middle - 1, member)]
    sent = [None] * (middle - 1) + [half_of(late_cores, middle - 1, 1 - member)]
    wide = shape(slices, height, LANES, dtype=jnp.bfloat16)
    room = [
        scratch(2 * height, LANES),
        scratch(height * slices, LANES),
        scratch(slices, HALF, LANES),
    ]
    parts = exchanged(part, "mode")
    block = shape(height // 2 + slices, LANES)
    keep, send, relay, *own_mixed = kernel_call(
        functools.partial(meet_kernel, len(parts)),
        [block, block, shape(height // 2 + slices, LANES), wide, wide],
        room,
        *parts,
        here,
        first_cores,
        last_cores,
        masks[middle],
        kept[-1],
        sent[-1],
        sketch_rows[-1],
    )
    later_cores, keep, send = lax.optimization_barrier((late_cores, keep, send))
    for position in range(middle - 1):
        if position == middle - 2:
            sent[position] = half_of(mid_cores, position, 1 - member)
        else:
            sent[position] = half_of(later_cores, position, 1 - member)
        kept[position] = half_of(later_cores, position, member)
    traded = [flip(sent[position], "rep", low) for position in range(middle)]
    cores = list(zip(kept, traded))
    keeps, sends = [keep], []
    sends.append(flip(send, "rep", low))
    for step in range(1, inner[0]):
        bits = step * inner[1]
        keeps.append(flip(keep, "mode", bits))
        pairs = [
            ((m * 2 * low + r), ((m ^ bits) * 2 * low + (r ^ low)))
            for m in range(lax.axis_size("mode"))
            for r in range(2 * low)
        ]
        sends.append(lax.ppermute(send, ("mode", "rep"), pairs))
    part, heads = kernel_call(
        functools.partial(merge_kernel, len(keeps), height // 2),
        [shape(height, LANES), shape(2 * len(keeps) * slices, LANES)],
        [],
        *keeps,
        *sends,
    )
    heads = spread(heads, "mode", outer)
    relay = flip(relay, "rep", low)
    mixed = [None] * middle
    mixed[-1] = kernel_call(
        mixed_kernel,
        [wide, wide],
        [scratch(height, LANES), scratch(height // 2 * slices, LANES)],
        relay,
        traded[-1],
        *own_mixed,
    )
    for position in range(middle - 2, -1, -1):
        if position == middle - 2:
            parts = spread(part, "mode", outer)
        else:
            parts = exchanged(part, "mode")
        body, more, result = sketch_kernel, (), shape(height, LANES)
        if position == 0:
            body = functools.partial(first_kernel, slices=slices)
            more, result = (*heads, spot), shape(total_slices // 2, LANES)
        part, *mixed[position] = kernel_call(
            functools.partial(body, len(parts)),
            [result, wide, wide],
            room,
            *parts,
            *more,
            *((masks[1], masks[0]) if position == 0 else (masks[position + 1],)),
            *cores[position],
            sketch_rows[position],
        )
    square = scratch(count * HALF, LANES)
    part = part + flip(part, "rep", 1)
    parts = exchanged(part, "mode")
    inverse, carried, basis, part = kernel_call(
        functools.partial(bond_one_kernel, float(total_slices), len(parts)),
        [shape(HALF, LANES), shape(height, LANES), shape(slices, LANES), shape(rows, LANES)],
        [square],
        *parts,
        *heads,
        spot,
        masks[0],
        *mixed[0],
    )
    row_count = float(total_slices * rank_size)
    whole = shape(members, middle, rows, LANES)
    blocks = ()
    for position in range(middle):
        near = flip(part, "rep", 1)
        mixture, part = kernel_call(
            gram_kernel,
            [shape(rows, LANES), shape(2 * HALF + 32, LANES)],
            [scratch(height * slices, LANES)],
            part,
            near,
            carried,
            *cores[position],
        )
        parts = exchanged(part, "mode")
        mask = masks[position + 1]
        if position < middle - 1:
            inverse, carried, part = kernel_call(
                functools.partial(bond_kernel, row_count, len(parts)),
                [shape(HALF, LANES), shape(height, LANES), shape(rows, LANES)],
                [square],
                *parts,
                mask,
                *mixed[position + 1],
            )
            (own,) = kernel_call(basis_kernel, [shape(rows, LANES)], [], mixture, inverse)
            other = flip(own, "rep", low)
            blocks = kernel_call(
                functools.partial(place_kernel, position),
                [whole],
                [pltpu.SemaphoreType.DMA((2,))],
                here,
                own,
                other,
                *blocks,
                aliases={3: 0} if blocks else None,
                in_hbm=(3, 4),
            )
    away = flip(mixture, "rep", low)
    (last,) = kernel_call(
        functools.partial(last_kernel, row_count, len(parts)),
        [shape(slices + HALF, LANES)],
        [],
        *parts,
        mask,
        here,
        last_cores,
        relay,
        basis,
    )
    near, far, across = (flip(last, "rep", bits) for bits in (1, low, low + 1))
    blocks = kernel_call(
        functools.partial(own_kernel, middle - 1),
        [whole],
        [scratch(rows, LANES), pltpu.SemaphoreType.DMA],
        here,
        last,
        mixture,
        *blocks,
        aliases={3: 0},
        in_hbm=(3, 4),
    )
    pieces = slices // SUBLANES
    rounded_first, rounded_last, blocks = kernel_call(
        functools.partial(final_kernel, middle - 1),
        [shape(members, slices, rank_size), shape(members, slices, rank_size), whole],
        [scratch(pieces, rows // pieces, LANES), pltpu.SemaphoreType.DMA((pieces,))],
        here,
        last,
        near,
        far,
        across,
        away,
        *blocks,
        aliases={6: 2},
        in_hbm=(6, 9),
    )
    return (rounded_first, out_of_rows(blocks, slices), rounded_last)


def per_device(*arguments):
    members, count, slices, rank_size = arguments[0].shape
    steps = radices(lax.axis_size("mode"))
    fits = (
        members == 2
        and count == 2
        and rank_size == HALF
        and slices % SUBLANES == 0
        and slices * lax.axis_size("mode") == LANES
        and lax.axis_size("rep") == 2 * members
        and len(steps) == 2
    )
    return tiled(*arguments) if fits else general(*arguments)


def solution(mesh):
    return jax.shard_map(
        per_device,
        mesh=mesh,
        in_specs=(
            P(None, "rep", "mode", None),
            P(None, "rep", None, "mode", None),
            P(None, "rep", "mode", None),
            P(None, "mode", None),
            P("mode", None),
            P(),
        ),
        out_specs=(P(None, "mode", None), P(None, None, "mode", None), P(None, "mode", None)),
        check_vma=False,
    )
```

```python
import functools

import jax
import jax.numpy as jnp
from jax import lax
from jax.experimental import pallas as pl
from jax.experimental.pallas import tpu as pltpu
from jax.sharding import PartitionSpec as P

PRECISE = lax.Precision.HIGHEST
FAST = lax.Precision.HIGH


def lower_inverse(gram_matrix):
    factor = jnp.linalg.cholesky(gram_matrix)
    identity = jnp.eye(gram_matrix.shape[-1], dtype=gram_matrix.dtype)
    return jax.scipy.linalg.solve_triangular(factor, identity, lower=True)


def flip(value, axis, bits):
    size = lax.axis_size(axis)
    return lax.ppermute(value, axis, [(index, index ^ bits) for index in range(size)])


def radices(size):
    stride, out = 1, []
    if (size.bit_length() - 1) % 2:
        out.append((2, stride))
        stride *= 2
    while stride < size:
        out.append((4, stride))
        stride *= 4
    return out


def total(value, axis, size=None):
    for radix, stride in radices(size or lax.axis_size(axis)):
        parts = [flip(value, axis, step * stride) for step in range(1, radix)]
        value = sum(parts, value)
    return value


def gathered(value, axis, dim):
    for radix, stride in radices(lax.axis_size(axis)):
        parts = [flip(value, axis, step * stride) for step in range(1, radix)]
        value = jnp.concatenate([value] + parts, axis=dim)
    return value


def general(first_cores, mid_cores, last_cores, sketch_mid, sketch_last, ranks):
    members, _, slices, rank_size = first_cores.shape
    middle = mid_cores.shape[2]
    total_slices = slices * lax.axis_size("mode")
    low = lax.axis_size("rep") // members
    member = lax.axis_index("rep") // low
    masks = (jnp.arange(rank_size, dtype=jnp.int32)[None, :] < ranks[:, None]).astype(jnp.float32)

    def own_and_other(value):
        kept = lax.dynamic_index_in_dim(value, member, 0, keepdims=False)
        sent = lax.dynamic_index_in_dim(value, 1 - member, 0, keepdims=False)
        return jnp.concatenate([kept, flip(sent, "rep", low)], axis=0)

    def both_members(value):
        other = flip(value, "rep", low)
        return jnp.stack(
            [jnp.where(member == 0, value, other), jnp.where(member == 0, other, value)]
        )

    last = own_and_other(last_cores)
    first = own_and_other(first_cores)
    cores = [None] * middle
    for position in range(middle - 1, -1, -1):
        cores[position] = own_and_other(
            mid_cores[:, :, position].reshape(members, -1, slices, rank_size, rank_size)
        )
    sketch_cores = sketch_mid.reshape(middle, slices, rank_size, rank_size)
    sketches = [None] * (middle + 1)
    mixed = [None] * middle
    sketches[middle] = (
        total(jnp.einsum("sic,ie->sce", last, sketch_last, precision=FAST), "mode") * masks[middle]
    )
    for position in range(middle - 1, -1, -1):
        mixed[position] = jnp.einsum(
            "sicd,sde->sice", cores[position], sketches[position + 1], precision=FAST
        )
        folded = jnp.einsum(
            "sice,ife->scf", mixed[position], sketch_cores[position], precision=FAST
        )
        sketches[position] = total(folded, "mode") * masks[position]

    everything = gathered(first, "mode", 1)
    mixture = total(
        jnp.einsum("sid,sde->ie", everything, sketches[0], precision=PRECISE), "rep", low
    )
    gram = jnp.einsum("ie,if->ef", mixture, mixture, precision=PRECISE)
    raw = jnp.einsum("ie,sid->sed", mixture, everything, precision=PRECISE)
    inverse = lower_inverse(gram / total_slices + jnp.diag(1.0 - masks[0]))
    carried = jnp.einsum("fe,sed->sfd", inverse, raw, precision=PRECISE) / total_slices
    basis = jnp.einsum("ie,fe->if", mixture[:slices], inverse, precision=PRECISE)
    rounded_first = both_members(basis)

    rows = total_slices * rank_size
    blocks = []
    for position in range(middle):
        mixture = total(
            jnp.einsum("sac,sice->iae", carried, mixed[position], precision=FAST), "rep", low
        )
        gram = jnp.einsum("iae,iaf->ef", mixture, mixture, precision=PRECISE)
        spread = jnp.einsum("sac,iae->sice", carried, mixture, precision=FAST)
        raw = jnp.einsum("sice,sicd->sed", spread, cores[position], precision=FAST)
        both = total(jnp.concatenate([raw, gram[None]], axis=0), "mode")
        raw, gram = both[:-1], both[-1]
        inverse = lower_inverse(gram / rows + jnp.diag(1.0 - masks[position + 1]))
        carried = jnp.einsum("fe,sed->sfd", inverse, raw, precision=PRECISE) / rows
        basis = jnp.einsum("iae,fe->iaf", mixture, inverse, precision=FAST)
        blocks.append(both_members(basis.reshape(slices, rank_size * rank_size)))
    rounded_mid = jnp.stack(blocks, axis=1)
    local_last = jnp.einsum("sac,sic->ia", carried, last, precision=PRECISE)
    rounded_last = both_members(total(local_last, "rep", low))
    return (rounded_first, rounded_mid, rounded_last)


LANES = 128
SUBLANES = 8
HALF = 64
NN = (((1,), (0,)), ((), ()))
NT = (((1,), (1,)), ((), ()))
TN = (((0,), (0,)), ((), ()))


def left_half(rows):
    return lax.broadcasted_iota(jnp.int32, (rows, LANES), 1) < HALF


def swap(value):
    return pltpu.roll(value, HALF, 1)


def pick(left, right):
    return jnp.where(left_half(left.shape[0]), left, right)


def split(value):
    high = value.astype(jnp.bfloat16)
    return high, (value - high.astype(jnp.float32)).astype(jnp.bfloat16)


def dot(left, right, dims=NN):
    return lax.dot_general(left, right, dims, preferred_element_type=jnp.float32)


def dot3(left, right, dims=NN):
    (lh, ll), (rh, rl) = left, right
    at_left, at_right = dims[0][0][0], dims[0][1][0]
    zero = jnp.zeros_like(rl)
    wide = jnp.concatenate(
        [
            jnp.concatenate([rh, rh], axis=at_right),
            jnp.concatenate([rl, zero], axis=at_right),
        ],
        axis=1 - at_right,
    )
    value = dot(jnp.concatenate([lh, ll], axis=at_left), wide, dims)
    return value[:, :LANES] + value[:, LANES:]


def exact(left, right, dims=NN):
    return lax.dot_general(
        left, right, dims, precision=PRECISE, preferred_element_type=jnp.float32
    )


def block_diagonal(value):
    zero = jnp.zeros_like(value)
    return jnp.concatenate([pick(value, zero), pick(zero, swap(value))], axis=0)


def spread_rows(packed, scratch):
    count = packed.shape[0]
    scratch[pl.ds(0, count, stride=2), :] = packed
    scratch[pl.ds(1, count, stride=2), :] = swap(packed)
    return scratch[pl.ds(0, 2 * count), :]


def start_kernel(member, _, last, sketch, out, scratch):
    count = last.shape[1]
    for half, index in enumerate((member[0], 1 - member[0])):
        cores = last[index]
        for s in range(count):
            scratch[pl.ds((half * count + s) * HALF, HALF), pl.ds(0, HALF)] = exact(
                cores[s], sketch[...], TN
            )
    rows = out.shape[0]
    even = scratch[pl.ds(0, rows, stride=2), :]
    odd = scratch[pl.ds(1, rows, stride=2), :]
    out[...] = pick(even, swap(odd))


def merge_kernel(n_parts, rows, *refs):
    keeps, sends, (part, heads) = refs[:n_parts], refs[n_parts : 2 * n_parts], refs[2 * n_parts :]
    height = keeps[0].shape[0] - rows
    for pair, terms in enumerate((keeps, sends)):
        part[pl.ds(pair * rows, rows), :] = added([term.at[pl.ds(0, rows)] for term in terms])
        for at, term in enumerate(terms):
            place = pl.ds((pair * n_parts + at) * height, height)
            heads[place, :] = term[pl.ds(rows, height), :]


def heads_of(parts, pair):
    rows = parts[0].shape[0] // 2
    return jnp.concatenate([part[pl.ds(pair * rows, rows), :] for part in parts], axis=0)


def added(parts):
    value = parts[0][...]
    for part in parts[1:]:
        value = value + part[...]
    return value


def sketch_step(parts, mask, kept, other, sketch, high, low, wide, product, narrow):
    count = kept.shape[0]
    rows = kept.shape[1]
    tiles = rows // 256
    natural = spread_rows(added(parts) * mask[...], wide)
    for half, cores in enumerate((kept, other)):
        for index in range(count):
            s = half * count + index
            weight = split(block_diagonal(natural[s * HALF : (s + 1) * HALF]))
            result = dot3(split(cores[index]), weight)
            for tile in range(tiles):
                product[pl.ds((tile * 2 * count + s) * 256, 256), :] = result[
                    tile * 256 : (tile + 1) * 256
                ]
    height = 2 * count * 32
    total_value = None
    for tile in range(tiles):
        for sub in range(SUBLANES):
            i = tile * SUBLANES + sub
            packed = sketch[pl.ds(tile * 256 + sub, 32, stride=SUBLANES), :]
            weight = split(block_diagonal(spread_rows(packed, narrow.at[i])))
            own = split(product[pl.ds(tile * height * SUBLANES + sub, height, stride=SUBLANES), :])
            high[i] = own[0]
            low[i] = own[1]
            term = dot3(own, weight, NT)
            total_value = term if total_value is None else total_value + term
    return total_value


def sketch_kernel(n_parts, *refs):
    parts, refs = refs[:n_parts], refs[n_parts:]
    mask, kept, other, sketch, out, *rest = refs
    out[...] = sketch_step(parts, mask, kept, other, sketch, *rest)


def meet_kernel(n_parts, *refs):
    parts, refs = refs[:n_parts], refs[n_parts:]
    member, first, last, mask, kept, other, sketch, keep, send, relay, *rest = refs
    value = sketch_step(parts, mask, kept, other, sketch, *rest)
    rows = value.shape[0] // 2
    slices = first.shape[2]
    for out, half, index in ((keep, 0, member[0]), (send, 1, 1 - member[0])):
        out[pl.ds(0, rows), :] = value[half * rows : (half + 1) * rows]
        heads = first[index]
        out[pl.ds(rows, slices), :] = jnp.concatenate([heads[0], heads[1]], axis=1)
    tail = last[1 - member[0]]
    relay[pl.ds(0, rows), :] = added([part.at[pl.ds(rows, rows)] for part in parts]) * mask[...]
    relay[pl.ds(rows, slices), :] = jnp.concatenate([tail[0], tail[1]], axis=1)


def mixed_kernel(relay, cores, own_high, own_low, high, low, wide, product):
    count, rows = cores.shape[:2]
    tiles = rows // 256
    height = count * 32
    natural = spread_rows(relay[pl.ds(0, height), :], wide)
    for index in range(count):
        weight = split(block_diagonal(natural[index * HALF : (index + 1) * HALF]))
        result = dot3(split(cores[index]), weight)
        for tile in range(tiles):
            product[pl.ds((tile * count + index) * 256, 256), :] = result[
                tile * 256 : (tile + 1) * 256
            ]
    for i in range(high.shape[0]):
        start = i // SUBLANES * height * SUBLANES + i % SUBLANES
        value = split(product[pl.ds(start, height, stride=SUBLANES), :])
        high[i] = jnp.concatenate([own_high[i][:height], value[0]], axis=0)
        low[i] = jnp.concatenate([own_low[i][:height], value[1]], axis=0)


OTHERS = (1, 3, 2)


def slice_blocks(spot, n_inner):
    inner, outer = spot % n_inner, spot // n_inner
    return [
        (outer ^ by) * n_inner + (inner ^ step)
        for by in (0,) + OTHERS
        for step in range(n_inner)
    ]


def block_rows(block, count):
    return pl.ds(pl.multiple_of(block * count, SUBLANES), count)


def first_kernel(n_parts, *refs, slices):
    parts, heads, refs = refs[:n_parts], refs[n_parts : 2 * n_parts], refs[2 * n_parts :]
    spot, mask, next_mask, kept, other, sketch, out, *rest = refs
    value = sketch_step(parts, mask, kept, other, sketch, *rest)
    natural = spread_rows(value * next_mask[...], rest[2])
    natural = pick(natural, jnp.zeros_like(natural))
    value = dot3(split(heads_of(heads, 0)), split(natural[:LANES]))
    value = value + dot3(split(heads_of(heads, 1)), split(natural[LANES:]))
    shared = rest[2]
    blocks = slice_blocks(spot[0], LANES // slices // n_parts)
    for at, block in enumerate(blocks):
        shared[block_rows(block, slices), :] = value[at * slices : (at + 1) * slices]
    value = shared[pl.ds(0, LANES), :]
    out[...] = pick(value[:HALF], swap(value[HALF:]))


def eliminate(gram, mask, row_count):
    size = gram.shape[0]
    row = lax.broadcasted_iota(jnp.int32, (size, LANES), 0)
    lane = lax.broadcasted_iota(jnp.int32, (size, LANES), 1)
    scaled = gram * (1.0 / row_count)
    unit = lax.rsqrt(jnp.broadcast_to(scaled[0:1, 0:1], (1, LANES)))
    scaled = scaled * unit * unit
    diagonal = jnp.where(lane == row, 1.0 - mask, 0.0)
    work = jnp.where(lane < HALF, scaled + diagonal, jnp.where(lane - HALF == row, 1.0, 0.0))
    done = []
    for base in range(0, size, SUBLANES):
        live = size - base
        columns = [
            jnp.broadcast_to(work[:, base + k : base + k + 1], (live, LANES))
            for k in range(SUBLANES)
        ]
        pivots = [work[k : k + 1] for k in range(SUBLANES)]
        for k in range(0, SUBLANES, 2):
            first, second = columns[k], columns[k + 1]
            a, b, c = first[k : k + 1], first[k + 1 : k + 2], second[k + 1 : k + 2]
            root = lax.rsqrt(a)
            next_root = lax.rsqrt(a * c - b * b) * (a * root)
            ratio = b * (root * root)
            columns[k : k + 2] = first * root, (second - first * ratio) * next_root
            pivots[k : k + 2] = pivots[k] * root, (pivots[k + 1] - pivots[k] * ratio) * next_root
            for m in range(k + 2, SUBLANES):
                for at in (k, k + 1):
                    weight = columns[at][m : m + 1]
                    columns[m] = columns[m] - columns[at] * weight
                    pivots[m] = pivots[m] - pivots[at] * weight
        done.append(jnp.concatenate(pivots, axis=0))
        work = work[SUBLANES:]
        for k in range(SUBLANES):
            work = work - columns[k][SUBLANES:] * pivots[k]
    return jnp.concatenate(done, axis=0) * unit


def project(raw, gram, mask, row_count, square):
    solved = eliminate(gram, mask, row_count)
    square[pl.ds(0, HALF), :] = solved
    planar = jnp.concatenate(
        [square[pl.ds(0, HALF // 2, stride=2), :], square[pl.ds(1, HALF // 2, stride=2), :]], axis=0
    )
    carried = dot3(split(raw), split(block_diagonal(swap(planar))), NT) * (1.0 / row_count)
    square[...] = carried
    pairs = carried.shape[0] // HALF
    even = square[pl.ds(0, pairs * 32, stride=2), :]
    odd = square[pl.ds(1, pairs * 32, stride=2), :]
    first, second = pick(even, swap(odd)), pick(swap(even), odd)
    blocks = []
    for pair in range(pairs):
        blocks += [first[pair * 32 : (pair + 1) * 32], second[pair * 32 : (pair + 1) * 32]]
    return swap(solved), jnp.concatenate(blocks, axis=0)


def mix(carried, high, low, out):
    weight = split(carried.T)
    for i in range(high.shape[0]):
        tile, sub = i // SUBLANES, i % SUBLANES
        value = dot3(weight, (high[i], low[i]))
        straight = pick(value[0:32], value[96:128])
        crossed = pick(value[32:64], value[64:96])
        out[pl.ds(tile * 256 + sub, 32, stride=SUBLANES), :] = straight + swap(crossed)


def unpack_gram(packed):
    return jnp.concatenate([packed, swap(packed)], axis=0)


def bond_one_kernel(row_count, n_parts, *refs):
    parts, heads, refs = refs[:n_parts], refs[n_parts : 2 * n_parts], refs[2 * n_parts :]
    spot, mask, high, low, inverse, carried, basis, out, square = refs
    packed = added(parts)
    zero = jnp.zeros_like(packed)
    square[...] = jnp.concatenate([pick(packed, zero), pick(swap(packed), zero)], axis=0)
    slices = basis.shape[0]
    blocks = slice_blocks(spot[0], LANES // slices // n_parts)
    mixture = jnp.concatenate([square[block_rows(block, slices), :] for block in blocks], axis=0)
    gram = dot3(split(mixture), split(mixture), TN)[:HALF]
    raw = []
    for pair in range(2):
        value = dot3(split(heads_of(heads, pair)), split(mixture), TN)
        raw.append(pick(value[:HALF], swap(value[HALF:])))
    solved, moved = project(jnp.concatenate(raw, axis=0), gram, mask[...], row_count, square)
    inverse[...] = solved
    carried[...] = moved
    full = jnp.concatenate([pick(solved, jnp.zeros_like(solved)), jnp.zeros_like(solved)], axis=0)
    basis[...] = exact(mixture[:slices], full, NT)
    mix(moved, high, low, out)


def bond_kernel(row_count, n_parts, *refs):
    parts, refs = refs[:n_parts], refs[n_parts:]
    mask, high, low, inverse, carried, out, square = refs
    value = added(parts)
    solved, moved = project(
        value[:LANES], unpack_gram(value[LANES:]), mask[...], row_count, square
    )
    inverse[...] = solved
    carried[...] = moved
    mix(moved, high, low, out)


def last_kernel(row_count, n_parts, *refs):
    parts, refs = refs[:n_parts], refs[n_parts:]
    mask, member, kept, relay, basis, out = refs
    value = added(parts)
    solved = swap(eliminate(unpack_gram(value[LANES:]), mask[...], row_count))
    carried = exact(value[:LANES], block_diagonal(solved), NT) * (1.0 / row_count)
    cores = kept[member[0]]
    slices = cores.shape[1]
    own = jnp.concatenate([cores[0], cores[1]], axis=1)
    term = None
    for pair, both in enumerate((own, relay[pl.ds(HALF, slices), :])):
        side = carried[pair * HALF : (pair + 1) * HALF]
        zero = jnp.zeros_like(side)
        both = exact(both, jnp.concatenate([pick(side, zero), pick(swap(side), zero)], axis=0))
        term = both if term is None else term + both
    out[pl.ds(0, slices), :] = pick(term, swap(basis[...]))
    out[pl.ds(slices, HALF), :] = solved


def place_kernel(position, member, mine, theirs, *refs):
    out, sems = refs[-2:]
    here = member[0]
    copies = [
        pltpu.make_async_copy(mine, out.at[here, position], sems.at[0]),
        pltpu.make_async_copy(theirs, out.at[1 - here, position], sems.at[1]),
    ]
    for copy in copies:
        copy.start()
    for copy in copies:
        copy.wait()


def own_kernel(position, member, mine, mixture, before, *refs):
    out, block, sem = refs
    slices = mine.shape[0] - HALF
    weight = split(block_diagonal(mine[pl.ds(slices, HALF), :]))
    block[...] = dot3(split(mixture[...]), weight, NT)
    copy = pltpu.make_async_copy(block, out.at[member[0], position], sem)
    copy.start()
    copy.wait()


def final_kernel(position, member, mine, near, far, across, away, before, *refs):
    first, last, out, blocks, sems = refs
    here = member[0]
    slices = first.shape[1]
    weight = split(block_diagonal(far[pl.ds(slices, HALF), :]))
    count = blocks.shape[0]
    height = away.shape[0] // count
    copies = []
    for at in range(count):
        value = away[pl.ds(at * height, height), :]
        blocks[at] = dot3(split(value), weight, NT)
        place = out.at[1 - here, position, pl.ds(at * height, height), :]
        copies.append(pltpu.make_async_copy(blocks.at[at], place, sems.at[at]))
        copies[-1].start()
    for place, terms in ((here, (mine, near)), (1 - here, (far, across))):
        head = terms[0][pl.ds(0, slices), :]
        first[place] = swap(head)[:, :HALF]
        last[place] = (head + terms[1][pl.ds(0, slices), :])[:, :HALF]
    for copy in copies:
        copy.wait()


def gram_kernel(mine, theirs, carried, kept, other, mixture, out, spread):
    count, rows = kept.shape[0], kept.shape[1]
    tiles = rows // 256
    mixture[...] = mine[...] + theirs[...]
    everything = split(mixture[...])
    gram = dot3(everything, everything, TN)
    weight = split(carried[...])
    height = 2 * count * 32
    for tile in range(tiles):
        for sub in range(SUBLANES):
            packed = mixture[pl.ds(tile * 256 + sub, 32, stride=SUBLANES), :]
            crossed = swap(packed)
            zero = jnp.zeros_like(packed)
            blocks = jnp.concatenate(
                [pick(packed, zero), pick(crossed, zero), pick(zero, crossed), pick(zero, packed)],
                axis=0,
            )
            spread[pl.ds(tile * height * SUBLANES + sub, height, stride=SUBLANES), :] = dot3(
                weight, split(blocks)
            )
    raw = []
    for half, cores in enumerate((kept, other)):
        for index in range(count):
            s = half * count + index
            own = jnp.concatenate(
                [spread[pl.ds((tile * 2 * count + s) * 256, 256), :] for tile in range(tiles)],
                axis=0,
            )
            raw.append(dot3(split(cores[index]), split(own), TN))
    for pair in range(count):
        even, odd = raw[2 * pair], raw[2 * pair + 1]
        out[pl.ds(pair * HALF, HALF), :] = pick(even[:HALF], odd[HALF:]) + swap(
            pick(odd[:HALF], even[HALF:])
        )
    gram = gram[:HALF] + swap(gram[HALF:])
    out[pl.ds(2 * HALF, 32), :] = pick(gram[:32], swap(gram[32:]))


def basis_kernel(mixture, inverse, out):
    weight = split(block_diagonal(inverse[...]))
    out[...] = dot3(split(mixture[...]), weight, NT)


def kernel_call(body, outs, scratch, *operands, aliases=None, in_hbm=(), limit=24 << 20):
    moved = sum(x.size * x.dtype.itemsize for x in (*operands, *outs))
    specs = []
    for at, x in enumerate((*operands, *outs)):
        space = pltpu.VMEM
        if at in in_hbm:
            space = pltpu.HBM
        elif x.dtype == jnp.int32:
            space = pltpu.SMEM
        specs.append(pl.BlockSpec(memory_space=space))
    return pl.pallas_call(
        body,
        out_shape=outs,
        in_specs=specs[: len(operands)],
        out_specs=specs[len(operands) :],
        scratch_shapes=scratch,
        input_output_aliases=aliases or {},
        compiler_params=pltpu.CompilerParams(vmem_limit_bytes=limit),
        cost_estimate=pl.CostEstimate(flops=0, bytes_accessed=moved, transcendentals=0),
    )(*operands)


def shape(*dims, dtype=jnp.float32):
    return jax.ShapeDtypeStruct(dims, dtype)


def scratch(*dims):
    return pltpu.VMEM(dims, jnp.float32)


def in_rows(value):
    lead, (slices, width) = value.shape[:-2], value.shape[-2:]
    value = value.reshape(*lead, slices // SUBLANES, SUBLANES, width // LANES, LANES)
    value = jnp.swapaxes(value, -2, -3)
    return value.reshape(*lead, slices * width // LANES, LANES)


def out_of_rows(value, slices):
    lead, (rows, _) = value.shape[:-2], value.shape[-2:]
    value = value.reshape(*lead, slices // SUBLANES, rows // slices, SUBLANES, LANES)
    value = jnp.swapaxes(value, -2, -3)
    return value.reshape(*lead, slices, rows // slices * LANES)


def spread(value, axis, step):
    radix, stride = step
    if radix == 2:
        return [value, flip(value, axis, stride)]
    size = lax.axis_size(axis)
    parts = [value]
    for by in OTHERS:
        pairs = [(index, index ^ (by * stride)) for index in range(size)]
        parts.append(lax.ppermute(value, axis, pairs))
    return parts


def exchanged(value, axis):
    steps = radices(lax.axis_size(axis))
    for at, (radix, stride) in enumerate(steps):
        parts = spread(value, axis, (radix, stride))
        if at < len(steps) - 1:
            value = sum(parts[1:], parts[0])
    return parts


def tiled(first_cores, mid_cores, last_cores, sketch_mid, sketch_last, ranks):
    members, count, slices, rank_size = first_cores.shape
    middle = mid_cores.shape[2]
    width = mid_cores.shape[4]
    total_slices = slices * lax.axis_size("mode")
    low = lax.axis_size("rep") // members
    member = lax.axis_index("rep") // low
    here = member[None].astype(jnp.int32)
    spot = lax.axis_index("mode")[None].astype(jnp.int32)
    height = 2 * count * 32
    rows = slices * 32
    inner, outer = radices(lax.axis_size("mode"))

    def half_of(source, position, index):
        part = lax.dynamic_slice(
            source, (index, 0, position, 0, 0), (1, count, 1, slices, width)
        )
        return in_rows(part.reshape(count, slices, width))

    (part,) = kernel_call(
        start_kernel,
        [shape(height, LANES)],
        [scratch(2 * height, LANES)],
        here,
        spot,
        last_cores,
        sketch_last,
    )
    late_cores, late_sketch, late_ranks, part = lax.optimization_barrier(
        (mid_cores, sketch_mid, ranks, part)
    )
    masks = (jnp.arange(rank_size, dtype=jnp.int32)[None, :] < late_ranks[:, None]).astype(
        jnp.float32
    )
    masks = jnp.concatenate([masks, masks], axis=1)[:, None, :]
    sketch_rows = in_rows(late_sketch)
    sketch_rows = [sketch_rows[position] for position in range(middle)]
    kept = [None] * (middle - 1) + [half_of(late_cores, middle - 1, member)]
    sent = [None] * (middle - 1) + [half_of(late_cores, middle - 1, 1 - member)]
    wide = shape(slices, height, LANES, dtype=jnp.bfloat16)
    room = [
        scratch(2 * height, LANES),
        scratch(height * slices, LANES),
        scratch(slices, HALF, LANES),
    ]
    parts = exchanged(part, "mode")
    block = shape(height // 2 + slices, LANES)
    keep, send, relay, *own_mixed = kernel_call(
        functools.partial(meet_kernel, len(parts)),
        [block, block, shape(height // 2 + slices, LANES), wide, wide],
        room,
        *parts,
        here,
        first_cores,
        last_cores,
        masks[middle],
        kept[-1],
        sent[-1],
        sketch_rows[-1],
    )
    later_cores, keep, send = lax.optimization_barrier((late_cores, keep, send))
    for position in range(middle - 1):
        if position == middle - 2:
            sent[position] = half_of(mid_cores, position, 1 - member)
        else:
            sent[position] = half_of(later_cores, position, 1 - member)
        kept[position] = half_of(later_cores, position, member)
    traded = [flip(sent[position], "rep", low) for position in range(middle)]
    cores = list(zip(kept, traded))
    keeps, sends = [keep], []
    sends.append(flip(send, "rep", low))
    for step in range(1, inner[0]):
        bits = step * inner[1]
        keeps.append(flip(keep, "mode", bits))
        pairs = [
            ((m * 2 * low + r), ((m ^ bits) * 2 * low + (r ^ low)))
            for m in range(lax.axis_size("mode"))
            for r in range(2 * low)
        ]
        sends.append(lax.ppermute(send, ("mode", "rep"), pairs))
    part, heads = kernel_call(
        functools.partial(merge_kernel, len(keeps), height // 2),
        [shape(height, LANES), shape(2 * len(keeps) * slices, LANES)],
        [],
        *keeps,
        *sends,
    )
    heads = spread(heads, "mode", outer)
    relay = flip(relay, "rep", low)
    mixed = [None] * middle
    mixed[-1] = kernel_call(
        mixed_kernel,
        [wide, wide],
        [scratch(height, LANES), scratch(height // 2 * slices, LANES)],
        relay,
        traded[-1],
        *own_mixed,
    )
    for position in range(middle - 2, -1, -1):
        if position == middle - 2:
            parts = spread(part, "mode", outer)
        else:
            parts = exchanged(part, "mode")
        body, more, result = sketch_kernel, (), shape(height, LANES)
        if position == 0:
            body = functools.partial(first_kernel, slices=slices)
            more, result = (*heads, spot), shape(total_slices // 2, LANES)
        part, *mixed[position] = kernel_call(
            functools.partial(body, len(parts)),
            [result, wide, wide],
            room,
            *parts,
            *more,
            *((masks[1], masks[0]) if position == 0 else (masks[position + 1],)),
            *cores[position],
            sketch_rows[position],
        )
    square = scratch(count * HALF, LANES)
    part = part + flip(part, "rep", 1)
    parts = exchanged(part, "mode")
    inverse, carried, basis, part = kernel_call(
        functools.partial(bond_one_kernel, float(total_slices), len(parts)),
        [shape(HALF, LANES), shape(height, LANES), shape(slices, LANES), shape(rows, LANES)],
        [square],
        *parts,
        *heads,
        spot,
        masks[0],
        *mixed[0],
    )
    row_count = float(total_slices * rank_size)
    whole = shape(members, middle, rows, LANES)
    blocks = ()
    for position in range(middle):
        near = flip(part, "rep", 1)
        mixture, part = kernel_call(
            gram_kernel,
            [shape(rows, LANES), shape(2 * HALF + 32, LANES)],
            [scratch(height * slices, LANES)],
            part,
            near,
            carried,
            *cores[position],
        )
        parts = exchanged(part, "mode")
        mask = masks[position + 1]
        if position < middle - 1:
            inverse, carried, part = kernel_call(
                functools.partial(bond_kernel, row_count, len(parts)),
                [shape(HALF, LANES), shape(height, LANES), shape(rows, LANES)],
                [square],
                *parts,
                mask,
                *mixed[position + 1],
            )
            (own,) = kernel_call(basis_kernel, [shape(rows, LANES)], [], mixture, inverse)
            other = flip(own, "rep", low)
            blocks = kernel_call(
                functools.partial(place_kernel, position),
                [whole],
                [pltpu.SemaphoreType.DMA((2,))],
                here,
                own,
                other,
                *blocks,
                aliases={3: 0} if blocks else None,
                in_hbm=(3, 4),
            )
    away = flip(mixture, "rep", low)
    (last,) = kernel_call(
        functools.partial(last_kernel, row_count, len(parts)),
        [shape(slices + HALF, LANES)],
        [],
        *parts,
        mask,
        here,
        last_cores,
        relay,
        basis,
    )
    near, far, across = (flip(last, "rep", bits) for bits in (1, low, low + 1))
    blocks = kernel_call(
        functools.partial(own_kernel, middle - 1),
        [whole],
        [scratch(rows, LANES), pltpu.SemaphoreType.DMA],
        here,
        last,
        mixture,
        *blocks,
        aliases={3: 0},
        in_hbm=(3, 4),
    )
    pieces = slices // SUBLANES
    rounded_first, rounded_last, blocks = kernel_call(
        functools.partial(final_kernel, middle - 1),
        [shape(members, slices, rank_size), shape(members, slices, rank_size), whole],
        [scratch(pieces, rows // pieces, LANES), pltpu.SemaphoreType.DMA((pieces,))],
        here,
        last,
        near,
        far,
        across,
        away,
        *blocks,
        aliases={6: 2},
        in_hbm=(6, 9),
    )
    return (rounded_first, out_of_rows(blocks, slices), rounded_last)


def per_device(*arguments):
    members, count, slices, rank_size = arguments[0].shape
    steps = radices(lax.axis_size("mode"))
    fits = (
        members == 2
        and count == 2
        and rank_size == HALF
        and slices % SUBLANES == 0
        and slices * lax.axis_size("mode") == LANES
        and lax.axis_size("rep") == 2 * members
        and len(steps) == 2
    )
    return tiled(*arguments) if fits else general(*arguments)


def solution(mesh):
    return jax.shard_map(
        per_device,
        mesh=mesh,
        in_specs=(
            P(None, "rep", "mode", None),
            P(None, "rep", None, "mode", None),
            P(None, "rep", "mode", None),
            P(None, "mode", None),
            P("mode", None),
            P(),
        ),
        out_specs=(P(None, "mode", None), P(None, None, "mode", None), P(None, "mode", None)),
        check_vma=False,
    )
```
